32 devices in a mesh: gx: 4 (over y, x), gy: 2 (over core), gz: 4 (over z).
Axes of the slice: x: 2, y: 2, z: 4, core: 2. Of those that a mesh axis runs over, the one named last changes fastest.
Arguments:
- fields: float32 [64, 8, 16, 256], P(('gx', 'gy', 'gz')), may hold values from 0 to 1
- seed_labels: int32 [64, 256], P(('gx', 'gy', 'gz')), may hold values from 0 to 3
- coords: int32 [48, 3], replicated, may hold values from 0 to 5, as said below
- neighbours: int32 [48, 6], replicated, may hold values from -1 to 47, as said below
- owner_before: int32 [48], replicated, may hold values from 0 to 63, as said below
- owner_after: int32 [48], replicated, may hold values from 0 to 63, as said below
- couple: float32 [4, 4], replicated, may hold values from -3 to 3
- latent: float32 [4, 4], replicated, may hold values from -3 to 3
- diffuse: float32 [4], replicated, may hold values from 0.3 to 1.5
- thermal_gain: float32 [4], replicated, may hold values from -4 to 4
Outputs:
- fields_out: float32 [64, 8, 16, 256], P(('gx', 'gy', 'gz'))
The draws below stay inside these ranges and needn't reach their ends.
Inputs may be any that keep to these rules, and one draw needn't show every extreme that they name: `coords`: a permutation of the positions of a 4 x 2 x 6 grid of blocks. `neighbours`: the block beside b across each side by coords; -1 beyond the ends along x and y; along z the blocks close into a loop. `owner_before`: distinct for distinct blocks; a place p is slot p % 2 of device p // 2, devices counted over gx, gy, gz in order; block b's device has index coords[b, 0] along gx and coords[b, 1] along gy. `owner_after`: distinct for distinct blocks; a block's device after migration is its device before or the next one along gz, cyclic, with the same gx and gy indices; at most one block of a device moves; in every group of devices along gz at least one block moves.
All inputs are finite; a program needn't handle non-finite values.
Results may differ from the reference program's by a relative error of at most 0.0003.
Values sent between devices are 32-bit elements; how exact they have to be, the bound alone decides.
A program may use at most 64 MiB of HBM per device.

```python
import math
import jax
import jax.numpy as jnp
from jax import lax

CB = 16
NPHASE = 4
NPOT = 4
STEPS = 2
BLX = 4
BLY = 2
BLZ = 6
NBLK = 48
SLOTS_ALL = 64


def layout(key):
    base = jax.random.fold_in(key, 101)
    streams = jax.random.split(base, 6)
    cycle_len = BLZ * 2 // 3
    columns = BLX * BLY
    spare_slots = 2 * (cycle_len - 2)
    rotation = jax.random.randint(streams[0], (columns,), 0, cycle_len)
    picks = jax.vmap(lambda sub_key: jax.random.permutation(sub_key, spare_slots))(jax.random.split(streams[1], columns))
    picks = picks[:, :BLZ - 2].astype(jnp.int32)
    relative = jnp.concatenate([jnp.zeros((columns, 2), jnp.int32), picks // 2 + 2], 1)
    slot_pick = jnp.concatenate([jnp.tile(jnp.array([[0, 1]], jnp.int32), (columns, 1)), picks % 2], 1)
    depth_of = jax.vmap(lambda sub_key: jax.random.permutation(sub_key, BLZ))(jax.random.split(streams[2], columns)).astype(jnp.int32)
    loads = jnp.sum((relative[:, :, None] == jnp.arange(cycle_len, dtype=jnp.int32)[None, None, :]).astype(jnp.int32), 1)
    mover = jnp.logical_and(loads == 2, jnp.roll(loads, -1, axis=1) == 0)
    leave_bit = jax.random.randint(streams[3], (columns, cycle_len), 0, 2)
    land_bit = jax.random.randint(streams[4], (columns, cycle_len), 0, 2)
    moving = jnp.logical_and(jnp.take_along_axis(mover, relative, 1), slot_pick == jnp.take_along_axis(leave_bit, relative, 1))
    after_rel = relative + moving.astype(jnp.int32)
    after_slot = jnp.where(moving, jnp.take_along_axis(land_bit, relative, 1), slot_pick).astype(jnp.int32)
    column_ids = jnp.arange(columns, dtype=jnp.int32)[:, None]
    cycle_before = (rotation[:, None] + relative) % cycle_len
    cycle_after = (rotation[:, None] + after_rel) % cycle_len
    own_before = (column_ids * cycle_len + cycle_before) * 2 + slot_pick
    own_after = (column_ids * cycle_len + cycle_after) * 2 + after_slot
    ident = jax.random.permutation(streams[5], NBLK).astype(jnp.int32)
    position = column_ids * BLZ + depth_of
    block_of_entry = ident[position].reshape(-1)
    owners_first = jnp.zeros((NBLK,), jnp.int32).at[block_of_entry].set(own_before.reshape(-1).astype(jnp.int32))
    owners_second = jnp.zeros((NBLK,), jnp.int32).at[block_of_entry].set(own_after.reshape(-1).astype(jnp.int32))
    places = jnp.arange(NBLK, dtype=jnp.int32)
    grid_x = places // (BLY * BLZ)
    grid_y = places // BLZ % BLY
    grid_z = places % BLZ
    coords_pos = jnp.stack([grid_x, grid_y, grid_z], 1)
    coords_all = jnp.zeros((NBLK, 3), jnp.int32).at[ident].set(coords_pos)
    beside = jnp.stack([jnp.where(grid_x > 0, places - BLY * BLZ, -1), jnp.where(grid_x < BLX - 1, places + BLY * BLZ, -1), jnp.where(grid_y > 0, places - BLZ, -1), jnp.where(grid_y < BLY - 1, places + BLZ, -1), places - grid_z + (grid_z + BLZ - 1) % BLZ, places - grid_z + (grid_z + 1) % BLZ], 1)
    beside_ids = jnp.where(beside >= 0, ident[jnp.maximum(beside, 0)], -1).astype(jnp.int32)
    neighbour_all = jnp.zeros((NBLK, 6), jnp.int32).at[ident].set(beside_ids)
    return (coords_all, neighbour_all, owners_first, owners_second)


def draw_coords(key, part):
    return layout(key)[0]


def draw_neighbours(key, part):
    return layout(key)[1]


def draw_owner_before(key, part):
    return layout(key)[2]


def draw_owner_after(key, part):
    return layout(key)[3]


def set_ends(values, stream_key, smallest, top_value):
    longest = values.shape.index(max(values.shape))
    spots = []
    for shift in (0, 1):
        where = [jax.random.randint(jax.random.fold_in(stream_key, axis), (), 0, length) for axis, length in enumerate(values.shape)]
        where[longest] = (where[longest] + shift) % values.shape[longest]
        spots.append(tuple(where))
    return values.at[spots[0]].set(smallest).at[spots[1]].set(top_value)


def block_scale(key, dims, cuts, smallest, high):
    def one(dim, blocks):
        draws = jax.random.uniform(jax.random.fold_in(jax.random.fold_in(key, 6), dim), (blocks,), jnp.float32, smallest / len(cuts), high / len(cuts))
        return jnp.repeat(jnp.exp(draws), dims[dim] // blocks).reshape((-1,) + (1,) * (len(dims) - dim - 1))

    loudness = one(*cuts[0])
    for cut in cuts[1:]:
        loudness = loudness * one(*cut)
    return loudness


def centred(key, shape, scale, reach, kind=jnp.bfloat16):
    return jnp.clip(scale * jax.random.normal(key, shape, jnp.float32), -reach, reach).astype(kind)


def setup_inputs(seed: int = 0) -> dict:
    key_list = jax.random.split(jax.random.key(seed), 11)
    return {
        "fields": jnp.clip(1.0 * jax.random.uniform(key_list[0], (SLOTS_ALL, NPHASE + NPOT, CB, CB * CB), jnp.float32) ** block_scale(key_list[0], (SLOTS_ALL, NPHASE + NPOT, CB, CB * CB), ((0, 32),), -0.2, 0.2), 0.0, 1.0),
        "seed_labels": set_ends(jax.random.randint(key_list[1], (SLOTS_ALL, CB * CB), 0, NPHASE), jax.random.fold_in(key_list[1], 1), 0, NPHASE - 1).astype(jnp.int32),
        "coords": draw_coords(jax.random.fold_in(key_list[10], 71), 0),
        "neighbours": draw_neighbours(jax.random.fold_in(key_list[10], 71), 0),
        "owner_before": draw_owner_before(jax.random.fold_in(key_list[10], 71), 0),
        "owner_after": draw_owner_after(jax.random.fold_in(key_list[10], 71), 0),
        "couple": centred(key_list[6], (NPHASE, NPOT), NPOT ** -0.5, 3.0, jnp.float32),
        "latent": centred(key_list[7], (NPOT, NPHASE), 0.5, 3.0, jnp.float32),
        "diffuse": jnp.clip(jnp.exp(jax.random.uniform(key_list[8], (NPOT,), jnp.float32, math.log(0.3), math.log(1.5))), 0.3, 1.5),
        "thermal_gain": centred(key_list[9], (NPHASE,), 1.0, 4.0, jnp.float32),
    }


OPPOSITE = (1, 0, 3, 2, 5, 4)
seed_gain = 2.0


def faces_of(volume):
    components, extent, surface = volume.shape
    low_x = volume[:, 0, :]
    high_x = volume[:, extent - 1, :]
    low_y = volume[:, :, :extent].reshape(components, extent * extent)
    high_y = volume[:, :, surface - extent:].reshape(components, extent * extent)
    low_z = volume[:, :, 0::extent].reshape(components, extent * extent)
    high_z = volume[:, :, extent - 1::extent].reshape(components, extent * extent)
    return jnp.stack([low_x, high_x, low_y, high_y, low_z, high_z], 0)


def laplace(volume, ghosts):
    components, extent, surface = volume.shape
    below_x = jnp.concatenate([ghosts[0][:, None, :], volume[:, :-1, :]], 1)
    above_x = jnp.concatenate([volume[:, 1:, :], ghosts[1][:, None, :]], 1)
    below_y = jnp.concatenate([ghosts[2].reshape(components, extent, extent), volume[:, :, :-extent]], 2)
    above_y = jnp.concatenate([volume[:, :, extent:], ghosts[3].reshape(components, extent, extent)], 2)
    offset_z = jnp.arange(surface) % extent
    zeros_col = jnp.zeros((components, extent, 1), volume.dtype)
    below_z = jnp.where(offset_z == 0, jnp.repeat(ghosts[4].reshape(components, extent, extent), extent, axis=2),
                        jnp.concatenate([zeros_col, volume[:, :, :-1]], 2))
    above_z = jnp.where(offset_z == extent - 1, jnp.repeat(ghosts[5].reshape(components, extent, extent), extent, axis=2),
                        jnp.concatenate([volume[:, :, 1:], zeros_col], 2))
    return below_x + above_x + below_y + above_y + below_z + above_z - 6.0 * volume


def phase_step(phases, potential, ghosts, x_global, seed_row, iteration, couple, thermal_gain, seeded):
    extent = phases.shape[1]
    thermal = x_global / (2.0 * extent) - 1.0 - 0.25 * iteration
    driving = jnp.einsum('kj,jxc->kxc', couple, potential, precision=lax.Precision.HIGHEST)
    driving = driving + thermal_gain[:, None, None] * thermal[None, :, None]
    if seeded:
        marks = seed_row[None, None, :] == jnp.arange(phases.shape[0], dtype=jnp.int32)[:, None, None]
        driving = driving + seed_gain * marks.astype(jnp.float32)
    return phases + 0.12 * laplace(phases, ghosts) + phases * (1.0 - phases) * (phases - 0.5 + driving)


def potential_step(potential, ghosts, old_phases, new_phases, diffuse, latent):
    release = jnp.einsum('jk,kxc->jxc', latent, new_phases - old_phases, precision=lax.Precision.HIGHEST)
    return potential + 0.1 * diffuse[:, None, None] * laplace(potential, ghosts) - release


def ghosts_of(values, neighbours):
    surfaces = jax.vmap(faces_of)(values)
    present = neighbours >= 0
    safe_ids = jnp.where(present, neighbours, 0)
    picked = jnp.stack([surfaces[safe_ids[:, side], OPPOSITE[side]] for side in range(6)], 1)
    return jnp.where(present[:, :, None, None], picked, surfaces)


def reference(fields, seed_labels, coords, neighbours, owner_before, owner_after, couple, latent, diffuse, thermal_gain):
    blocks = fields[owner_before]
    seed_rows = seed_labels[owner_before]
    x_global = (coords[:, 0:1] * CB + jnp.arange(CB, dtype=jnp.int32)[None, :]).astype(jnp.float32)
    phases = blocks[:, :NPHASE]
    potential = blocks[:, NPHASE:]
    for iteration in range(STEPS):
        phase_ghost = ghosts_of(phases, neighbours)
        new_phases = lax.map(
            lambda member: phase_step(member[0], member[1], member[2], member[3], member[4],
                                      iteration, couple, thermal_gain, iteration == 0),
            (phases, potential, phase_ghost, x_global, seed_rows))
        pot_ghost = ghosts_of(potential, neighbours)
        potential = lax.map(
            lambda member: potential_step(member[0], member[1], member[2], member[3], diffuse, latent),
            (potential, pot_ghost, phases, new_phases))
        phases = new_phases
    result = jnp.concatenate([phases, potential], 1)
    return jnp.zeros_like(fields).at[owner_after].set(result)
```

```python
import functools

import jax
import jax.numpy as jnp
from jax import lax
from jax.experimental import pallas as pl
from jax.experimental.pallas import tpu as pltpu
from jax.sharding import PartitionSpec as P

NPHASE = 4
STEPS = 2
LANES = 128
SEED_GAIN = 2.0
MESH = pl.DeviceIdType.MESH


def kernel(
    sizes,
    fields,
    seeds,
    coords,
    before,
    after,
    couple,
    latent,
    diffuse,
    gain,
    out,
    recv,
    seed_recv,
    vals,
    xsend,
    xghost,
    ysend,
    yghost,
    result,
    outbuf,
    in_send,
    in_recv,
    seed_send,
    seed_got,
    x_send,
    x_recv,
    y_send,
    y_recv,
    out_send,
    out_recv,
    local_sem,
):
    gx_n, gy_n, gz_n, nblk, cells, surface = sizes
    slots, nfield = outbuf.shape[1], outbuf.shape[2]
    rows = outbuf.shape[3]
    halves = surface // LANES
    per_column = vals.shape[1]
    x_parts = gz_n // halves
    gx, gy, gz = lax.axis_index("gx"), lax.axis_index("gy"), lax.axis_index("gz")
    odd_x, odd_y = gx % 2, gy % 2

    def part_of(g):
        a, b = g // halves, g % halves
        xh = a + odd_x * (x_parts - 1 - 2 * a)
        yh = b + odd_y * (halves - 1 - 2 * b)
        return xh, yh

    def window(ref, g):
        xh, yh = part_of(g)
        x0 = pl.multiple_of(xh * rows, rows)
        y0 = pl.multiple_of(yh * LANES, LANES)
        return ref.at[:, :, pl.ds(x0, rows), pl.ds(y0, LANES)]

    def seed_window(g):
        _, yh = part_of(g)
        return seeds.at[:, pl.ds(pl.multiple_of(yh * LANES, LANES), LANES)]

    xh, yh = part_of(gz)
    xpos = gx * x_parts + xh
    ypos = gy * halves + yh
    x_total, y_total = gx_n * x_parts, gy_n * halves
    dir_x = 1 - 2 * odd_x
    dir_y = 1 - 2 * odd_y
    xlo_in, xhi_in = xh > 0, xh < x_parts - 1
    ylo_in, yhi_in = yh > 0, yh < halves - 1
    sides = []
    for exists, inside, step_x, step_y, move in (
        (xpos > 0, xlo_in, -1, 0, -halves * dir_x),
        (xpos < x_total - 1, xhi_in, 1, 0, halves * dir_x),
        (ypos > 0, ylo_in, 0, -1, -dir_y),
        (ypos < y_total - 1, yhi_in, 0, 1, dir_y),
    ):
        ins = inside.astype(jnp.int32)
        device = (gx + step_x * (1 - ins), gy + step_y * (1 - ins), gz + move * ins)
        sides.append((exists, inside, device))

    barrier = pltpu.get_barrier_semaphore()
    for d in range(1, gz_n):
        pl.semaphore_signal(
            barrier, inc=1, device_id=(gx, gy, (gz + d) % gz_n), device_id_type=MESH
        )
    expected = gz_n - 1
    for exists, inside, device in sides:
        outside = jnp.logical_and(exists, jnp.logical_not(inside))

        @pl.when(outside)
        def _(device=device):
            pl.semaphore_signal(barrier, inc=1, device_id=device, device_id_type=MESH)

        expected = expected + outside.astype(jnp.int32)
    pl.semaphore_wait(barrier, expected)

    moves = []
    for d in range(gz_n - 1, 0, -1):
        to = (gz + d) % gz_n
        for src, dst, s_sem, r_sem in (
            (window(fields, to), recv.at[pl.ds(slots * gz, slots)], in_send, in_recv),
            (seed_window(to), seed_recv.at[gz], seed_send, seed_got),
        ):
            copy = pltpu.make_async_remote_copy(
                src_ref=src,
                dst_ref=dst,
                send_sem=s_sem.at[d - 1],
                recv_sem=r_sem.at[d - 1],
                device_id=(gx, gy, to),
                device_id_type=MESH,
            )
            copy.start()
            moves.append(copy)
    own = pltpu.make_async_copy(
        window(fields, gz), recv.at[pl.ds(slots * gz, slots)], local_sem.at[0]
    )
    own.start()
    own_seed = pltpu.make_async_copy(seed_window(gz), seed_recv.at[gz], local_sem.at[1])
    own_seed.start()

    base = (gx * gy_n + gy) * (gz_n * slots)
    places = gz_n * slots

    def lookup(b, carry):
        source, depth = carry
        here = jnp.logical_and(coords[0, b] == gx, coords[1, b] == gy)
        z = jnp.where(here, coords[2, b], -1)
        was = before[b] - base
        now = jnp.where(here, after[b] - base, -1)
        source = tuple(jnp.where(z == k, was, source[k]) for k in range(per_column))
        depth = tuple(jnp.where(now == q, z, depth[q]) for q in range(places))
        return source, depth

    source, depth = lax.fori_loop(
        0,
        nblk,
        lookup,
        ((jnp.int32(0),) * per_column, (jnp.int32(-1),) * places),
    )

    own.wait()
    own_seed.wait()
    for copy in moves:
        copy.wait()

    marks = []
    for k in range(per_column):
        p = source[k]
        vals[:, k] = recv[p]
        pair = seed_recv[p // slots]
        row = pair[0:1]
        for s in range(1, slots):
            row = jnp.where(p % slots == s, pair[s : s + 1], row)
        marks.append(row[None])
    marks = jnp.concatenate(marks, 0)

    shape = (per_column, rows, LANES)
    lane = lax.broadcasted_iota(jnp.int32, shape, 2)
    row_id = lax.broadcasted_iota(jnp.int32, shape, 1)
    z_cell = lane % cells
    group = lane // cells
    xglob = (row_id + (gx * cells + xh * rows)).astype(jnp.float32)

    def rolled(v, shift):
        shift = shift % LANES
        return v if shift == 0 else pltpu.roll(v, shift, 2)

    def exchange(step, old):
        low_y = jnp.zeros(shape, jnp.float32)
        high_y = low_y
        for f in range(nfield):
            v = old[f]
            xsend[step, 0, :, f : f + 1, :] = v[:, 0:1, :]
            xsend[step, 1, :, f : f + 1, :] = v[:, rows - 1 : rows, :]
            low_y = jnp.where(group == f, rolled(v, cells * f), low_y)
            high_y = jnp.where(group == f, rolled(v, cells * f + cells), high_y)
        ysend[step, 0] = low_y
        ysend[step, 1] = high_y
        for phase in ("start", "wait"):
            for side, (exists, _, device) in enumerate(sides):
                send, ghost, s_sem, r_sem = (
                    (xsend, xghost, x_send, x_recv)
                    if side < 2
                    else (ysend, yghost, y_send, y_recv)
                )
                e = side % 2

                @pl.when(exists)
                def _(send=send, ghost=ghost, s_sem=s_sem, r_sem=r_sem, e=e, device=device):
                    if phase == "start":
                        pltpu.make_async_remote_copy(
                            src_ref=send.at[step, e],
                            dst_ref=ghost.at[step, 1 - e],
                            send_sem=s_sem.at[step, e],
                            recv_sem=r_sem.at[step, 1 - e],
                            device_id=device,
                            device_id_type=MESH,
                        ).start()
                    else:
                        pltpu.make_async_remote_copy(
                            src_ref=send.at[step, e],
                            dst_ref=ghost.at[step, e],
                            send_sem=s_sem.at[step, e],
                            recv_sem=r_sem.at[step, e],
                            device_id=device,
                            device_id_type=MESH,
                        ).wait()

                if phase == "start":

                    @pl.when(jnp.logical_not(exists))
                    def _(send=send, ghost=ghost, e=e):
                        ghost[step, e] = send[step, e]

    def laplace(step, f, v):
        below_x = jnp.concatenate([xghost[step, 0, :, f : f + 1, :], v[:, :-1, :]], 1)
        above_x = jnp.concatenate([v[:, 1:, :], xghost[step, 1, :, f : f + 1, :]], 1)
        below_y = jnp.where(
            group == 0, rolled(yghost[step, 0], -cells * f), rolled(v, cells)
        )
        above_y = jnp.where(
            group == LANES // cells - 1,
            rolled(yghost[step, 1], -cells * f - cells),
            rolled(v, -cells),
        )
        before_k = jnp.concatenate([v[-1:], v[:-1]], 0)
        after_k = jnp.concatenate([v[1:], v[:1]], 0)
        below_z = jnp.where(z_cell == 0, rolled(before_k, 1 - cells), rolled(v, 1))
        above_z = jnp.where(z_cell == cells - 1, rolled(after_k, cells - 1), rolled(v, -1))
        return below_x + above_x + below_y + above_y + below_z + above_z - 6.0 * v

    for step in range(STEPS):
        src = vals if step == 0 else result.at[step - 1]
        exchange(step, [src[f] for f in range(nfield)])
        thermal = xglob / (2.0 * cells) - 1.0 - 0.25 * step
        change = []
        for k in range(NPHASE):
            phi = src[k]
            drive = gain[k] * thermal
            for j in range(nfield - NPHASE):
                drive = drive + couple[k, j] * src[NPHASE + j]
            if step == 0:
                drive = drive + SEED_GAIN * (marks == k).astype(jnp.float32)
            delta = 0.12 * laplace(step, k, phi) + phi * (1.0 - phi) * (phi - 0.5 + drive)
            new = phi + delta
            result[step, k] = new
            change.append(new - phi)
        for j in range(nfield - NPHASE):
            mu = src[NPHASE + j]
            new = mu + (0.1 * diffuse[j]) * laplace(step, NPHASE + j, mu)
            for k in range(NPHASE):
                new = new - latent[j, k] * change[k]
            result[step, NPHASE + j] = new

    for q in range(places):
        k = depth[q]
        tile = result[STEPS - 1, :, jnp.maximum(k, 0)]
        outbuf[q // slots, q % slots] = jnp.where(k >= 0, tile, 0.0)
    moves = []
    for d in range(gz_n - 1, 0, -1):
        to = (gz + d) % gz_n
        copy = pltpu.make_async_remote_copy(
            src_ref=outbuf.at[to],
            dst_ref=window(out, gz),
            send_sem=out_send.at[d - 1],
            recv_sem=out_recv.at[d - 1],
            device_id=(gx, gy, to),
            device_id_type=MESH,
        )
        copy.start()
        moves.append(copy)
    own = pltpu.make_async_copy(outbuf.at[gz], window(out, gz), local_sem.at[2])
    own.start()
    own.wait()
    for copy in moves:
        copy.wait()


def solution(mesh):
    gx_n, gy_n, gz_n = mesh.shape["gx"], mesh.shape["gy"], mesh.shape["gz"]

    def per_device(fields, seeds, coords, neighbours, before, after, couple, latent, diffuse, gain):
        slots, nfield, cells, surface = fields.shape
        nblk = coords.shape[0]
        per_column = nblk // (gx_n * gy_n)
        halves = surface // LANES
        rows = cells * halves // gz_n
        f32, i32 = jnp.float32, jnp.int32
        dma = pltpu.SemaphoreType.DMA
        smem = pl.BlockSpec(memory_space=pltpu.SMEM)
        anyspace = pl.BlockSpec(memory_space=pl.ANY)
        faces_x = (STEPS, 2, per_column, nfield, LANES)
        faces_y = (STEPS, 2, per_column, rows, LANES)
        return pl.pallas_call(
            functools.partial(kernel, (gx_n, gy_n, gz_n, nblk, cells, surface)),
            out_shape=pltpu.VMEM(fields.shape, f32),
            in_specs=[anyspace, anyspace] + [smem] * 7,
            out_specs=pl.BlockSpec(memory_space=pltpu.VMEM),
            scratch_shapes=[
                pltpu.VMEM((gz_n * slots, nfield, rows, LANES), f32),
                pltpu.VMEM((gz_n, slots, LANES), i32),
                pltpu.VMEM((nfield, per_column, rows, LANES), f32),
                pltpu.VMEM(faces_x, f32),
                pltpu.VMEM(faces_x, f32),
                pltpu.VMEM(faces_y, f32),
                pltpu.VMEM(faces_y, f32),
                pltpu.VMEM((STEPS, nfield, per_column, rows, LANES), f32),
                pltpu.VMEM((gz_n, slots, nfield, rows, LANES), f32),
                dma((gz_n,)),
                dma((gz_n,)),
                dma((gz_n,)),
                dma((gz_n,)),
                dma((STEPS, 2)),
                dma((STEPS, 2)),
                dma((STEPS, 2)),
                dma((STEPS, 2)),
                dma((gz_n,)),
                dma((gz_n,)),
                dma((3,)),
            ],
            compiler_params=pltpu.CompilerParams(collective_id=0, has_side_effects=True),
        )(fields, seeds, coords.T, before, after, couple, latent, diffuse, gain)

    placed = (
        P(("gx", "gy", "gz"), None, None, None),
        P(("gx", "gy", "gz"), None),
    ) + (P(),) * 8
    return jax.shard_map(
        per_device,
        mesh=mesh,
        in_specs=placed,
        out_specs=P(("gx", "gy", "gz"), None, None, None),
        check_vma=False,
    )
```

```python
import functools

import jax
import jax.numpy as jnp
from jax import lax
from jax.experimental import pallas as pl
from jax.experimental.pallas import tpu as pltpu
from jax.sharding import PartitionSpec as P

NPHASE = 4
STEPS = 2
LANES = 128
SEED_GAIN = 2.0
MESH = pl.DeviceIdType.MESH


def tile_kernel(
    sizes,
    fields,
    seeds,
    coords,
    before,
    after,
    couple,
    latent,
    diffuse,
    gain,
    out,
    recv,
    seed_recv,
    vals,
    xsend,
    xghost,
    ysend,
    yghost,
    result,
    outbuf,
    in_send,
    in_recv,
    seed_send,
    seed_got,
    x_send,
    x_recv,
    y_send,
    y_recv,
    out_send,
    out_recv,
    local_sem,
):
    gx_n, gy_n, gz_n, nblk, cells, surface = sizes
    slots, nfield = outbuf.shape[1], outbuf.shape[2]
    rows = outbuf.shape[3]
    halves = surface // LANES
    per_column = vals.shape[1]
    x_parts = gz_n // halves
    gx, gy, gz = lax.axis_index("gx"), lax.axis_index("gy"), lax.axis_index("gz")
    odd_x, odd_y = gx % 2, gy % 2

    def part_of(g):
        a, b = g // halves, g % halves
        xh = a + odd_x * (x_parts - 1 - 2 * a)
        yh = b + odd_y * (halves - 1 - 2 * b)
        return xh, yh

    def window(ref, g):
        xh, yh = part_of(g)
        x0 = pl.multiple_of(xh * rows, rows)
        y0 = pl.multiple_of(yh * LANES, LANES)
        return ref.at[:, :, pl.ds(x0, rows), pl.ds(y0, LANES)]

    def seed_window(g):
        _, yh = part_of(g)
        return seeds.at[:, pl.ds(pl.multiple_of(yh * LANES, LANES), LANES)]

    xh, yh = part_of(gz)
    xpos = gx * x_parts + xh
    ypos = gy * halves + yh
    x_total, y_total = gx_n * x_parts, gy_n * halves
    dir_x = 1 - 2 * odd_x
    dir_y = 1 - 2 * odd_y
    xlo_in, xhi_in = xh > 0, xh < x_parts - 1
    ylo_in, yhi_in = yh > 0, yh < halves - 1
    sides = []
    for exists, inside, step_x, step_y, move in (
        (xpos > 0, xlo_in, -1, 0, -halves * dir_x),
        (xpos < x_total - 1, xhi_in, 1, 0, halves * dir_x),
        (ypos > 0, ylo_in, 0, -1, -dir_y),
        (ypos < y_total - 1, yhi_in, 0, 1, dir_y),
    ):
        ins = inside.astype(jnp.int32)
        device = (gx + step_x * (1 - ins), gy + step_y * (1 - ins), gz + move * ins)
        sides.append((exists, inside, device))

    barrier = pltpu.get_barrier_semaphore()
    for d in range(1, gz_n):
        pl.semaphore_signal(
            barrier, inc=1, device_id=(gx, gy, (gz + d) % gz_n), device_id_type=MESH
        )
    expected = gz_n - 1
    for exists, inside, device in sides:
        outside = jnp.logical_and(exists, jnp.logical_not(inside))

        @pl.when(outside)
        def _(device=device):
            pl.semaphore_signal(barrier, inc=1, device_id=device, device_id_type=MESH)

        expected = expected + outside.astype(jnp.int32)
    pl.semaphore_wait(barrier, expected)

    moves = []
    for d in range(gz_n - 1, 0, -1):
        to = (gz + d) % gz_n
        for src, dst, s_sem, r_sem in (
            (window(fields, to), recv.at[pl.ds(slots * gz, slots)], in_send, in_recv),
            (seed_window(to), seed_recv.at[gz], seed_send, seed_got),
        ):
            copy = pltpu.make_async_remote_copy(
                src_ref=src,
                dst_ref=dst,
                send_sem=s_sem.at[d - 1],
                recv_sem=r_sem.at[d - 1],
                device_id=(gx, gy, to),
                device_id_type=MESH,
            )
            copy.start()
            moves.append(copy)
    own = pltpu.make_async_copy(
        window(fields, gz), recv.at[pl.ds(slots * gz, slots)], local_sem.at[0]
    )
    own.start()
    own_seed = pltpu.make_async_copy(seed_window(gz), seed_recv.at[gz], local_sem.at[1])
    own_seed.start()

    base = (gx * gy_n + gy) * (gz_n * slots)
    places = gz_n * slots

    def lookup(b, carry):
        source, depth = carry
        here = jnp.logical_and(coords[0, b] == gx, coords[1, b] == gy)
        z = jnp.where(here, coords[2, b], -1)
        was = before[b] - base
        now = jnp.where(here, after[b] - base, -1)
        source = tuple(jnp.where(z == k, was, source[k]) for k in range(per_column))
        depth = tuple(jnp.where(now == q, z, depth[q]) for q in range(places))
        return source, depth

    source, depth = lax.fori_loop(
        0,
        nblk,
        lookup,
        ((jnp.int32(0),) * per_column, (jnp.int32(-1),) * places),
    )

    own.wait()
    own_seed.wait()
    for copy in moves:
        copy.wait()

    marks = []
    for k in range(per_column):
        p = source[k]
        vals[:, k] = recv[p]
        pair = seed_recv[p // slots]
        row = pair[0:1]
        for s in range(1, slots):
            row = jnp.where(p % slots == s, pair[s : s + 1], row)
        marks.append(row[None])
    marks = jnp.concatenate(marks, 0)

    shape = (per_column, rows, LANES)
    lane = lax.broadcasted_iota(jnp.int32, shape, 2)
    row_id = lax.broadcasted_iota(jnp.int32, shape, 1)
    z_cell = lane % cells
    group = lane // cells
    xglob = (row_id + (gx * cells + xh * rows)).astype(jnp.float32)

    def rolled(v, shift):
        shift = shift % LANES
        return v if shift == 0 else pltpu.roll(v, shift, 2)

    def exchange(step, old):
        low_y = jnp.zeros(shape, jnp.float32)
        high_y = low_y
        for f in range(nfield):
            v = old[f]
            xsend[step, 0, :, f : f + 1, :] = v[:, 0:1, :]
            xsend[step, 1, :, f : f + 1, :] = v[:, rows - 1 : rows, :]
            low_y = jnp.where(group == f, rolled(v, cells * f), low_y)
            high_y = jnp.where(group == f, rolled(v, cells * f + cells), high_y)
        ysend[step, 0] = low_y
        ysend[step, 1] = high_y
        for phase in ("start", "wait"):
            for side, (exists, _, device) in enumerate(sides):
                send, ghost, s_sem, r_sem = (
                    (xsend, xghost, x_send, x_recv)
                    if side < 2
                    else (ysend, yghost, y_send, y_recv)
                )
                e = side % 2

                @pl.when(exists)
                def _(send=send, ghost=ghost, s_sem=s_sem, r_sem=r_sem, e=e, device=device):
                    if phase == "start":
                        pltpu.make_async_remote_copy(
                            src_ref=send.at[step, e],
                            dst_ref=ghost.at[step, 1 - e],
                            send_sem=s_sem.at[step, e],
                            recv_sem=r_sem.at[step, 1 - e],
                            device_id=device,
                            device_id_type=MESH,
                        ).start()
                    else:
                        pltpu.make_async_remote_copy(
                            src_ref=send.at[step, e],
                            dst_ref=ghost.at[step, e],
                            send_sem=s_sem.at[step, e],
                            recv_sem=r_sem.at[step, e],
                            device_id=device,
                            device_id_type=MESH,
                        ).wait()

                if phase == "start":

                    @pl.when(jnp.logical_not(exists))
                    def _(send=send, ghost=ghost, e=e):
                        ghost[step, e] = send[step, e]

    def laplace(step, f, v):
        below_x = jnp.concatenate([xghost[step, 0, :, f : f + 1, :], v[:, :-1, :]], 1)
        above_x = jnp.concatenate([v[:, 1:, :], xghost[step, 1, :, f : f + 1, :]], 1)
        below_y = jnp.where(
            group == 0, rolled(yghost[step, 0], -cells * f), rolled(v, cells)
        )
        above_y = jnp.where(
            group == LANES // cells - 1,
            rolled(yghost[step, 1], -cells * f - cells),
            rolled(v, -cells),
        )
        before_k = jnp.concatenate([v[-1:], v[:-1]], 0)
        after_k = jnp.concatenate([v[1:], v[:1]], 0)
        below_z = jnp.where(z_cell == 0, rolled(before_k, 1 - cells), rolled(v, 1))
        above_z = jnp.where(z_cell == cells - 1, rolled(after_k, cells - 1), rolled(v, -1))
        return below_x + above_x + below_y + above_y + below_z + above_z - 6.0 * v

    for step in range(STEPS):
        src = vals if step == 0 else result.at[step - 1]
        exchange(step, [src[f] for f in range(nfield)])
        thermal = xglob / (2.0 * cells) - 1.0 - 0.25 * step
        change = []
        for k in range(NPHASE):
            phi = src[k]
            drive = gain[k] * thermal
            for j in range(nfield - NPHASE):
                drive = drive + couple[k, j] * src[NPHASE + j]
            if step == 0:
                drive = drive + SEED_GAIN * (marks == k).astype(jnp.float32)
            delta = 0.12 * laplace(step, k, phi) + phi * (1.0 - phi) * (phi - 0.5 + drive)
            new = phi + delta
            result[step, k] = new
            change.append(new - phi)
        for j in range(nfield - NPHASE):
            mu = src[NPHASE + j]
            new = mu + (0.1 * diffuse[j]) * laplace(step, NPHASE + j, mu)
            for k in range(NPHASE):
                new = new - latent[j, k] * change[k]
            result[step, NPHASE + j] = new

    for q in range(places):
        k = depth[q]
        tile = result[STEPS - 1, :, jnp.maximum(k, 0)]
        outbuf[q // slots, q % slots] = jnp.where(k >= 0, tile, 0.0)
    moves = []
    for d in range(gz_n - 1, 0, -1):
        to = (gz + d) % gz_n
        copy = pltpu.make_async_remote_copy(
            src_ref=outbuf.at[to],
            dst_ref=window(out, gz),
            send_sem=out_send.at[d - 1],
            recv_sem=out_recv.at[d - 1],
            device_id=(gx, gy, to),
            device_id_type=MESH,
        )
        copy.start()
        moves.append(copy)
    own = pltpu.make_async_copy(outbuf.at[gz], window(out, gz), local_sem.at[2])
    own.start()
    own.wait()
    for copy in moves:
        copy.wait()


def deep_kernel(sizes, fields, seeds, *refs):
    gx_n, gy_n, gz_n, nblk, cells, surface = sizes
    tables, (
        out,
        coords,
        before,
        after,
        couple,
        latent,
        diffuse,
        gain,
        table_sem,
        mine,
        bulk,
        seed_recv,
        strip,
        vals,
        edge,
        mid,
        mid_edge,
        marks,
        edge_marks,
        xsend,
        xghost,
        xsmall,
        xgsmall,
        packed,
        unpack,
        result,
        outbuf,
        outrecv,
        local_sem,
        in_sem,
        seed_sem,
        strip_sem,
        strip_seed_sem,
        x_sem,
        xs_sem,
        out_sem,
        *arrivals,
    ) = refs[:7], refs[7:]
    slots, nfield = mine.shape[0], mine.shape[1]
    tiles = surface // LANES
    strip_recv, strip_seed, recv = arrivals[:2], arrivals[2:4], arrivals[4:]
    per_column = vals.shape[2]
    rows, halo = cells // gz_n, STEPS
    ext = rows + 2 * halo
    strip_lanes = halo * cells
    per_pack = LANES // strip_lanes
    packs = -(-nfield // per_pack)
    places = gz_n * slots
    gx, gy, gz = lax.axis_index("gx"), lax.axis_index("gy"), lax.axis_index("gz")
    odd_x = gx % 2
    turn = 1 - 2 * odd_x

    def tile_of(g):
        return g + odd_x * (gz_n - 1 - 2 * g)

    part = tile_of(gz)
    xpos = gx * gz_n + part
    sides_x = []
    for exists, inside, step_x in (
        (xpos > 0, part > 0, -1),
        (xpos < gx_n * gz_n - 1, part < gz_n - 1, 1),
    ):
        ins = inside.astype(jnp.int32)
        device = (gx + step_x * (1 - ins), gy, gz + step_x * turn * ins)
        sides_x.append((exists, inside, device))
    sides_y = ((gy > 0, gy - 1), (gy < gy_n - 1, gy + 1))

    barrier = pltpu.get_barrier_semaphore()
    expected = gz_n - 1
    for d in range(1, gz_n):
        pl.semaphore_signal(
            barrier, inc=1, device_id=(gx, gy, (gz + d) % gz_n), device_id_type=MESH
        )
    for exists, other in sides_y:

        @pl.when(exists)
        def _(other=other):
            for z in range(gz_n):
                pl.semaphore_signal(
                    barrier, inc=1, device_id=(gx, other, z), device_id_type=MESH
                )

        expected = expected + gz_n * exists.astype(jnp.int32)
    for exists, inside, device in sides_x:
        outside = jnp.logical_and(exists, jnp.logical_not(inside))

        @pl.when(outside)
        def _(device=device):
            pl.semaphore_signal(barrier, inc=1, device_id=device, device_id_type=MESH)

        expected = expected + outside.astype(jnp.int32)

    load = pltpu.make_async_copy(fields, mine, local_sem.at[0])
    load.start()
    load_seed = pltpu.make_async_copy(seeds, seed_recv.at[gz], local_sem.at[1])
    load_seed.start()
    small = (coords, before, after, couple, latent, diffuse, gain)
    fetches = [
        pltpu.make_async_copy(src, dst, table_sem.at[n])
        for n, (src, dst) in enumerate(zip(tables, small))
    ]
    for fetch in fetches:
        fetch.start()

    lane = lax.broadcasted_iota(jnp.int32, (1, 1, LANES), 2)

    def rolled(v, shift):
        shift = shift % LANES
        return v if shift == 0 else pltpu.roll(v, shift, 2)

    def pack(s, n, t, e):
        row = None
        for j in range(min(per_pack, nfield - n * per_pack)):
            v = mine[s, pl.ds(n * per_pack + j, 1), :, pl.ds(t * LANES, LANES)]
            v = rolled(v, strip_lanes * (j + e))
            row = v if row is None else jnp.where(lane // strip_lanes == j, v, row)
        return [row[:, q * rows : (q + 1) * rows] for q in range(gz_n)]

    load.wait()
    for s in range(slots):
        for n in range(packs):
            for e, t in ((0, 0), (1, tiles - 1)):
                for q, row in enumerate(pack(s, n, t, e)):
                    strip[e, q, s, pl.ds(n, 1)] = row
            for t in range(tiles - 1):
                for q, row in enumerate(pack(s, n, t + 1, 0)):
                    bulk[t, q, s, pl.ds(nfield + n, 1)] = row
    for t in range(tiles):
        for q in range(gz_n):
            bulk[t, q, :, pl.ds(0, nfield)] = mine[
                :, :, q * rows : (q + 1) * rows, t * LANES : (t + 1) * LANES
            ]
    pl.semaphore_wait(barrier, expected)

    for e, (exists, other) in enumerate(sides_y):

        @pl.when(exists)
        def _(e=e, other=other):
            for z in range(gz_n):
                pltpu.make_async_remote_copy(
                    src_ref=strip.at[e, tile_of(z)],
                    dst_ref=strip_recv[1 - e].at[pl.ds(slots * gz, slots)],
                    send_sem=strip_sem.at[e],
                    recv_sem=strip_sem.at[2 + 1 - e],
                    device_id=(gx, other, z),
                    device_id_type=MESH,
                ).start()
                pltpu.make_async_remote_copy(
                    src_ref=seeds,
                    dst_ref=strip_seed[1 - e].at[gz],
                    send_sem=strip_seed_sem.at[e],
                    recv_sem=strip_seed_sem.at[2 + 1 - e],
                    device_id=(gx, other, z),
                    device_id_type=MESH,
                ).start()

    for d in range(1, gz_n):
        pltpu.make_async_remote_copy(
            src_ref=seeds,
            dst_ref=seed_recv.at[gz],
            send_sem=seed_sem.at[0],
            recv_sem=seed_sem.at[1],
            device_id=(gx, gy, (gz + d) % gz_n),
            device_id_type=MESH,
        ).start()

    width = [nfield + packs] * (tiles - 1) + [nfield]
    for t in range(tiles):
        for d in range(gz_n - 1, 0, -1):
            to = (gz + d) % gz_n
            pltpu.make_async_remote_copy(
                src_ref=bulk.at[t, tile_of(to), :, pl.ds(0, width[t])],
                dst_ref=recv[t].at[pl.ds(slots * gz, slots), pl.ds(0, width[t])],
                send_sem=in_sem.at[t],
                recv_sem=in_sem.at[tiles + t],
                device_id=(gx, gy, to),
                device_id_type=MESH,
            ).start()
    for t in range(tiles):
        recv[t][pl.ds(slots * gz, slots), pl.ds(0, width[t])] = bulk[t, part, :, pl.ds(0, width[t])]
    for fetch in fetches:
        fetch.wait()

    base = (gx * gy_n + gy) * places

    def lookup(b, carry):
        source, low, high, depth = carry
        cy, z = coords[1, b], coords[2, b]
        same = coords[0, b] == gx
        was, now = before[b] - base, after[b] - base
        here = jnp.where(jnp.logical_and(same, cy == gy), z, -1)
        under = jnp.where(jnp.logical_and(same, cy == gy - 1), z, -1)
        over = jnp.where(jnp.logical_and(same, cy == gy + 1), z, -1)
        now = jnp.where(here >= 0, now, -1)
        source = tuple(jnp.where(here == k, was, source[k]) for k in range(per_column))
        low = tuple(jnp.where(under == k, was + places, low[k]) for k in range(per_column))
        high = tuple(jnp.where(over == k, was - places, high[k]) for k in range(per_column))
        depth = tuple(jnp.where(now == p, z, depth[p]) for p in range(places))
        return source, low, high, depth

    none = (jnp.int32(0),) * per_column
    source, low, high, depth = lax.fori_loop(
        0, nblk, lookup, (none, none, none, (jnp.int32(-1),) * places)
    )

    def drain(ref, sem):
        pltpu.make_async_copy(ref, ref, sem).wait()

    def seed_row(ref, p):
        pair = ref[p // slots]
        row = pair[0:1]
        for s in range(1, slots):
            row = jnp.where(p % slots == s, pair[s : s + 1], row)
        return row.astype(jnp.float32)

    load_seed.wait()
    drain(seed_recv.at[pl.ds(0, gz_n - 1)], seed_sem.at[1])
    for k in range(per_column):
        row = seed_row(seed_recv, source[k])
        for t in range(tiles):
            piece = row[:, t * LANES : (t + 1) * LANES]
            wide = jnp.broadcast_to(piece, (ext, LANES))
            marks[t, k] = wide
            if t > 0:
                edge_marks[t, k] = wide
            for x in range(2):
                xsmall[t, x, k, pl.ds(2 * packs, 1)] = piece
                if t > 0:
                    xsmall[t, x, k, pl.ds(0, packs)] = jnp.zeros((packs, LANES), jnp.float32)

    for e, (exists, _) in enumerate(sides_y):
        spot, at = (0, 0) if e == 0 else (tiles, tiles - 1)

        @pl.when(exists)
        def _(e=e, spot=spot, at=at):
            drain(strip_recv[e], strip_sem.at[2 + e])
            drain(strip_seed[e], strip_seed_sem.at[2 + e])
            for k in range(per_column):
                p = (low, high)[e][k]
                piece = strip_recv[e][p]
                packed[spot, k] = piece
                for x, r in ((0, 0), (1, rows - 1)):
                    for n in range(packs):
                        xsmall[at, x, k, pl.ds(e * packs + n, 1)] = piece[n, r : r + 1]
                row = seed_row(strip_seed[e], p)
                piece = row[:, surface - LANES :] if e == 0 else row[:, :LANES]
                edge_marks[spot, k] = jnp.broadcast_to(piece, (ext, LANES))

        @pl.when(jnp.logical_not(exists))
        def _(e=e, at=at):
            for k in range(per_column):
                for x in range(2):
                    xsmall[at, x, k, pl.ds(e * packs, packs)] = jnp.zeros((packs, LANES), jnp.float32)

    for t in range(tiles):
        drain(recv[t].at[pl.ds(0, (gz_n - 1) * slots), pl.ds(0, width[t])], in_sem.at[tiles + t])
        for k in range(per_column):
            block = recv[t][source[k]]
            xsend[t, 0, k] = block[:nfield, :halo]
            xsend[t, 1, k] = block[:nfield, rows - halo :]
            vals[:, t, k, halo : halo + rows, :] = block[:nfield]
            if t < tiles - 1:
                piece = block[nfield:]
                packed[1 + t, k] = piece
                for x, r in ((0, 0), (1, rows - 1)):
                    for n in range(packs):
                        xsmall[t, x, k, pl.ds(packs + n, 1)] = piece[n, r : r + 1]

        for e, (exists, _, device) in enumerate(sides_x):

            @pl.when(exists)
            def _(t=t, e=e, device=device):
                for src, dst, sem in ((xsend, xghost, x_sem), (xsmall, xgsmall, xs_sem)):
                    pltpu.make_async_remote_copy(
                        src_ref=src.at[t, e],
                        dst_ref=dst.at[t, 1 - e],
                        send_sem=sem.at[t, e],
                        recv_sem=sem.at[t, 2 + 1 - e],
                        device_id=device,
                        device_id_type=MESH,
                    ).start()

            @pl.when(jnp.logical_not(exists))
            def _(t=t, e=e):
                for h in range(halo):
                    xghost[t, e, :, :, h : h + 1, :] = xsend[t, e, :, :, halo - 1 - h : halo - h, :]
                xgsmall[t, e] = xsmall[t, e]

    near = (halo - 1, halo + rows)
    first = (0, halo + rows)
    shape = (per_column, ext, LANES)
    lane3 = lax.broadcasted_iota(jnp.int32, shape, 2)
    z_cell = lane3 % cells
    group = lane3 // cells
    last_group = LANES // cells - 1
    row_id = lax.broadcasted_iota(jnp.int32, shape, 1)
    far = lane3 >= LANES // 2

    def mirror(v, e):
        ring = None
        for h in range(halo):
            shift = (2 * h + 1) * cells
            w = rolled(v, shift if e else -shift)
            spot = h if e else last_group - h
            ring = w if ring is None else jnp.where(group == spot, w, ring)
        return ring

    def spread(t, e):
        for n in range(packs):
            unpack[:, halo : halo + rows, :] = packed[e and 1 + t, :, n]
            for x in range(2):
                unpack[:, near[x] : near[x] + 1, :] = xgsmall[t, x, :, pl.ds(e * packs + n, 1), :]
            whole = unpack[...]
            for j in range(min(per_pack, nfield - n * per_pack)):
                shift = -strip_lanes * j if e else -strip_lanes * (j + 1)
                edge[e and 1 + t, n * per_pack + j] = rolled(whole, shift)

    def shift_rows(v, by):
        if ext % 8 == 0:
            return pltpu.roll(v, by % ext, 1)
        cut = by % ext
        return jnp.concatenate([v[:, ext - cut :], v[:, : ext - cut]], 1)

    def around(v, below, above):
        below_y = jnp.where(group == 0, below, rolled(v, cells))
        above_y = jnp.where(group == last_group, above, rolled(v, -cells))
        before_k = jnp.concatenate([v[-1:], v[:-1]], 0)
        after_k = jnp.concatenate([v[1:], v[:1]], 0)
        below_z = jnp.where(z_cell == 0, rolled(before_k, 1 - cells), rolled(v, 1))
        above_z = jnp.where(z_cell == cells - 1, rolled(after_k, cells - 1), rolled(v, -1))
        total = shift_rows(v, 1) + shift_rows(v, -1) + below_y + above_y + below_z + above_z
        return total - 6.0 * v

    x_cell = row_id + (gx * cells + part * rows - halo)
    x_cell = jnp.where(x_cell < 0, -1 - x_cell, x_cell)
    x_end = gx_n * cells
    x_cell = jnp.where(x_cell > x_end - 1, 2 * x_end - 1 - x_cell, x_cell)
    xglob = x_cell.astype(jnp.float32)
    unpack[...] = jnp.zeros_like(unpack)

    for t in range(tiles):
        for e, (exists, _, device) in enumerate(sides_x):

            @pl.when(exists)
            def _(t=t, e=e):
                drain(xghost.at[t, e], x_sem.at[t, 2 + e])
                drain(xgsmall.at[t, e], xs_sem.at[t, 2 + e])

        for k in range(per_column):
            for e in range(2):
                vals[:, t, k, first[e] : first[e] + halo, :] = xghost[t, e, k]
                marks[t, k, near[e] : near[e] + 1, :] = xgsmall[t, e, k, pl.ds(2 * packs, 1)]
        for e, (exists, _) in enumerate(sides_y):
            if e == 0 and t > 0:
                continue
            if e == 1 and t < tiles - 1:
                spread(t, e)
                continue

            @pl.when(exists)
            def _(t=t, e=e):
                spread(t, e)

            @pl.when(jnp.logical_not(exists))
            def _(t=t, e=e):
                for f in range(nfield):
                    edge[e and 1 + t, f] = mirror(vals[f, t], e)
                edge_marks[e and 1 + t] = mirror(marks[t], e)

        def join(low, high):
            return jnp.where(far, low, high) if t == 0 else high

        for step in range(STEPS):
            last = step == STEPS - 1
            if step == 0:
                body = [vals[f, t] for f in range(nfield)]
                rim = [join(edge[0, f], edge[1 + t, f]) for f in range(nfield)]
                seed = (marks[t], join(edge_marks[0], edge_marks[1 + t]))
            else:
                body = [mid[f, t] for f in range(nfield)]
                rim = [mid_edge[f] for f in range(nfield)]

            def laplace(f):
                v, w = body[f], rim[f]
                prior = w if t == 0 else (vals[f, t - 1] if step == 0 else mid[f, t - 1])
                sums = [around(v, rolled(prior, cells), rolled(w, -cells))]
                if not last:
                    sums.append(around(w, rolled(v, cells), rolled(v, -cells)))
                return sums

            def keep(f, i, new):
                if last:
                    result[t, :, f] = new[:, halo : halo + rows]
                elif i == 0:
                    mid[f, t] = new
                else:
                    mid_edge[f] = new

            thermal = xglob / (2.0 * cells) - 1.0 - 0.25 * step
            change = []
            for k in range(NPHASE):
                moved = []
                for i, lap in enumerate(laplace(k)):
                    have = (body, rim)[i]
                    phi = have[k]
                    drive = gain[k] * thermal
                    for j in range(nfield - NPHASE):
                        drive = drive + couple[k, j] * have[NPHASE + j]
                    if step == 0:
                        drive = drive + jnp.where(seed[i] == float(k), SEED_GAIN, 0.0)
                    delta = 0.12 * lap + phi * (1.0 - phi) * (phi - 0.5 + drive)
                    moved.append(delta)
                    keep(k, i, phi + delta)
                change.append(moved)
            for j in range(nfield - NPHASE):
                for i, lap in enumerate(laplace(NPHASE + j)):
                    new = (body, rim)[i][NPHASE + j] + (0.1 * diffuse[j]) * lap
                    for k in range(NPHASE):
                        new = new - latent[j, k] * change[k][i]
                    keep(NPHASE + j, i, new)

        for p in range(places):
            k = depth[p]
            outbuf[t, p // slots, p % slots] = jnp.where(k >= 0, result[t, jnp.maximum(k, 0)], 0.0)
        for d in range(gz_n - 1, 0, -1):
            to = (gz + d) % gz_n
            pltpu.make_async_remote_copy(
                src_ref=outbuf.at[t, to],
                dst_ref=outrecv.at[t, part],
                send_sem=out_sem.at[t],
                recv_sem=out_sem.at[tiles + t],
                device_id=(gx, gy, to),
                device_id_type=MESH,
            ).start()
        outrecv[t, part] = outbuf[t, gz]

    for e, (exists, _) in enumerate(sides_y):

        @pl.when(exists)
        def _(e=e):
            drain(strip.at[e], strip_sem.at[e])
            drain(strip_seed[e], strip_seed_sem.at[e])

    drain(seed_recv.at[pl.ds(0, gz_n - 1)], seed_sem.at[0])
    for t in range(tiles):
        drain(recv[t].at[pl.ds(0, (gz_n - 1) * slots), pl.ds(0, width[t])], in_sem.at[t])
        for e, (exists, _, device) in enumerate(sides_x):

            @pl.when(exists)
            def _(t=t, e=e):
                drain(xsend.at[t, e], x_sem.at[t, e])
                drain(xsmall.at[t, e], xs_sem.at[t, e])

    for t in range(tiles):
        drain(outrecv.at[t, pl.ds(0, gz_n - 1)], out_sem.at[tiles + t])
        for q in range(gz_n):
            out[:, :, q * rows : (q + 1) * rows, t * LANES : (t + 1) * LANES] = outrecv[t, q]
    for t in range(tiles):
        drain(outbuf.at[t, pl.ds(0, gz_n - 1)], out_sem.at[t])


def solution(mesh):
    gx_n, gy_n, gz_n = mesh.shape["gx"], mesh.shape["gy"], mesh.shape["gz"]

    def deep(fields, seeds, *tables):
        slots, nfield, cells, surface = fields.shape
        tables = (tables[0].T,) + tables[1:]
        nblk = tables[0].shape[1]
        column = nblk // (gx_n * gy_n)
        tiles = surface // LANES
        rows = cells // gz_n
        ext = rows + 2 * STEPS
        packs = -(-nfield // (LANES // (STEPS * cells)))
        places = gz_n * slots
        f32, i32 = jnp.float32, jnp.int32
        dma = pltpu.SemaphoreType.DMA
        anyspace = pl.BlockSpec(memory_space=pl.ANY)
        block = (column, ext, LANES)
        faces = (tiles, 2, column, nfield, STEPS, LANES)
        thin = (tiles, 2, column, 2 * packs + 1, LANES)
        return pl.pallas_call(
            functools.partial(deep_kernel, (gx_n, gy_n, gz_n, nblk, cells, surface)),
            out_shape=pltpu.VMEM(fields.shape, f32),
            in_specs=[anyspace] * 9,
            out_specs=pl.BlockSpec(memory_space=pltpu.VMEM),
            scratch_shapes=[pltpu.SMEM(a.shape, a.dtype) for a in tables]
            + [
                dma((len(tables),)),
                pltpu.VMEM(fields.shape, f32),
                pltpu.VMEM((tiles, gz_n, slots, nfield + packs, rows, LANES), f32),
                pltpu.VMEM((gz_n, slots, surface), i32),
                pltpu.VMEM((2, gz_n, slots, packs, rows, LANES), f32),
                pltpu.VMEM((nfield, tiles) + block, f32),
                pltpu.VMEM((tiles + 1, nfield) + block, f32),
                pltpu.VMEM((nfield, tiles) + block, f32),
                pltpu.VMEM((nfield,) + block, f32),
                pltpu.VMEM((tiles,) + block, f32),
                pltpu.VMEM((tiles + 1,) + block, f32),
                pltpu.VMEM(faces, f32),
                pltpu.VMEM(faces, f32),
                pltpu.VMEM(thin, f32),
                pltpu.VMEM(thin, f32),
                pltpu.VMEM((tiles + 1, column, packs, rows, LANES), f32),
                pltpu.VMEM(block, f32),
                pltpu.VMEM((tiles, column, nfield, rows, LANES), f32),
                pltpu.VMEM((tiles, gz_n, slots, nfield, rows, LANES), f32),
                pltpu.VMEM((tiles, gz_n, slots, nfield, rows, LANES), f32),
                dma((2,)),
                dma((2 * tiles,)),
                dma((2,)),
                dma((4,)),
                dma((4,)),
                dma((tiles, 4)),
                dma((tiles, 4)),
                dma((2 * tiles,)),
            ]
            + [pltpu.VMEM((places, packs, rows, LANES), f32)] * 2
            + [pltpu.VMEM((gz_n, slots, surface), i32)] * 2
            + [pltpu.VMEM((places, w, rows, LANES), f32) for w in [nfield + packs] * (tiles - 1) + [nfield]],
            compiler_params=pltpu.CompilerParams(collective_id=0, has_side_effects=True),
        )(fields, seeds, *tables)

    def per_device(fields, seeds, coords, neighbours, before, after, couple, latent, diffuse, gain):
        slots, nfield, cells, surface = fields.shape
        nblk = coords.shape[0]
        per_column = nblk // (gx_n * gy_n)
        halves = surface // LANES
        rows = cells * halves // gz_n
        f32, i32 = jnp.float32, jnp.int32
        dma = pltpu.SemaphoreType.DMA
        smem = pl.BlockSpec(memory_space=pltpu.SMEM)
        anyspace = pl.BlockSpec(memory_space=pl.ANY)
        if cells % gz_n == 0 and cells // gz_n >= STEPS and 2 * STEPS * cells <= LANES:
            return deep(fields, seeds, coords, before, after, couple, latent, diffuse, gain)
        faces_x = (STEPS, 2, per_column, nfield, LANES)
        faces_y = (STEPS, 2, per_column, rows, LANES)
        return pl.pallas_call(
            functools.partial(tile_kernel, (gx_n, gy_n, gz_n, nblk, cells, surface)),
            out_shape=pltpu.VMEM(fields.shape, f32),
            in_specs=[anyspace, anyspace] + [smem] * 7,
            out_specs=pl.BlockSpec(memory_space=pltpu.VMEM),
            scratch_shapes=[
                pltpu.VMEM((gz_n * slots, nfield, rows, LANES), f32),
                pltpu.VMEM((gz_n, slots, LANES), i32),
                pltpu.VMEM((nfield, per_column, rows, LANES), f32),
                pltpu.VMEM(faces_x, f32),
                pltpu.VMEM(faces_x, f32),
                pltpu.VMEM(faces_y, f32),
                pltpu.VMEM(faces_y, f32),
                pltpu.VMEM((STEPS, nfield, per_column, rows, LANES), f32),
                pltpu.VMEM((gz_n, slots, nfield, rows, LANES), f32),
                dma((gz_n,)),
                dma((gz_n,)),
                dma((gz_n,)),
                dma((gz_n,)),
                dma((STEPS, 2)),
                dma((STEPS, 2)),
                dma((STEPS, 2)),
                dma((STEPS, 2)),
                dma((gz_n,)),
                dma((gz_n,)),
                dma((3,)),
            ],
            compiler_params=pltpu.CompilerParams(collective_id=0, has_side_effects=True),
        )(fields, seeds, coords.T, before, after, couple, latent, diffuse, gain)

    placed = (
        P(("gx", "gy", "gz"), None, None, None),
        P(("gx", "gy", "gz"), None),
    ) + (P(),) * 8
    return jax.shard_map(
        per_device,
        mesh=mesh,
        in_specs=placed,
        out_specs=P(("gx", "gy", "gz"), None, None, None),
        check_vma=False,
    )
```

```python
import functools

import jax
import jax.numpy as jnp
from jax import lax
from jax.experimental import pallas as pl
from jax.experimental.pallas import tpu as pltpu
from jax.sharding import PartitionSpec as P

NPHASE = 4
STEPS = 2
LANES = 128
SEED_GAIN = 2.0
MESH = pl.DeviceIdType.MESH


def tile_kernel(
    sizes,
    fields,
    seeds,
    coords,
    before,
    after,
    couple,
    latent,
    diffuse,
    gain,
    out,
    recv,
    seed_recv,
    vals,
    xsend,
    xghost,
    ysend,
    yghost,
    result,
    outbuf,
    in_send,
    in_recv,
    seed_send,
    seed_got,
    x_send,
    x_recv,
    y_send,
    y_recv,
    out_send,
    out_recv,
    local_sem,
):
    gx_n, gy_n, gz_n, nblk, cells, surface = sizes
    slots, nfield = outbuf.shape[1], outbuf.shape[2]
    rows = outbuf.shape[3]
    halves = surface // LANES
    per_column = vals.shape[1]
    x_parts = gz_n // halves
    gx, gy, gz = lax.axis_index("gx"), lax.axis_index("gy"), lax.axis_index("gz")
    odd_x, odd_y = gx % 2, gy % 2

    def part_of(g):
        a, b = g // halves, g % halves
        xh = a + odd_x * (x_parts - 1 - 2 * a)
        yh = b + odd_y * (halves - 1 - 2 * b)
        return xh, yh

    def window(ref, g):
        xh, yh = part_of(g)
        x0 = pl.multiple_of(xh * rows, rows)
        y0 = pl.multiple_of(yh * LANES, LANES)
        return ref.at[:, :, pl.ds(x0, rows), pl.ds(y0, LANES)]

    def seed_window(g):
        _, yh = part_of(g)
        return seeds.at[:, pl.ds(pl.multiple_of(yh * LANES, LANES), LANES)]

    xh, yh = part_of(gz)
    xpos = gx * x_parts + xh
    ypos = gy * halves + yh
    x_total, y_total = gx_n * x_parts, gy_n * halves
    dir_x = 1 - 2 * odd_x
    dir_y = 1 - 2 * odd_y
    xlo_in, xhi_in = xh > 0, xh < x_parts - 1
    ylo_in, yhi_in = yh > 0, yh < halves - 1
    sides = []
    for exists, inside, step_x, step_y, move in (
        (xpos > 0, xlo_in, -1, 0, -halves * dir_x),
        (xpos < x_total - 1, xhi_in, 1, 0, halves * dir_x),
        (ypos > 0, ylo_in, 0, -1, -dir_y),
        (ypos < y_total - 1, yhi_in, 0, 1, dir_y),
    ):
        ins = inside.astype(jnp.int32)
        device = (gx + step_x * (1 - ins), gy + step_y * (1 - ins), gz + move * ins)
        sides.append((exists, inside, device))

    barrier = pltpu.get_barrier_semaphore()
    for d in range(1, gz_n):
        pl.semaphore_signal(
            barrier, inc=1, device_id=(gx, gy, (gz + d) % gz_n), device_id_type=MESH
        )
    expected = gz_n - 1
    for exists, inside, device in sides:
        outside = jnp.logical_and(exists, jnp.logical_not(inside))

        @pl.when(outside)
        def _(device=device):
            pl.semaphore_signal(barrier, inc=1, device_id=device, device_id_type=MESH)

        expected = expected + outside.astype(jnp.int32)
    pl.semaphore_wait(barrier, expected)

    moves = []
    for d in range(gz_n - 1, 0, -1):
        to = (gz + d) % gz_n
        for src, dst, s_sem, r_sem in (
            (window(fields, to), recv.at[pl.ds(slots * gz, slots)], in_send, in_recv),
            (seed_window(to), seed_recv.at[gz], seed_send, seed_got),
        ):
            copy = pltpu.make_async_remote_copy(
                src_ref=src,
                dst_ref=dst,
                send_sem=s_sem.at[d - 1],
                recv_sem=r_sem.at[d - 1],
                device_id=(gx, gy, to),
                device_id_type=MESH,
            )
            copy.start()
            moves.append(copy)
    own = pltpu.make_async_copy(
        window(fields, gz), recv.at[pl.ds(slots * gz, slots)], local_sem.at[0]
    )
    own.start()
    own_seed = pltpu.make_async_copy(seed_window(gz), seed_recv.at[gz], local_sem.at[1])
    own_seed.start()

    base = (gx * gy_n + gy) * (gz_n * slots)
    places = gz_n * slots

    def lookup(b, carry):
        source, depth = carry
        here = jnp.logical_and(coords[0, b] == gx, coords[1, b] == gy)
        z = jnp.where(here, coords[2, b], -1)
        was = before[b] - base
        now = jnp.where(here, after[b] - base, -1)
        source = tuple(jnp.where(z == k, was, source[k]) for k in range(per_column))
        depth = tuple(jnp.where(now == q, z, depth[q]) for q in range(places))
        return source, depth

    source, depth = lax.fori_loop(
        0,
        nblk,
        lookup,
        ((jnp.int32(0),) * per_column, (jnp.int32(-1),) * places),
    )

    own.wait()
    own_seed.wait()
    for copy in moves:
        copy.wait()

    marks = []
    for k in range(per_column):
        p = source[k]
        vals[:, k] = recv[p]
        pair = seed_recv[p // slots]
        row = pair[0:1]
        for s in range(1, slots):
            row = jnp.where(p % slots == s, pair[s : s + 1], row)
        marks.append(row[None])
    marks = jnp.concatenate(marks, 0)

    shape = (per_column, rows, LANES)
    lane = lax.broadcasted_iota(jnp.int32, shape, 2)
    row_id = lax.broadcasted_iota(jnp.int32, shape, 1)
    z_cell = lane % cells
    group = lane // cells
    xglob = (row_id + (gx * cells + xh * rows)).astype(jnp.float32)

    def rolled(v, shift):
        shift = shift % LANES
        return v if shift == 0 else pltpu.roll(v, shift, 2)

    def exchange(step, old):
        low_y = jnp.zeros(shape, jnp.float32)
        high_y = low_y
        for f in range(nfield):
            v = old[f]
            xsend[step, 0, :, f : f + 1, :] = v[:, 0:1, :]
            xsend[step, 1, :, f : f + 1, :] = v[:, rows - 1 : rows, :]
            low_y = jnp.where(group == f, rolled(v, cells * f), low_y)
            high_y = jnp.where(group == f, rolled(v, cells * f + cells), high_y)
        ysend[step, 0] = low_y
        ysend[step, 1] = high_y
        for phase in ("start", "wait"):
            for side, (exists, _, device) in enumerate(sides):
                send, ghost, s_sem, r_sem = (
                    (xsend, xghost, x_send, x_recv)
                    if side < 2
                    else (ysend, yghost, y_send, y_recv)
                )
                e = side % 2

                @pl.when(exists)
                def _(send=send, ghost=ghost, s_sem=s_sem, r_sem=r_sem, e=e, device=device):
                    if phase == "start":
                        pltpu.make_async_remote_copy(
                            src_ref=send.at[step, e],
                            dst_ref=ghost.at[step, 1 - e],
                            send_sem=s_sem.at[step, e],
                            recv_sem=r_sem.at[step, 1 - e],
                            device_id=device,
                            device_id_type=MESH,
                        ).start()
                    else:
                        pltpu.make_async_remote_copy(
                            src_ref=send.at[step, e],
                            dst_ref=ghost.at[step, e],
                            send_sem=s_sem.at[step, e],
                            recv_sem=r_sem.at[step, e],
                            device_id=device,
                            device_id_type=MESH,
                        ).wait()

                if phase == "start":

                    @pl.when(jnp.logical_not(exists))
                    def _(send=send, ghost=ghost, e=e):
                        ghost[step, e] = send[step, e]

    def laplace(step, f, v):
        below_x = jnp.concatenate([xghost[step, 0, :, f : f + 1, :], v[:, :-1, :]], 1)
        above_x = jnp.concatenate([v[:, 1:, :], xghost[step, 1, :, f : f + 1, :]], 1)
        below_y = jnp.where(
            group == 0, rolled(yghost[step, 0], -cells * f), rolled(v, cells)
        )
        above_y = jnp.where(
            group == LANES // cells - 1,
            rolled(yghost[step, 1], -cells * f - cells),
            rolled(v, -cells),
        )
        before_k = jnp.concatenate([v[-1:], v[:-1]], 0)
        after_k = jnp.concatenate([v[1:], v[:1]], 0)
        below_z = jnp.where(z_cell == 0, rolled(before_k, 1 - cells), rolled(v, 1))
        above_z = jnp.where(z_cell == cells - 1, rolled(after_k, cells - 1), rolled(v, -1))
        return below_x + above_x + below_y + above_y + below_z + above_z - 6.0 * v

    for step in range(STEPS):
        src = vals if step == 0 else result.at[step - 1]
        exchange(step, [src[f] for f in range(nfield)])
        thermal = xglob / (2.0 * cells) - 1.0 - 0.25 * step
        change = []
        for k in range(NPHASE):
            phi = src[k]
            drive = gain[k] * thermal
            for j in range(nfield - NPHASE):
                drive = drive + couple[k, j] * src[NPHASE + j]
            if step == 0:
                drive = drive + SEED_GAIN * (marks == k).astype(jnp.float32)
            delta = 0.12 * laplace(step, k, phi) + phi * (1.0 - phi) * (phi - 0.5 + drive)
            new = phi + delta
            result[step, k] = new
            change.append(new - phi)
        for j in range(nfield - NPHASE):
            mu = src[NPHASE + j]
            new = mu + (0.1 * diffuse[j]) * laplace(step, NPHASE + j, mu)
            for k in range(NPHASE):
                new = new - latent[j, k] * change[k]
            result[step, NPHASE + j] = new

    for q in range(places):
        k = depth[q]
        tile = result[STEPS - 1, :, jnp.maximum(k, 0)]
        outbuf[q // slots, q % slots] = jnp.where(k >= 0, tile, 0.0)
    moves = []
    for d in range(gz_n - 1, 0, -1):
        to = (gz + d) % gz_n
        copy = pltpu.make_async_remote_copy(
            src_ref=outbuf.at[to],
            dst_ref=window(out, gz),
            send_sem=out_send.at[d - 1],
            recv_sem=out_recv.at[d - 1],
            device_id=(gx, gy, to),
            device_id_type=MESH,
        )
        copy.start()
        moves.append(copy)
    own = pltpu.make_async_copy(outbuf.at[gz], window(out, gz), local_sem.at[2])
    own.start()
    own.wait()
    for copy in moves:
        copy.wait()


def widths(nfield, tiles, cells):
    per_pack = LANES // (STEPS * cells)
    packs = -(-nfield // per_pack)
    fold = per_pack > 1 and nfield % per_pack == 0
    data = [nfield - packs if fold and t > 0 else nfield for t in range(tiles)]
    return data, [w + (packs if t < tiles - 1 else 0) for t, w in enumerate(data)]


def deep_kernel(sizes, fields, seeds, *refs):
    gx_n, gy_n, gz_n, nblk, cells, surface = sizes
    tables, (
        out,
        coords,
        before,
        after,
        couple,
        latent,
        diffuse,
        gain,
        table_sem,
        mine,
        bulk,
        seed_recv,
        strip,
        vals,
        edge,
        mid,
        mid_edge,
        marks,
        edge_marks,
        xsend,
        xghost,
        xsmall,
        xgsmall,
        packed,
        unpack,
        result,
        outbuf,
        outrecv,
        local_sem,
        in_sem,
        seed_sem,
        strip_sem,
        strip_seed_sem,
        x_sem,
        xs_sem,
        out_sem,
        *arrivals,
    ) = refs[:7], refs[7:]
    slots, nfield = mine.shape[0], mine.shape[1]
    tiles = surface // LANES
    strip_recv, strip_seed, recv = arrivals[:2], arrivals[2:4], arrivals[4:]
    per_column = vals.shape[2]
    rows, halo = cells // gz_n, STEPS
    ext = rows + 2 * halo
    strip_lanes = halo * cells
    per_pack = LANES // strip_lanes
    packs = -(-nfield // per_pack)
    places = gz_n * slots
    data_width, width = widths(nfield, tiles, cells)
    gx, gy, gz = lax.axis_index("gx"), lax.axis_index("gy"), lax.axis_index("gz")
    odd_x = gx % 2
    turn = 1 - 2 * odd_x

    def tile_of(g):
        return g + odd_x * (gz_n - 1 - 2 * g)

    part = tile_of(gz)
    xpos = gx * gz_n + part
    sides_x = []
    for exists, inside, step_x in (
        (xpos > 0, part > 0, -1),
        (xpos < gx_n * gz_n - 1, part < gz_n - 1, 1),
    ):
        ins = inside.astype(jnp.int32)
        device = (gx + step_x * (1 - ins), gy, gz + step_x * turn * ins)
        sides_x.append((exists, inside, device))
    sides_y = ((gy > 0, gy - 1), (gy < gy_n - 1, gy + 1))

    barrier = pltpu.get_barrier_semaphore()
    expected = gz_n - 1
    for d in range(1, gz_n):
        pl.semaphore_signal(
            barrier, inc=1, device_id=(gx, gy, (gz + d) % gz_n), device_id_type=MESH
        )
    for exists, other in sides_y:

        @pl.when(exists)
        def _(other=other):
            for z in range(gz_n):
                pl.semaphore_signal(
                    barrier, inc=1, device_id=(gx, other, z), device_id_type=MESH
                )

        expected = expected + gz_n * exists.astype(jnp.int32)
    for exists, inside, device in sides_x:
        outside = jnp.logical_and(exists, jnp.logical_not(inside))

        @pl.when(outside)
        def _(device=device):
            pl.semaphore_signal(barrier, inc=1, device_id=device, device_id_type=MESH)

        expected = expected + outside.astype(jnp.int32)

    load = pltpu.make_async_copy(fields, mine, local_sem.at[0])
    load.start()
    load_seed = pltpu.make_async_copy(seeds, seed_recv.at[gz], local_sem.at[1])
    load_seed.start()
    small = (coords, before, after, couple, latent, diffuse, gain)
    fetches = [
        pltpu.make_async_copy(src, dst, table_sem.at[n])
        for n, (src, dst) in enumerate(zip(tables, small))
    ]
    for fetch in fetches:
        fetch.start()

    lane = lax.broadcasted_iota(jnp.int32, (1, 1, LANES), 2)

    def rolled(v, shift):
        shift = shift % LANES
        return v if shift == 0 else pltpu.roll(v, shift, 2)

    def pack(s, n, t, e):
        row = None
        for j in range(min(per_pack, nfield - n * per_pack)):
            v = mine[s, pl.ds(n * per_pack + j, 1), :, pl.ds(t * LANES, LANES)]
            v = rolled(v, strip_lanes * (j + e))
            row = v if row is None else jnp.where(lane // strip_lanes == j, v, row)
        return [row[:, q * rows : (q + 1) * rows] for q in range(gz_n)]

    load.wait()
    for s in range(slots):
        for n in range(packs):
            for e, t in ((0, 0), (1, tiles - 1)):
                for q, row in enumerate(pack(s, n, t, e)):
                    strip[e, q, s, pl.ds(n, 1)] = row
            for t in range(tiles - 1):
                for q, row in enumerate(pack(s, n, t + 1, 0)):
                    bulk[t, q, s, pl.ds(data_width[t] + n, 1)] = row
    folds = per_pack - 1
    for t in range(tiles):
        if data_width[t] == nfield:
            for q in range(gz_n):
                bulk[t, q, :, pl.ds(0, nfield)] = mine[
                    :, :, q * rows : (q + 1) * rows, t * LANES : (t + 1) * LANES
                ]
            continue
        for n in range(packs):
            extra = mine[:, n * per_pack + folds, :, t * LANES : (t + 1) * LANES]
            for i in range(folds):
                row = mine[:, n * per_pack + i, :, t * LANES : (t + 1) * LANES]
                row = jnp.where(lane < strip_lanes, rolled(extra, -strip_lanes * (i + 1)), row)
                for q in range(gz_n):
                    bulk[t, q, :, n * folds + i] = row[:, q * rows : (q + 1) * rows]
    pl.semaphore_wait(barrier, expected)

    for e, (exists, other) in enumerate(sides_y):

        @pl.when(exists)
        def _(e=e, other=other):
            for z in range(gz_n):
                pltpu.make_async_remote_copy(
                    src_ref=strip.at[e, tile_of(z)],
                    dst_ref=strip_recv[1 - e].at[pl.ds(slots * gz, slots)],
                    send_sem=strip_sem.at[e],
                    recv_sem=strip_sem.at[2 + 1 - e],
                    device_id=(gx, other, z),
                    device_id_type=MESH,
                ).start()
                pltpu.make_async_remote_copy(
                    src_ref=seeds,
                    dst_ref=strip_seed[1 - e].at[gz],
                    send_sem=strip_seed_sem.at[e],
                    recv_sem=strip_seed_sem.at[2 + 1 - e],
                    device_id=(gx, other, z),
                    device_id_type=MESH,
                ).start()

    for d in range(1, gz_n):
        pltpu.make_async_remote_copy(
            src_ref=seeds,
            dst_ref=seed_recv.at[gz],
            send_sem=seed_sem.at[0],
            recv_sem=seed_sem.at[1],
            device_id=(gx, gy, (gz + d) % gz_n),
            device_id_type=MESH,
        ).start()

    for t in range(tiles):
        for d in range(gz_n - 1, 0, -1):
            to = (gz + d) % gz_n
            pltpu.make_async_remote_copy(
                src_ref=bulk.at[t, tile_of(to), :, pl.ds(0, width[t])],
                dst_ref=recv[t].at[pl.ds(slots * gz, slots), pl.ds(0, width[t])],
                send_sem=in_sem.at[t],
                recv_sem=in_sem.at[tiles + t],
                device_id=(gx, gy, to),
                device_id_type=MESH,
            ).start()
    for t in range(tiles):
        recv[t][pl.ds(slots * gz, slots), pl.ds(0, width[t])] = bulk[t, part, :, pl.ds(0, width[t])]
    for fetch in fetches:
        fetch.wait()

    base = (gx * gy_n + gy) * places

    def lookup(b, carry):
        source, low, high, depth = carry
        cy, z = coords[1, b], coords[2, b]
        same = coords[0, b] == gx
        was, now = before[b] - base, after[b] - base
        here = jnp.where(jnp.logical_and(same, cy == gy), z, -1)
        under = jnp.where(jnp.logical_and(same, cy == gy - 1), z, -1)
        over = jnp.where(jnp.logical_and(same, cy == gy + 1), z, -1)
        now = jnp.where(here >= 0, now, -1)
        source = tuple(jnp.where(here == k, was, source[k]) for k in range(per_column))
        low = tuple(jnp.where(under == k, was + places, low[k]) for k in range(per_column))
        high = tuple(jnp.where(over == k, was - places, high[k]) for k in range(per_column))
        depth = tuple(jnp.where(now == p, z, depth[p]) for p in range(places))
        return source, low, high, depth

    none = (jnp.int32(0),) * per_column
    source, low, high, depth = lax.fori_loop(
        0, nblk, lookup, (none, none, none, (jnp.int32(-1),) * places)
    )

    def drain(ref, sem):
        pltpu.make_async_copy(ref, ref, sem).wait()

    def seed_row(ref, p):
        pair = ref[p // slots]
        row = pair[0:1]
        for s in range(1, slots):
            row = jnp.where(p % slots == s, pair[s : s + 1], row)
        return row.astype(jnp.float32)

    load_seed.wait()
    drain(seed_recv.at[pl.ds(0, gz_n - 1)], seed_sem.at[1])
    for k in range(per_column):
        row = seed_row(seed_recv, source[k])
        for t in range(tiles):
            piece = row[:, t * LANES : (t + 1) * LANES]
            wide = jnp.broadcast_to(piece, (ext, LANES))
            marks[t, k] = wide
            if t > 0:
                edge_marks[t, k] = wide
            for x in range(2):
                xsmall[t, x, k, pl.ds(2 * packs, 1)] = piece
                if t > 0:
                    xsmall[t, x, k, pl.ds(0, packs)] = jnp.zeros((packs, LANES), jnp.float32)

    for e, (exists, _) in enumerate(sides_y):
        spot, at = (0, 0) if e == 0 else (tiles, tiles - 1)

        @pl.when(exists)
        def _(e=e, spot=spot, at=at):
            drain(strip_recv[e], strip_sem.at[2 + e])
            drain(strip_seed[e], strip_seed_sem.at[2 + e])
            for k in range(per_column):
                p = (low, high)[e][k]
                piece = strip_recv[e][p]
                packed[spot, k] = piece
                for x, r in ((0, 0), (1, rows - 1)):
                    for n in range(packs):
                        xsmall[at, x, k, pl.ds(e * packs + n, 1)] = piece[n, r : r + 1]
                row = seed_row(strip_seed[e], p)
                piece = row[:, surface - LANES :] if e == 0 else row[:, :LANES]
                edge_marks[spot, k] = jnp.broadcast_to(piece, (ext, LANES))

        @pl.when(jnp.logical_not(exists))
        def _(e=e, at=at):
            for k in range(per_column):
                for x in range(2):
                    xsmall[at, x, k, pl.ds(e * packs, packs)] = jnp.zeros((packs, LANES), jnp.float32)

    def unfold(block, strips):
        fields_of = []
        for n in range(packs):
            strip_n = strips[n : n + 1]
            extra = rolled(strip_n, -strip_lanes * folds)
            for i in range(folds):
                row = block[n * folds + i : n * folds + i + 1]
                fields_of.append(
                    jnp.where(lane < strip_lanes, rolled(strip_n, -strip_lanes * i), row)
                )
                extra = jnp.where(
                    lane // strip_lanes == i + 1, rolled(row, strip_lanes * (i + 1)), extra
                )
            fields_of.append(extra)
        return fields_of

    for t in range(tiles):
        drain(recv[t].at[pl.ds(0, (gz_n - 1) * slots), pl.ds(0, width[t])], in_sem.at[tiles + t])
        for k in range(per_column):
            block = recv[t][source[k]]
            if data_width[t] == nfield:
                full = block[:nfield]
                xsend[t, 0, k] = full[:, :halo]
                xsend[t, 1, k] = full[:, rows - halo :]
                vals[:, t, k, halo : halo + rows, :] = full
            else:
                for f, v in enumerate(unfold(block, packed[t, k])):
                    xsend[t, 0, k, pl.ds(f, 1)] = v[:, :halo]
                    xsend[t, 1, k, pl.ds(f, 1)] = v[:, rows - halo :]
                    vals[pl.ds(f, 1), t, k, halo : halo + rows, :] = v
            if t < tiles - 1:
                piece = block[data_width[t] :]
                packed[1 + t, k] = piece
                for x, r in ((0, 0), (1, rows - 1)):
                    for n in range(packs):
                        xsmall[t, x, k, pl.ds(packs + n, 1)] = piece[n, r : r + 1]

        for e, (exists, _, device) in enumerate(sides_x):

            @pl.when(exists)
            def _(t=t, e=e, device=device):
                for src, dst, sem in ((xsend, xghost, x_sem), (xsmall, xgsmall, xs_sem)):
                    pltpu.make_async_remote_copy(
                        src_ref=src.at[t, e],
                        dst_ref=dst.at[t, 1 - e],
                        send_sem=sem.at[t, e],
                        recv_sem=sem.at[t, 2 + 1 - e],
                        device_id=device,
                        device_id_type=MESH,
                    ).start()

            @pl.when(jnp.logical_not(exists))
            def _(t=t, e=e):
                for h in range(halo):
                    xghost[t, e, :, :, h : h + 1, :] = xsend[t, e, :, :, halo - 1 - h : halo - h, :]
                xgsmall[t, e] = xsmall[t, e]

    near = (halo - 1, halo + rows)
    first = (0, halo + rows)
    shape = (per_column, ext, LANES)
    lane3 = lax.broadcasted_iota(jnp.int32, shape, 2)
    z_cell = lane3 % cells
    group = lane3 // cells
    last_group = LANES // cells - 1
    row_id = lax.broadcasted_iota(jnp.int32, shape, 1)
    far = lane3 >= LANES // 2

    def mirror(v, e):
        ring = None
        for h in range(halo):
            shift = (2 * h + 1) * cells
            w = rolled(v, shift if e else -shift)
            spot = h if e else last_group - h
            ring = w if ring is None else jnp.where(group == spot, w, ring)
        return ring

    def spread(t, e):
        for n in range(packs):
            unpack[:, halo : halo + rows, :] = packed[e and 1 + t, :, n]
            for x in range(2):
                unpack[:, near[x] : near[x] + 1, :] = xgsmall[t, x, :, pl.ds(e * packs + n, 1), :]
            whole = unpack[...]
            for j in range(min(per_pack, nfield - n * per_pack)):
                shift = -strip_lanes * j if e else -strip_lanes * (j + 1)
                edge[e and 1 + t, n * per_pack + j] = rolled(whole, shift)

    def shift_rows(v, by):
        if ext % 8 == 0:
            return pltpu.roll(v, by % ext, 1)
        cut = by % ext
        return jnp.concatenate([v[:, ext - cut :], v[:, : ext - cut]], 1)

    def around(v, below, above):
        below_y = jnp.where(group == 0, below, rolled(v, cells))
        above_y = jnp.where(group == last_group, above, rolled(v, -cells))
        before_k = jnp.concatenate([v[-1:], v[:-1]], 0)
        after_k = jnp.concatenate([v[1:], v[:1]], 0)
        below_z = jnp.where(z_cell == 0, rolled(before_k, 1 - cells), rolled(v, 1))
        above_z = jnp.where(z_cell == cells - 1, rolled(after_k, cells - 1), rolled(v, -1))
        total = shift_rows(v, 1) + shift_rows(v, -1) + below_y + above_y + below_z + above_z
        return total - 6.0 * v

    x_cell = row_id + (gx * cells + part * rows - halo)
    x_cell = jnp.where(x_cell < 0, -1 - x_cell, x_cell)
    x_end = gx_n * cells
    x_cell = jnp.where(x_cell > x_end - 1, 2 * x_end - 1 - x_cell, x_cell)
    xglob = x_cell.astype(jnp.float32)
    unpack[...] = jnp.zeros_like(unpack)

    for t in range(tiles):
        for e, (exists, _, device) in enumerate(sides_x):

            @pl.when(exists)
            def _(t=t, e=e):
                drain(xghost.at[t, e], x_sem.at[t, 2 + e])
                drain(xgsmall.at[t, e], xs_sem.at[t, 2 + e])

        for k in range(per_column):
            for e in range(2):
                vals[:, t, k, first[e] : first[e] + halo, :] = xghost[t, e, k]
                marks[t, k, near[e] : near[e] + 1, :] = xgsmall[t, e, k, pl.ds(2 * packs, 1)]
        for e, (exists, _) in enumerate(sides_y):
            if e == 0 and t > 0:
                continue
            if e == 1 and t < tiles - 1:
                spread(t, e)
                continue

            @pl.when(exists)
            def _(t=t, e=e):
                spread(t, e)

            @pl.when(jnp.logical_not(exists))
            def _(t=t, e=e):
                for f in range(nfield):
                    edge[e and 1 + t, f] = mirror(vals[f, t], e)
                edge_marks[e and 1 + t] = mirror(marks[t], e)

        def join(low, high):
            return jnp.where(far, low, high) if t == 0 else high

        for step in range(STEPS):
            last = step == STEPS - 1
            if step == 0:
                body = [vals[f, t] for f in range(nfield)]
                rim = [join(edge[0, f], edge[1 + t, f]) for f in range(nfield)]
                seed = (marks[t], join(edge_marks[0], edge_marks[1 + t]))
            else:
                body = [mid[f, t] for f in range(nfield)]
                rim = [mid_edge[f] for f in range(nfield)]

            def laplace(f):
                v, w = body[f], rim[f]
                prior = w if t == 0 else (vals[f, t - 1] if step == 0 else mid[f, t - 1])
                sums = [around(v, rolled(prior, cells), rolled(w, -cells))]
                if not last:
                    sums.append(around(w, rolled(v, cells), rolled(v, -cells)))
                return sums

            def keep(f, i, new):
                if last:
                    result[t, :, f] = new[:, halo : halo + rows]
                elif i == 0:
                    mid[f, t] = new
                else:
                    mid_edge[f] = new

            thermal = xglob / (2.0 * cells) - 1.0 - 0.25 * step
            change = []
            for k in range(NPHASE):
                moved = []
                for i, lap in enumerate(laplace(k)):
                    have = (body, rim)[i]
                    phi = have[k]
                    drive = gain[k] * thermal
                    for j in range(nfield - NPHASE):
                        drive = drive + couple[k, j] * have[NPHASE + j]
                    if step == 0:
                        drive = drive + jnp.where(seed[i] == float(k), SEED_GAIN, 0.0)
                    delta = 0.12 * lap + phi * (1.0 - phi) * (phi - 0.5 + drive)
                    moved.append(delta)
                    keep(k, i, phi + delta)
                change.append(moved)
            for j in range(nfield - NPHASE):
                for i, lap in enumerate(laplace(NPHASE + j)):
                    new = (body, rim)[i][NPHASE + j] + (0.1 * diffuse[j]) * lap
                    for k in range(NPHASE):
                        new = new - latent[j, k] * change[k][i]
                    keep(NPHASE + j, i, new)

        for p in range(places):
            k = depth[p]
            outbuf[t, p // slots, p % slots] = jnp.where(k >= 0, result[t, jnp.maximum(k, 0)], 0.0)
        for d in range(gz_n - 1, 0, -1):
            to = (gz + d) % gz_n
            pltpu.make_async_remote_copy(
                src_ref=outbuf.at[t, to],
                dst_ref=outrecv.at[t, part],
                send_sem=out_sem.at[t],
                recv_sem=out_sem.at[tiles + t],
                device_id=(gx, gy, to),
                device_id_type=MESH,
            ).start()
        outrecv[t, part] = outbuf[t, gz]

    for e, (exists, _) in enumerate(sides_y):

        @pl.when(exists)
        def _(e=e):
            drain(strip.at[e], strip_sem.at[e])
            drain(strip_seed[e], strip_seed_sem.at[e])

    drain(seed_recv.at[pl.ds(0, gz_n - 1)], seed_sem.at[0])
    for t in range(tiles):
        drain(recv[t].at[pl.ds(0, (gz_n - 1) * slots), pl.ds(0, width[t])], in_sem.at[t])
        for e, (exists, _, device) in enumerate(sides_x):

            @pl.when(exists)
            def _(t=t, e=e):
                drain(xsend.at[t, e], x_sem.at[t, e])
                drain(xsmall.at[t, e], xs_sem.at[t, e])

    for t in range(tiles):
        drain(outrecv.at[t, pl.ds(0, gz_n - 1)], out_sem.at[tiles + t])
        for q in range(gz_n):
            out[:, :, q * rows : (q + 1) * rows, t * LANES : (t + 1) * LANES] = outrecv[t, q]
    for t in range(tiles):
        drain(outbuf.at[t, pl.ds(0, gz_n - 1)], out_sem.at[t])


def solution(mesh):
    gx_n, gy_n, gz_n = mesh.shape["gx"], mesh.shape["gy"], mesh.shape["gz"]

    def deep(fields, seeds, *tables):
        slots, nfield, cells, surface = fields.shape
        tables = (tables[0].T,) + tables[1:]
        nblk = tables[0].shape[1]
        column = nblk // (gx_n * gy_n)
        tiles = surface // LANES
        rows = cells // gz_n
        ext = rows + 2 * STEPS
        packs = -(-nfield // (LANES // (STEPS * cells)))
        places = gz_n * slots
        f32, i32 = jnp.float32, jnp.int32
        dma = pltpu.SemaphoreType.DMA
        anyspace = pl.BlockSpec(memory_space=pl.ANY)
        block = (column, ext, LANES)
        faces = (tiles, 2, column, nfield, STEPS, LANES)
        thin = (tiles, 2, column, 2 * packs + 1, LANES)
        return pl.pallas_call(
            functools.partial(deep_kernel, (gx_n, gy_n, gz_n, nblk, cells, surface)),
            out_shape=pltpu.VMEM(fields.shape, f32),
            in_specs=[anyspace] * 9,
            out_specs=pl.BlockSpec(memory_space=pltpu.VMEM),
            scratch_shapes=[pltpu.SMEM(a.shape, a.dtype) for a in tables]
            + [
                dma((len(tables),)),
                pltpu.VMEM(fields.shape, f32),
                pltpu.VMEM((tiles, gz_n, slots, nfield + packs, rows, LANES), f32),
                pltpu.VMEM((gz_n, slots, surface), i32),
                pltpu.VMEM((2, gz_n, slots, packs, rows, LANES), f32),
                pltpu.VMEM((nfield, tiles) + block, f32),
                pltpu.VMEM((tiles + 1, nfield) + block, f32),
                pltpu.VMEM((nfield, tiles) + block, f32),
                pltpu.VMEM((nfield,) + block, f32),
                pltpu.VMEM((tiles,) + block, f32),
                pltpu.VMEM((tiles + 1,) + block, f32),
                pltpu.VMEM(faces, f32),
                pltpu.VMEM(faces, f32),
                pltpu.VMEM(thin, f32),
                pltpu.VMEM(thin, f32),
                pltpu.VMEM((tiles + 1, column, packs, rows, LANES), f32),
                pltpu.VMEM(block, f32),
                pltpu.VMEM((tiles, column, nfield, rows, LANES), f32),
                pltpu.VMEM((tiles, gz_n, slots, nfield, rows, LANES), f32),
                pltpu.VMEM((tiles, gz_n, slots, nfield, rows, LANES), f32),
                dma((2,)),
                dma((2 * tiles,)),
                dma((2,)),
                dma((4,)),
                dma((4,)),
                dma((tiles, 4)),
                dma((tiles, 4)),
                dma((2 * tiles,)),
            ]
            + [pltpu.VMEM((places, packs, rows, LANES), f32)] * 2
            + [pltpu.VMEM((gz_n, slots, surface), i32)] * 2
            + [pltpu.VMEM((places, w, rows, LANES), f32) for w in widths(nfield, tiles, cells)[1]],
            compiler_params=pltpu.CompilerParams(collective_id=0, has_side_effects=True),
        )(fields, seeds, *tables)

    def per_device(fields, seeds, coords, neighbours, before, after, couple, latent, diffuse, gain):
        slots, nfield, cells, surface = fields.shape
        nblk = coords.shape[0]
        per_column = nblk // (gx_n * gy_n)
        halves = surface // LANES
        rows = cells * halves // gz_n
        f32, i32 = jnp.float32, jnp.int32
        dma = pltpu.SemaphoreType.DMA
        smem = pl.BlockSpec(memory_space=pltpu.SMEM)
        anyspace = pl.BlockSpec(memory_space=pl.ANY)
        if cells % gz_n == 0 and cells // gz_n >= STEPS and 2 * STEPS * cells <= LANES:
            return deep(fields, seeds, coords, before, after, couple, latent, diffuse, gain)
        faces_x = (STEPS, 2, per_column, nfield, LANES)
        faces_y = (STEPS, 2, per_column, rows, LANES)
        return pl.pallas_call(
            functools.partial(tile_kernel, (gx_n, gy_n, gz_n, nblk, cells, surface)),
            out_shape=pltpu.VMEM(fields.shape, f32),
            in_specs=[anyspace, anyspace] + [smem] * 7,
            out_specs=pl.BlockSpec(memory_space=pltpu.VMEM),
            scratch_shapes=[
                pltpu.VMEM((gz_n * slots, nfield, rows, LANES), f32),
                pltpu.VMEM((gz_n, slots, LANES), i32),
                pltpu.VMEM((nfield, per_column, rows, LANES), f32),
                pltpu.VMEM(faces_x, f32),
                pltpu.VMEM(faces_x, f32),
                pltpu.VMEM(faces_y, f32),
                pltpu.VMEM(faces_y, f32),
                pltpu.VMEM((STEPS, nfield, per_column, rows, LANES), f32),
                pltpu.VMEM((gz_n, slots, nfield, rows, LANES), f32),
                dma((gz_n,)),
                dma((gz_n,)),
                dma((gz_n,)),
                dma((gz_n,)),
                dma((STEPS, 2)),
                dma((STEPS, 2)),
                dma((STEPS, 2)),
                dma((STEPS, 2)),
                dma((gz_n,)),
                dma((gz_n,)),
                dma((3,)),
            ],
            compiler_params=pltpu.CompilerParams(collective_id=0, has_side_effects=True),
        )(fields, seeds, coords.T, before, after, couple, latent, diffuse, gain)

    placed = (
        P(("gx", "gy", "gz"), None, None, None),
        P(("gx", "gy", "gz"), None),
    ) + (P(),) * 8
    return jax.shard_map(
        per_device,
        mesh=mesh,
        in_specs=placed,
        out_specs=P(("gx", "gy", "gz"), None, None, None),
        check_vma=False,
    )
```

```python
import functools

import jax
import jax.numpy as jnp
from jax import lax
from jax.experimental import pallas as pl
from jax.experimental.pallas import tpu as pltpu
from jax.sharding import PartitionSpec as P

NPHASE = 4
STEPS = 2
LANES = 128
SEED_GAIN = 2.0
MESH = pl.DeviceIdType.MESH


def tile_kernel(
    sizes,
    fields,
    seeds,
    coords,
    before,
    after,
    couple,
    latent,
    diffuse,
    gain,
    out,
    recv,
    seed_recv,
    vals,
    xsend,
    xghost,
    ysend,
    yghost,
    result,
    outbuf,
    in_send,
    in_recv,
    seed_send,
    seed_got,
    x_send,
    x_recv,
    y_send,
    y_recv,
    out_send,
    out_recv,
    local_sem,
):
    gx_n, gy_n, gz_n, nblk, cells, surface = sizes
    slots, nfield = outbuf.shape[1], outbuf.shape[2]
    rows = outbuf.shape[3]
    halves = surface // LANES
    per_column = vals.shape[1]
    x_parts = gz_n // halves
    gx, gy, gz = lax.axis_index("gx"), lax.axis_index("gy"), lax.axis_index("gz")
    odd_x, odd_y = gx % 2, gy % 2

    def part_of(g):
        a, b = g // halves, g % halves
        xh = a + odd_x * (x_parts - 1 - 2 * a)
        yh = b + odd_y * (halves - 1 - 2 * b)
        return xh, yh

    def window(ref, g):
        xh, yh = part_of(g)
        x0 = pl.multiple_of(xh * rows, rows)
        y0 = pl.multiple_of(yh * LANES, LANES)
        return ref.at[:, :, pl.ds(x0, rows), pl.ds(y0, LANES)]

    def seed_window(g):
        _, yh = part_of(g)
        return seeds.at[:, pl.ds(pl.multiple_of(yh * LANES, LANES), LANES)]

    xh, yh = part_of(gz)
    xpos = gx * x_parts + xh
    ypos = gy * halves + yh
    x_total, y_total = gx_n * x_parts, gy_n * halves
    dir_x = 1 - 2 * odd_x
    dir_y = 1 - 2 * odd_y
    xlo_in, xhi_in = xh > 0, xh < x_parts - 1
    ylo_in, yhi_in = yh > 0, yh < halves - 1
    sides = []
    for exists, inside, step_x, step_y, move in (
        (xpos > 0, xlo_in, -1, 0, -halves * dir_x),
        (xpos < x_total - 1, xhi_in, 1, 0, halves * dir_x),
        (ypos > 0, ylo_in, 0, -1, -dir_y),
        (ypos < y_total - 1, yhi_in, 0, 1, dir_y),
    ):
        ins = inside.astype(jnp.int32)
        device = (gx + step_x * (1 - ins), gy + step_y * (1 - ins), gz + move * ins)
        sides.append((exists, inside, device))

    barrier = pltpu.get_barrier_semaphore()
    for d in range(1, gz_n):
        pl.semaphore_signal(
            barrier, inc=1, device_id=(gx, gy, (gz + d) % gz_n), device_id_type=MESH
        )
    expected = gz_n - 1
    for exists, inside, device in sides:
        outside = jnp.logical_and(exists, jnp.logical_not(inside))

        @pl.when(outside)
        def _(device=device):
            pl.semaphore_signal(barrier, inc=1, device_id=device, device_id_type=MESH)

        expected = expected + outside.astype(jnp.int32)
    pl.semaphore_wait(barrier, expected)

    moves = []
    for d in range(gz_n - 1, 0, -1):
        to = (gz + d) % gz_n
        for src, dst, s_sem, r_sem in (
            (window(fields, to), recv.at[pl.ds(slots * gz, slots)], in_send, in_recv),
            (seed_window(to), seed_recv.at[gz], seed_send, seed_got),
        ):
            copy = pltpu.make_async_remote_copy(
                src_ref=src,
                dst_ref=dst,
                send_sem=s_sem.at[d - 1],
                recv_sem=r_sem.at[d - 1],
                device_id=(gx, gy, to),
                device_id_type=MESH,
            )
            copy.start()
            moves.append(copy)
    own = pltpu.make_async_copy(
        window(fields, gz), recv.at[pl.ds(slots * gz, slots)], local_sem.at[0]
    )
    own.start()
    own_seed = pltpu.make_async_copy(seed_window(gz), seed_recv.at[gz], local_sem.at[1])
    own_seed.start()

    base = (gx * gy_n + gy) * (gz_n * slots)
    places = gz_n * slots

    def lookup(b, carry):
        source, depth = carry
        here = jnp.logical_and(coords[0, b] == gx, coords[1, b] == gy)
        z = jnp.where(here, coords[2, b], -1)
        was = before[b] - base
        now = jnp.where(here, after[b] - base, -1)
        source = tuple(jnp.where(z == k, was, source[k]) for k in range(per_column))
        depth = tuple(jnp.where(now == q, z, depth[q]) for q in range(places))
        return source, depth

    source, depth = lax.fori_loop(
        0,
        nblk,
        lookup,
        ((jnp.int32(0),) * per_column, (jnp.int32(-1),) * places),
    )

    own.wait()
    own_seed.wait()
    for copy in moves:
        copy.wait()

    marks = []
    for k in range(per_column):
        p = source[k]
        vals[:, k] = recv[p]
        pair = seed_recv[p // slots]
        row = pair[0:1]
        for s in range(1, slots):
            row = jnp.where(p % slots == s, pair[s : s + 1], row)
        marks.append(row[None])
    marks = jnp.concatenate(marks, 0)

    shape = (per_column, rows, LANES)
    lane = lax.broadcasted_iota(jnp.int32, shape, 2)
    row_id = lax.broadcasted_iota(jnp.int32, shape, 1)
    z_cell = lane % cells
    group = lane // cells
    xglob = (row_id + (gx * cells + xh * rows)).astype(jnp.float32)

    def rolled(v, shift):
        shift = shift % LANES
        return v if shift == 0 else pltpu.roll(v, shift, 2)

    def exchange(step, old):
        low_y = jnp.zeros(shape, jnp.float32)
        high_y = low_y
        for f in range(nfield):
            v = old[f]
            xsend[step, 0, :, f : f + 1, :] = v[:, 0:1, :]
            xsend[step, 1, :, f : f + 1, :] = v[:, rows - 1 : rows, :]
            low_y = jnp.where(group == f, rolled(v, cells * f), low_y)
            high_y = jnp.where(group == f, rolled(v, cells * f + cells), high_y)
        ysend[step, 0] = low_y
        ysend[step, 1] = high_y
        for phase in ("start", "wait"):
            for side, (exists, _, device) in enumerate(sides):
                send, ghost, s_sem, r_sem = (
                    (xsend, xghost, x_send, x_recv)
                    if side < 2
                    else (ysend, yghost, y_send, y_recv)
                )
                e = side % 2

                @pl.when(exists)
                def _(send=send, ghost=ghost, s_sem=s_sem, r_sem=r_sem, e=e, device=device):
                    if phase == "start":
                        pltpu.make_async_remote_copy(
                            src_ref=send.at[step, e],
                            dst_ref=ghost.at[step, 1 - e],
                            send_sem=s_sem.at[step, e],
                            recv_sem=r_sem.at[step, 1 - e],
                            device_id=device,
                            device_id_type=MESH,
                        ).start()
                    else:
                        pltpu.make_async_remote_copy(
                            src_ref=send.at[step, e],
                            dst_ref=ghost.at[step, e],
                            send_sem=s_sem.at[step, e],
                            recv_sem=r_sem.at[step, e],
                            device_id=device,
                            device_id_type=MESH,
                        ).wait()

                if phase == "start":

                    @pl.when(jnp.logical_not(exists))
                    def _(send=send, ghost=ghost, e=e):
                        ghost[step, e] = send[step, e]

    def laplace(step, f, v):
        below_x = jnp.concatenate([xghost[step, 0, :, f : f + 1, :], v[:, :-1, :]], 1)
        above_x = jnp.concatenate([v[:, 1:, :], xghost[step, 1, :, f : f + 1, :]], 1)
        below_y = jnp.where(
            group == 0, rolled(yghost[step, 0], -cells * f), rolled(v, cells)
        )
        above_y = jnp.where(
            group == LANES // cells - 1,
            rolled(yghost[step, 1], -cells * f - cells),
            rolled(v, -cells),
        )
        before_k = jnp.concatenate([v[-1:], v[:-1]], 0)
        after_k = jnp.concatenate([v[1:], v[:1]], 0)
        below_z = jnp.where(z_cell == 0, rolled(before_k, 1 - cells), rolled(v, 1))
        above_z = jnp.where(z_cell == cells - 1, rolled(after_k, cells - 1), rolled(v, -1))
        return below_x + above_x + below_y + above_y + below_z + above_z - 6.0 * v

    for step in range(STEPS):
        src = vals if step == 0 else result.at[step - 1]
        exchange(step, [src[f] for f in range(nfield)])
        thermal = xglob / (2.0 * cells) - 1.0 - 0.25 * step
        change = []
        for k in range(NPHASE):
            phi = src[k]
            drive = gain[k] * thermal
            for j in range(nfield - NPHASE):
                drive = drive + couple[k, j] * src[NPHASE + j]
            if step == 0:
                drive = drive + SEED_GAIN * (marks == k).astype(jnp.float32)
            delta = 0.12 * laplace(step, k, phi) + phi * (1.0 - phi) * (phi - 0.5 + drive)
            new = phi + delta
            result[step, k] = new
            change.append(new - phi)
        for j in range(nfield - NPHASE):
            mu = src[NPHASE + j]
            new = mu + (0.1 * diffuse[j]) * laplace(step, NPHASE + j, mu)
            for k in range(NPHASE):
                new = new - latent[j, k] * change[k]
            result[step, NPHASE + j] = new

    for q in range(places):
        k = depth[q]
        tile = result[STEPS - 1, :, jnp.maximum(k, 0)]
        outbuf[q // slots, q % slots] = jnp.where(k >= 0, tile, 0.0)
    moves = []
    for d in range(gz_n - 1, 0, -1):
        to = (gz + d) % gz_n
        copy = pltpu.make_async_remote_copy(
            src_ref=outbuf.at[to],
            dst_ref=window(out, gz),
            send_sem=out_send.at[d - 1],
            recv_sem=out_recv.at[d - 1],
            device_id=(gx, gy, to),
            device_id_type=MESH,
        )
        copy.start()
        moves.append(copy)
    own = pltpu.make_async_copy(outbuf.at[gz], window(out, gz), local_sem.at[2])
    own.start()
    own.wait()
    for copy in moves:
        copy.wait()


def widths(nfield, tiles, cells):
    per_pack = LANES // (STEPS * cells)
    packs = -(-nfield // per_pack)
    fold = per_pack > 1 and nfield % per_pack == 0
    data = [nfield - packs if fold and t > 0 else nfield for t in range(tiles)]
    return data, [w + (packs if t < tiles - 1 else 0) for t, w in enumerate(data)]


def deep_kernel(sizes, fields, seeds, *refs):
    gx_n, gy_n, gz_n, nblk, cells, surface = sizes
    tables, (
        out,
        coords,
        before,
        after,
        couple,
        latent,
        diffuse,
        gain,
        table_sem,
        mine,
        bulk,
        seed_recv,
        vals,
        edge,
        mid,
        mid_edge,
        marks,
        edge_marks,
        xsend,
        xghost,
        xsmall,
        xgsmall,
        packed,
        unpack,
        ysend,
        yrecv,
        ynear,
        ynear_recv,
        result,
        outbuf,
        outrecv,
        local_sem,
        in_sem,
        seed_sem,
        y_sem,
        yn_sem,
        x_sem,
        xs_sem,
        out_sem,
        *recv,
    ) = refs[:7], refs[7:]
    slots, nfield = mine.shape[0], mine.shape[1]
    tiles = surface // LANES
    per_column = vals.shape[2]
    rows, halo = cells // gz_n, STEPS
    ext = rows + 2 * halo
    strip_lanes = halo * cells
    per_pack = LANES // strip_lanes
    packs = -(-nfield // per_pack)
    places = gz_n * slots
    data_width, width = widths(nfield, tiles, cells)
    gx, gy, gz = lax.axis_index("gx"), lax.axis_index("gy"), lax.axis_index("gz")
    odd_x = gx % 2
    turn = 1 - 2 * odd_x

    def tile_of(g):
        return g + odd_x * (gz_n - 1 - 2 * g)

    part = tile_of(gz)
    xpos = gx * gz_n + part
    sides_x = []
    for exists, inside, step_x in (
        (xpos > 0, part > 0, -1),
        (xpos < gx_n * gz_n - 1, part < gz_n - 1, 1),
    ):
        ins = inside.astype(jnp.int32)
        device = (gx + step_x * (1 - ins), gy, gz + step_x * turn * ins)
        sides_x.append((exists, inside, device))
    odd_y = gy % 2
    sides_y = []
    for other in (gy - 1 + 2 * odd_y, gy + 1 - 2 * odd_y):
        sides_y.append((jnp.logical_and(other >= 0, other < gy_n), other))

    barrier = pltpu.get_barrier_semaphore()
    expected = gz_n - 1
    for d in range(1, gz_n):
        pl.semaphore_signal(
            barrier, inc=1, device_id=(gx, gy, (gz + d) % gz_n), device_id_type=MESH
        )
    targets = [(exists, (gx, other, gz)) for exists, other in sides_y]
    for exists_x, _, device in sides_x:
        for exists_y, other in sides_y:
            both = jnp.logical_and(exists_x, exists_y)
            targets.append((both, (device[0], other, device[2])))
    for exists, device in targets:

        @pl.when(exists)
        def _(device=device):
            pl.semaphore_signal(barrier, inc=1, device_id=device, device_id_type=MESH)

        expected = expected + exists.astype(jnp.int32)
    for exists, inside, device in sides_x:
        outside = jnp.logical_and(exists, jnp.logical_not(inside))

        @pl.when(outside)
        def _(device=device):
            pl.semaphore_signal(barrier, inc=1, device_id=device, device_id_type=MESH)

        expected = expected + outside.astype(jnp.int32)

    load = pltpu.make_async_copy(fields, mine, local_sem.at[0])
    load.start()
    load_seed = pltpu.make_async_copy(seeds, seed_recv.at[gz], local_sem.at[1])
    load_seed.start()
    small = (coords, before, after, couple, latent, diffuse, gain)
    fetches = [
        pltpu.make_async_copy(src, dst, table_sem.at[n])
        for n, (src, dst) in enumerate(zip(tables, small))
    ]
    for fetch in fetches:
        fetch.start()

    lane = lax.broadcasted_iota(jnp.int32, (1, 1, LANES), 2)

    def rolled(v, shift):
        shift = shift % LANES
        return v if shift == 0 else pltpu.roll(v, shift, 2)

    def pack(s, n, t):
        row = None
        for j in range(min(per_pack, nfield - n * per_pack)):
            v = mine[s, pl.ds(n * per_pack + j, 1), :, pl.ds(t * LANES, LANES)]
            v = rolled(v, strip_lanes * j)
            row = v if row is None else jnp.where(lane // strip_lanes == j, v, row)
        return [row[:, q * rows : (q + 1) * rows] for q in range(gz_n)]

    def flipped(v):
        count, size = LANES // cells, 1
        while size < count:
            odd_group = lane // cells // size % 2 == 1
            v = jnp.where(odd_group, rolled(v, size * cells), rolled(v, -size * cells))
            size *= 2
        return v

    load.wait()

    @pl.when(odd_y == 1)
    def _():
        for s in range(slots):
            for t in range((tiles + 1) // 2):
                a, b = pl.ds(t * LANES, LANES), pl.ds((tiles - 1 - t) * LANES, LANES)
                low, high = flipped(mine[s, :, :, a]), flipped(mine[s, :, :, b])
                mine[s, :, :, a] = high
                mine[s, :, :, b] = low

    for s in range(slots):
        for n in range(packs):
            for t in range(tiles - 1):
                for q, row in enumerate(pack(s, n, t + 1)):
                    bulk[t, q, s, pl.ds(data_width[t] + n, 1)] = row
    folds = per_pack - 1
    for t in range(tiles):
        if data_width[t] == nfield:
            for q in range(gz_n):
                bulk[t, q, :, pl.ds(0, nfield)] = mine[
                    :, :, q * rows : (q + 1) * rows, t * LANES : (t + 1) * LANES
                ]
            continue
        for n in range(packs):
            extra = mine[:, n * per_pack + folds, :, t * LANES : (t + 1) * LANES]
            for i in range(folds):
                row = mine[:, n * per_pack + i, :, t * LANES : (t + 1) * LANES]
                row = jnp.where(lane < strip_lanes, rolled(extra, -strip_lanes * (i + 1)), row)
                for q in range(gz_n):
                    bulk[t, q, :, n * folds + i] = row[:, q * rows : (q + 1) * rows]
    pl.semaphore_wait(barrier, expected)

    for d in range(1, gz_n):
        pltpu.make_async_remote_copy(
            src_ref=seeds,
            dst_ref=seed_recv.at[gz],
            send_sem=seed_sem.at[0],
            recv_sem=seed_sem.at[1],
            device_id=(gx, gy, (gz + d) % gz_n),
            device_id_type=MESH,
        ).start()

    for t in range(tiles):
        for d in range(gz_n - 1, 0, -1):
            to = (gz + d) % gz_n
            pltpu.make_async_remote_copy(
                src_ref=bulk.at[t, tile_of(to), :, pl.ds(0, width[t])],
                dst_ref=recv[t].at[pl.ds(slots * gz, slots), pl.ds(0, width[t])],
                send_sem=in_sem.at[t],
                recv_sem=in_sem.at[tiles + t],
                device_id=(gx, gy, to),
                device_id_type=MESH,
            ).start()
    for t in range(tiles):
        recv[t][pl.ds(slots * gz, slots), pl.ds(0, width[t])] = bulk[t, part, :, pl.ds(0, width[t])]
    for fetch in fetches:
        fetch.wait()

    base = (gx * gy_n + gy) * places

    def lookup(b, carry):
        source, depth = carry
        here = jnp.logical_and(coords[0, b] == gx, coords[1, b] == gy)
        z = jnp.where(here, coords[2, b], -1)
        was = before[b] - base
        now = jnp.where(here, after[b] - base, -1)
        source = tuple(jnp.where(z == k, was, source[k]) for k in range(per_column))
        depth = tuple(jnp.where(now == p, z, depth[p]) for p in range(places))
        return source, depth

    source, depth = lax.fori_loop(
        0,
        nblk,
        lookup,
        ((jnp.int32(0),) * per_column, (jnp.int32(-1),) * places),
    )

    def drain(ref, sem):
        pltpu.make_async_copy(ref, ref, sem).wait()

    def seed_row(ref, p):
        pair = ref[p // slots]
        row = pair[0:1]
        for s in range(1, slots):
            row = jnp.where(p % slots == s, pair[s : s + 1], row)
        return row.astype(jnp.float32)

    load_seed.wait()
    drain(seed_recv.at[pl.ds(0, gz_n - 1)], seed_sem.at[1])
    for k in range(per_column):
        row = seed_row(seed_recv, source[k])[None]
        cut = [row[:, :, t * LANES : (t + 1) * LANES] for t in range(tiles)]
        for t in range(tiles):
            piece = jnp.where(odd_y == 1, flipped(cut[tiles - 1 - t]), cut[t])[0]
            wide = jnp.broadcast_to(piece, (ext, LANES))
            marks[t, k] = wide
            if t > 0:
                edge_marks[t, k] = wide
            for x in range(2):
                xsmall[t, x, k, pl.ds(packs, 1)] = piece
                if t == tiles - 1:
                    xsmall[t, x, k, pl.ds(0, packs)] = jnp.zeros((packs, LANES), jnp.float32)

    def unfold(block, strips):
        fields_of = []
        for n in range(packs):
            strip_n = strips[n : n + 1]
            extra = rolled(strip_n, -strip_lanes * folds)
            for i in range(folds):
                row = block[n * folds + i : n * folds + i + 1]
                fields_of.append(
                    jnp.where(lane < strip_lanes, rolled(strip_n, -strip_lanes * i), row)
                )
                extra = jnp.where(
                    lane // strip_lanes == i + 1, rolled(row, strip_lanes * (i + 1)), extra
                )
            fields_of.append(extra)
        return fields_of

    near = (halo - 1, halo + rows)
    first = (0, halo + rows)
    shape = (per_column, ext, LANES)
    lane3 = lax.broadcasted_iota(jnp.int32, shape, 2)
    z_cell = lane3 % cells
    group = lane3 // cells
    last_group = LANES // cells - 1
    row_id = lax.broadcasted_iota(jnp.int32, shape, 1)
    far = lane3 >= LANES // 2

    def mirror(v, e):
        ring = None
        for h in range(halo):
            shift = (2 * h + 1) * cells
            w = rolled(v, shift if e else -shift)
            spot = h if e else last_group - h
            ring = w if ring is None else jnp.where(lane // cells == spot, w, ring)
        return ring

    def outer(t):
        return [e for e, spot in ((0, 0), (1, tiles - 1)) if t == spot]

    def send_strips(t, e, other):
        for n in range(packs):
            row = None
            for j in range(min(per_pack, nfield - n * per_pack)):
                v = mirror(vals[n * per_pack + j, t, :, halo : halo + rows, :], e)
                v = rolled(v, strip_lanes * (j if e else j + 1))
                row = v if row is None else jnp.where(lane // strip_lanes == j, v, row)
            ysend[e, :, n] = row
            for x, r in ((0, 0), (1, rows - 1)):
                ynear[e, x, :, pl.ds(n, 1), :] = row[:, r : r + 1]
        ysend[e, :, packs] = mirror(marks[t], e)[:, halo : halo + rows]
        pltpu.make_async_remote_copy(
            src_ref=ysend.at[e],
            dst_ref=yrecv.at[e],
            send_sem=y_sem.at[e],
            recv_sem=y_sem.at[2 + e],
            device_id=(gx, other, gz),
            device_id_type=MESH,
        ).start()
        for x, (exists, _, device) in enumerate(sides_x):

            @pl.when(exists)
            def _(x=x, device=device):
                pltpu.make_async_remote_copy(
                    src_ref=ynear.at[e, x],
                    dst_ref=ynear_recv.at[e, 1 - x],
                    send_sem=yn_sem.at[e, x],
                    recv_sem=yn_sem.at[e, 2 + 1 - x],
                    device_id=(device[0], other, device[2]),
                    device_id_type=MESH,
                ).start()

    def take_strips(e):
        drain(yrecv.at[e], y_sem.at[2 + e])
        for x, (exists, _, _) in enumerate(sides_x):

            @pl.when(exists)
            def _(x=x):
                drain(ynear_recv.at[e, x], yn_sem.at[e, 2 + x])

            @pl.when(jnp.logical_not(exists))
            def _(x=x):
                r = (rows - 1) * x
                for n in range(packs):
                    ynear_recv[e, x, :, pl.ds(n, 1), :] = yrecv[e, :, n, r : r + 1, :]

    for t in range(tiles):
        drain(recv[t].at[pl.ds(0, (gz_n - 1) * slots), pl.ds(0, width[t])], in_sem.at[tiles + t])
        for k in range(per_column):
            block = recv[t][source[k]]
            if data_width[t] == nfield:
                full = block[:nfield]
                xsend[t, 0, k] = full[:, :halo]
                xsend[t, 1, k] = full[:, rows - halo :]
                vals[:, t, k, halo : halo + rows, :] = full
            else:
                for f, v in enumerate(unfold(block, packed[t - 1, k])):
                    xsend[t, 0, k, pl.ds(f, 1)] = v[:, :halo]
                    xsend[t, 1, k, pl.ds(f, 1)] = v[:, rows - halo :]
                    vals[pl.ds(f, 1), t, k, halo : halo + rows, :] = v
            if t < tiles - 1:
                piece = block[data_width[t] :]
                packed[t, k] = piece
                for x, r in ((0, 0), (1, rows - 1)):
                    for n in range(packs):
                        xsmall[t, x, k, pl.ds(n, 1)] = piece[n, r : r + 1]

        for e in outer(t):
            exists, other = sides_y[e]

            @pl.when(exists)
            def _(t=t, e=e, other=other):
                send_strips(t, e, other)

        for e, (exists, _, device) in enumerate(sides_x):

            @pl.when(exists)
            def _(t=t, e=e, device=device):
                for src, dst, sem in ((xsend, xghost, x_sem), (xsmall, xgsmall, xs_sem)):
                    pltpu.make_async_remote_copy(
                        src_ref=src.at[t, e],
                        dst_ref=dst.at[t, 1 - e],
                        send_sem=sem.at[t, e],
                        recv_sem=sem.at[t, 2 + 1 - e],
                        device_id=device,
                        device_id_type=MESH,
                    ).start()

            @pl.when(jnp.logical_not(exists))
            def _(t=t, e=e):
                for h in range(halo):
                    xghost[t, e, :, :, h : h + 1, :] = xsend[t, e, :, :, halo - 1 - h : halo - h, :]
                xgsmall[t, e] = xsmall[t, e]

    def spread(t, e, inner):
        for n in range(packs):
            unpack[:, halo : halo + rows, :] = packed[t, :, n] if inner else yrecv[e, :, n]
            for x in range(2):
                row = xgsmall[t, x, :, pl.ds(n, 1), :] if inner else ynear_recv[e, x, :, pl.ds(n, 1), :]
                unpack[:, near[x] : near[x] + 1, :] = row
            whole = unpack[...]
            for j in range(min(per_pack, nfield - n * per_pack)):
                shift = -strip_lanes * j if e else -strip_lanes * (j + 1)
                edge[e and 1 + t, n * per_pack + j] = rolled(whole, shift)

    def shift_rows(v, by):
        if ext % 8 == 0:
            return pltpu.roll(v, by % ext, 1)
        cut = by % ext
        return jnp.concatenate([v[:, ext - cut :], v[:, : ext - cut]], 1)

    def around(v, below, above):
        below_y = jnp.where(group == 0, below, rolled(v, cells))
        above_y = jnp.where(group == last_group, above, rolled(v, -cells))
        before_k = jnp.concatenate([v[-1:], v[:-1]], 0)
        after_k = jnp.concatenate([v[1:], v[:1]], 0)
        below_z = jnp.where(z_cell == 0, rolled(before_k, 1 - cells), rolled(v, 1))
        above_z = jnp.where(z_cell == cells - 1, rolled(after_k, cells - 1), rolled(v, -1))
        total = shift_rows(v, 1) + shift_rows(v, -1) + below_y + above_y + below_z + above_z
        return total - 6.0 * v

    x_cell = row_id + (gx * cells + part * rows - halo)
    x_cell = jnp.where(x_cell < 0, -1 - x_cell, x_cell)
    x_end = gx_n * cells
    x_cell = jnp.where(x_cell > x_end - 1, 2 * x_end - 1 - x_cell, x_cell)
    xglob = x_cell.astype(jnp.float32)
    unpack[...] = jnp.zeros_like(unpack)

    for t in range(tiles):
        for e, (exists, _, device) in enumerate(sides_x):

            @pl.when(exists)
            def _(t=t, e=e):
                drain(xghost.at[t, e], x_sem.at[t, 2 + e])
                drain(xgsmall.at[t, e], xs_sem.at[t, 2 + e])

        for k in range(per_column):
            for e in range(2):
                vals[:, t, k, first[e] : first[e] + halo, :] = xghost[t, e, k]
                marks[t, k, near[e] : near[e] + 1, :] = xgsmall[t, e, k, pl.ds(packs, 1)]
        for e, (exists, _) in enumerate(sides_y):
            if e == 0 and t > 0:
                continue
            if e == 1 and t < tiles - 1:
                spread(t, e, True)
                continue

            @pl.when(exists)
            def _(t=t, e=e):
                take_strips(e)
                spread(t, e, False)
                for k in range(per_column):
                    edge_marks[e and 1 + t, k] = jnp.broadcast_to(
                        yrecv[e, k, packs, 0:1, :], (ext, LANES)
                    )

            @pl.when(jnp.logical_not(exists))
            def _(t=t, e=e):
                for f in range(nfield):
                    edge[e and 1 + t, f] = mirror(vals[f, t], e)
                edge_marks[e and 1 + t] = mirror(marks[t], e)

        def send_back(t, at, count):
            for p in range(places):
                k = depth[p]
                tile = result[t, jnp.maximum(k, 0), pl.ds(at, count)]
                outbuf[t, p // slots, p % slots, pl.ds(at, count)] = jnp.where(k >= 0, tile, 0.0)
            for d in range(gz_n - 1, 0, -1):
                to = (gz + d) % gz_n
                pltpu.make_async_remote_copy(
                    src_ref=outbuf.at[t, to, :, pl.ds(at, count)],
                    dst_ref=outrecv.at[t, part, :, pl.ds(at, count)],
                    send_sem=out_sem.at[t],
                    recv_sem=out_sem.at[tiles + t],
                    device_id=(gx, gy, to),
                    device_id_type=MESH,
                ).start()

        def join(low, high):
            return jnp.where(far, low, high) if t == 0 else high

        for step in range(STEPS):
            last = step == STEPS - 1
            if step == 0:
                body = [vals[f, t] for f in range(nfield)]
                rim = [join(edge[0, f], edge[1 + t, f]) for f in range(nfield)]
                seed = (marks[t], join(edge_marks[0], edge_marks[1 + t]))
            else:
                body = [mid[f, t] for f in range(nfield)]
                rim = [mid_edge[f] for f in range(nfield)]

            def laplace(f):
                v, w = body[f], rim[f]
                prior = w if t == 0 else (vals[f, t - 1] if step == 0 else mid[f, t - 1])
                sums = [around(v, rolled(prior, cells), rolled(w, -cells))]
                if not last:
                    sums.append(around(w, rolled(v, cells), rolled(v, -cells)))
                return sums

            def keep(f, i, new):
                if last:
                    result[t, :, f] = new[:, halo : halo + rows]
                elif i == 0:
                    mid[f, t] = new
                else:
                    mid_edge[f] = new

            thermal = xglob / (2.0 * cells) - 1.0 - 0.25 * step
            change = []
            for k in range(NPHASE):
                moved = []
                for i, lap in enumerate(laplace(k)):
                    have = (body, rim)[i]
                    phi = have[k]
                    drive = gain[k] * thermal
                    for j in range(nfield - NPHASE):
                        drive = drive + couple[k, j] * have[NPHASE + j]
                    if step == 0:
                        drive = drive + jnp.where(seed[i] == float(k), SEED_GAIN, 0.0)
                    delta = 0.12 * lap + phi * (1.0 - phi) * (phi - 0.5 + drive)
                    moved.append(delta)
                    keep(k, i, phi + delta)
                change.append(moved)
            if last:
                send_back(t, 0, NPHASE)
            for j in range(nfield - NPHASE):
                for i, lap in enumerate(laplace(NPHASE + j)):
                    new = (body, rim)[i][NPHASE + j] + (0.1 * diffuse[j]) * lap
                    for k in range(NPHASE):
                        new = new - latent[j, k] * change[k][i]
                    keep(NPHASE + j, i, new)

        send_back(t, NPHASE, nfield - NPHASE)
        outrecv[t, part] = outbuf[t, gz]

    for e, (exists, _) in enumerate(sides_y):

        @pl.when(exists)
        def _(e=e):
            drain(ysend.at[e], y_sem.at[e])
            for x, (exists_x, _, _) in enumerate(sides_x):

                @pl.when(exists_x)
                def _(x=x):
                    drain(ynear.at[e, x], yn_sem.at[e, x])

    drain(seed_recv.at[pl.ds(0, gz_n - 1)], seed_sem.at[0])
    for t in range(tiles):
        drain(recv[t].at[pl.ds(0, (gz_n - 1) * slots), pl.ds(0, width[t])], in_sem.at[t])
        for e, (exists, _, device) in enumerate(sides_x):

            @pl.when(exists)
            def _(t=t, e=e):
                drain(xsend.at[t, e], x_sem.at[t, e])
                drain(xsmall.at[t, e], xs_sem.at[t, e])

    for t in range(tiles):
        drain(outrecv.at[t, pl.ds(0, gz_n - 1)], out_sem.at[tiles + t])

        @pl.when(odd_y == 0)
        def _(t=t):
            for q in range(gz_n):
                out[:, :, q * rows : (q + 1) * rows, t * LANES : (t + 1) * LANES] = outrecv[t, q]

        @pl.when(odd_y == 1)
        def _(t=t):
            lanes = pl.ds((tiles - 1 - t) * LANES, LANES)
            for q in range(gz_n):
                for s in range(slots):
                    out[s, :, q * rows : (q + 1) * rows, lanes] = flipped(outrecv[t, q, s])

    for t in range(tiles):
        drain(outbuf.at[t, pl.ds(0, gz_n - 1)], out_sem.at[t])


def solution(mesh):
    gx_n, gy_n, gz_n = mesh.shape["gx"], mesh.shape["gy"], mesh.shape["gz"]

    def deep(fields, seeds, *tables):
        slots, nfield, cells, surface = fields.shape
        tables = (tables[0].T,) + tables[1:]
        nblk = tables[0].shape[1]
        column = nblk // (gx_n * gy_n)
        tiles = surface // LANES
        rows = cells // gz_n
        ext = rows + 2 * STEPS
        packs = -(-nfield // (LANES // (STEPS * cells)))
        places = gz_n * slots
        f32, i32 = jnp.float32, jnp.int32
        dma = pltpu.SemaphoreType.DMA
        anyspace = pl.BlockSpec(memory_space=pl.ANY)
        block = (column, ext, LANES)
        faces = (tiles, 2, column, nfield, STEPS, LANES)
        thin = (tiles, 2, column, packs + 1, LANES)
        return pl.pallas_call(
            functools.partial(deep_kernel, (gx_n, gy_n, gz_n, nblk, cells, surface)),
            out_shape=pltpu.VMEM(fields.shape, f32),
            in_specs=[anyspace] * 9,
            out_specs=pl.BlockSpec(memory_space=pltpu.VMEM),
            scratch_shapes=[pltpu.SMEM(a.shape, a.dtype) for a in tables]
            + [
                dma((len(tables),)),
                pltpu.VMEM(fields.shape, f32),
                pltpu.VMEM((tiles, gz_n, slots, nfield + packs, rows, LANES), f32),
                pltpu.VMEM((gz_n, slots, surface), i32),
                pltpu.VMEM((nfield, tiles) + block, f32),
                pltpu.VMEM((tiles + 1, nfield) + block, f32),
                pltpu.VMEM((nfield, tiles) + block, f32),
                pltpu.VMEM((nfield,) + block, f32),
                pltpu.VMEM((tiles,) + block, f32),
                pltpu.VMEM((tiles + 1,) + block, f32),
                pltpu.VMEM(faces, f32),
                pltpu.VMEM(faces, f32),
                pltpu.VMEM(thin, f32),
                pltpu.VMEM(thin, f32),
                pltpu.VMEM((max(tiles - 1, 1), column, packs, rows, LANES), f32),
                pltpu.VMEM(block, f32),
                pltpu.VMEM((2, column, packs + 1, rows, LANES), f32),
                pltpu.VMEM((2, column, packs + 1, rows, LANES), f32),
                pltpu.VMEM((2, 2, column, packs, LANES), f32),
                pltpu.VMEM((2, 2, column, packs, LANES), f32),
                pltpu.VMEM((tiles, column, nfield, rows, LANES), f32),
                pltpu.VMEM((tiles, gz_n, slots, nfield, rows, LANES), f32),
                pltpu.VMEM((tiles, gz_n, slots, nfield, rows, LANES), f32),
                dma((2,)),
                dma((2 * tiles,)),
                dma((2,)),
                dma((4,)),
                dma((2, 4)),
                dma((tiles, 4)),
                dma((tiles, 4)),
                dma((2 * tiles,)),
            ]
            + [pltpu.VMEM((places, w, rows, LANES), f32) for w in widths(nfield, tiles, cells)[1]],
            compiler_params=pltpu.CompilerParams(collective_id=0, has_side_effects=True),
        )(fields, seeds, *tables)

    def per_device(fields, seeds, coords, neighbours, before, after, couple, latent, diffuse, gain):
        slots, nfield, cells, surface = fields.shape
        nblk = coords.shape[0]
        per_column = nblk // (gx_n * gy_n)
        halves = surface // LANES
        rows = cells * halves // gz_n
        f32, i32 = jnp.float32, jnp.int32
        dma = pltpu.SemaphoreType.DMA
        smem = pl.BlockSpec(memory_space=pltpu.SMEM)
        anyspace = pl.BlockSpec(memory_space=pl.ANY)
        if cells % gz_n == 0 and cells // gz_n >= STEPS and 2 * STEPS * cells <= LANES:
            return deep(fields, seeds, coords, before, after, couple, latent, diffuse, gain)
        faces_x = (STEPS, 2, per_column, nfield, LANES)
        faces_y = (STEPS, 2, per_column, rows, LANES)
        return pl.pallas_call(
            functools.partial(tile_kernel, (gx_n, gy_n, gz_n, nblk, cells, surface)),
            out_shape=pltpu.VMEM(fields.shape, f32),
            in_specs=[anyspace, anyspace] + [smem] * 7,
            out_specs=pl.BlockSpec(memory_space=pltpu.VMEM),
            scratch_shapes=[
                pltpu.VMEM((gz_n * slots, nfield, rows, LANES), f32),
                pltpu.VMEM((gz_n, slots, LANES), i32),
                pltpu.VMEM((nfield, per_column, rows, LANES), f32),
                pltpu.VMEM(faces_x, f32),
                pltpu.VMEM(faces_x, f32),
                pltpu.VMEM(faces_y, f32),
                pltpu.VMEM(faces_y, f32),
                pltpu.VMEM((STEPS, nfield, per_column, rows, LANES), f32),
                pltpu.VMEM((gz_n, slots, nfield, rows, LANES), f32),
                dma((gz_n,)),
                dma((gz_n,)),
                dma((gz_n,)),
                dma((gz_n,)),
                dma((STEPS, 2)),
                dma((STEPS, 2)),
                dma((STEPS, 2)),
                dma((STEPS, 2)),
                dma((gz_n,)),
                dma((gz_n,)),
                dma((3,)),
            ],
            compiler_params=pltpu.CompilerParams(collective_id=0, has_side_effects=True),
        )(fields, seeds, coords.T, before, after, couple, latent, diffuse, gain)

    placed = (
        P(("gx", "gy", "gz"), None, None, None),
        P(("gx", "gy", "gz"), None),
    ) + (P(),) * 8
    return jax.shard_map(
        per_device,
        mesh=mesh,
        in_specs=placed,
        out_specs=P(("gx", "gy", "gz"), None, None, None),
        check_vma=False,
    )
```

```python
import functools

import jax
import jax.numpy as jnp
from jax import lax
from jax.experimental import pallas as pl
from jax.experimental.pallas import tpu as pltpu
from jax.sharding import PartitionSpec as P

NPHASE = 4
STEPS = 2
LANES = 128
SEED_GAIN = 2.0
MESH = pl.DeviceIdType.MESH


def tile_kernel(
    sizes,
    fields,
    seeds,
    coords,
    before,
    after,
    couple,
    latent,
    diffuse,
    gain,
    out,
    recv,
    seed_recv,
    vals,
    xsend,
    xghost,
    ysend,
    yghost,
    result,
    outbuf,
    in_send,
    in_recv,
    seed_send,
    seed_got,
    x_send,
    x_recv,
    y_send,
    y_recv,
    out_send,
    out_recv,
    local_sem,
):
    gx_n, gy_n, gz_n, nblk, cells, surface = sizes
    slots, nfield = outbuf.shape[1], outbuf.shape[2]
    rows = outbuf.shape[3]
    halves = surface // LANES
    per_column = vals.shape[1]
    x_parts = gz_n // halves
    gx, gy, gz = lax.axis_index("gx"), lax.axis_index("gy"), lax.axis_index("gz")
    odd_x, odd_y = gx % 2, gy % 2

    def part_of(g):
        a, b = g // halves, g % halves
        xh = a + odd_x * (x_parts - 1 - 2 * a)
        yh = b + odd_y * (halves - 1 - 2 * b)
        return xh, yh

    def window(ref, g):
        xh, yh = part_of(g)
        x0 = pl.multiple_of(xh * rows, rows)
        y0 = pl.multiple_of(yh * LANES, LANES)
        return ref.at[:, :, pl.ds(x0, rows), pl.ds(y0, LANES)]

    def seed_window(g):
        _, yh = part_of(g)
        return seeds.at[:, pl.ds(pl.multiple_of(yh * LANES, LANES), LANES)]

    xh, yh = part_of(gz)
    xpos = gx * x_parts + xh
    ypos = gy * halves + yh
    x_total, y_total = gx_n * x_parts, gy_n * halves
    dir_x = 1 - 2 * odd_x
    dir_y = 1 - 2 * odd_y
    xlo_in, xhi_in = xh > 0, xh < x_parts - 1
    ylo_in, yhi_in = yh > 0, yh < halves - 1
    sides = []
    for exists, inside, step_x, step_y, move in (
        (xpos > 0, xlo_in, -1, 0, -halves * dir_x),
        (xpos < x_total - 1, xhi_in, 1, 0, halves * dir_x),
        (ypos > 0, ylo_in, 0, -1, -dir_y),
        (ypos < y_total - 1, yhi_in, 0, 1, dir_y),
    ):
        ins = inside.astype(jnp.int32)
        device = (gx + step_x * (1 - ins), gy + step_y * (1 - ins), gz + move * ins)
        sides.append((exists, inside, device))

    barrier = pltpu.get_barrier_semaphore()
    for d in range(1, gz_n):
        pl.semaphore_signal(
            barrier, inc=1, device_id=(gx, gy, (gz + d) % gz_n), device_id_type=MESH
        )
    expected = gz_n - 1
    for exists, inside, device in sides:
        outside = jnp.logical_and(exists, jnp.logical_not(inside))

        @pl.when(outside)
        def _(device=device):
            pl.semaphore_signal(barrier, inc=1, device_id=device, device_id_type=MESH)

        expected = expected + outside.astype(jnp.int32)
    pl.semaphore_wait(barrier, expected)

    moves = []
    for d in range(gz_n - 1, 0, -1):
        to = (gz + d) % gz_n
        for src, dst, s_sem, r_sem in (
            (window(fields, to), recv.at[pl.ds(slots * gz, slots)], in_send, in_recv),
            (seed_window(to), seed_recv.at[gz], seed_send, seed_got),
        ):
            copy = pltpu.make_async_remote_copy(
                src_ref=src,
                dst_ref=dst,
                send_sem=s_sem.at[d - 1],
                recv_sem=r_sem.at[d - 1],
                device_id=(gx, gy, to),
                device_id_type=MESH,
            )
            copy.start()
            moves.append(copy)
    own = pltpu.make_async_copy(
        window(fields, gz), recv.at[pl.ds(slots * gz, slots)], local_sem.at[0]
    )
    own.start()
    own_seed = pltpu.make_async_copy(seed_window(gz), seed_recv.at[gz], local_sem.at[1])
    own_seed.start()

    base = (gx * gy_n + gy) * (gz_n * slots)
    places = gz_n * slots

    def lookup(b, carry):
        source, depth = carry
        here = jnp.logical_and(coords[0, b] == gx, coords[1, b] == gy)
        z = jnp.where(here, coords[2, b], -1)
        was = before[b] - base
        now = jnp.where(here, after[b] - base, -1)
        source = tuple(jnp.where(z == k, was, source[k]) for k in range(per_column))
        depth = tuple(jnp.where(now == q, z, depth[q]) for q in range(places))
        return source, depth

    source, depth = lax.fori_loop(
        0,
        nblk,
        lookup,
        ((jnp.int32(0),) * per_column, (jnp.int32(-1),) * places),
    )

    own.wait()
    own_seed.wait()
    for copy in moves:
        copy.wait()

    marks = []
    for k in range(per_column):
        p = source[k]
        vals[:, k] = recv[p]
        pair = seed_recv[p // slots]
        row = pair[0:1]
        for s in range(1, slots):
            row = jnp.where(p % slots == s, pair[s : s + 1], row)
        marks.append(row[None])
    marks = jnp.concatenate(marks, 0)

    shape = (per_column, rows, LANES)
    lane = lax.broadcasted_iota(jnp.int32, shape, 2)
    row_id = lax.broadcasted_iota(jnp.int32, shape, 1)
    z_cell = lane % cells
    group = lane // cells
    xglob = (row_id + (gx * cells + xh * rows)).astype(jnp.float32)

    def rolled(v, shift):
        shift = shift % LANES
        return v if shift == 0 else pltpu.roll(v, shift, 2)

    def exchange(step, old):
        low_y = jnp.zeros(shape, jnp.float32)
        high_y = low_y
        for f in range(nfield):
            v = old[f]
            xsend[step, 0, :, f : f + 1, :] = v[:, 0:1, :]
            xsend[step, 1, :, f : f + 1, :] = v[:, rows - 1 : rows, :]
            low_y = jnp.where(group == f, rolled(v, cells * f), low_y)
            high_y = jnp.where(group == f, rolled(v, cells * f + cells), high_y)
        ysend[step, 0] = low_y
        ysend[step, 1] = high_y
        for phase in ("start", "wait"):
            for side, (exists, _, device) in enumerate(sides):
                send, ghost, s_sem, r_sem = (
                    (xsend, xghost, x_send, x_recv)
                    if side < 2
                    else (ysend, yghost, y_send, y_recv)
                )
                e = side % 2

                @pl.when(exists)
                def _(send=send, ghost=ghost, s_sem=s_sem, r_sem=r_sem, e=e, device=device):
                    if phase == "start":
                        pltpu.make_async_remote_copy(
                            src_ref=send.at[step, e],
                            dst_ref=ghost.at[step, 1 - e],
                            send_sem=s_sem.at[step, e],
                            recv_sem=r_sem.at[step, 1 - e],
                            device_id=device,
                            device_id_type=MESH,
                        ).start()
                    else:
                        pltpu.make_async_remote_copy(
                            src_ref=send.at[step, e],
                            dst_ref=ghost.at[step, e],
                            send_sem=s_sem.at[step, e],
                            recv_sem=r_sem.at[step, e],
                            device_id=device,
                            device_id_type=MESH,
                        ).wait()

                if phase == "start":

                    @pl.when(jnp.logical_not(exists))
                    def _(send=send, ghost=ghost, e=e):
                        ghost[step, e] = send[step, e]

    def laplace(step, f, v):
        below_x = jnp.concatenate([xghost[step, 0, :, f : f + 1, :], v[:, :-1, :]], 1)
        above_x = jnp.concatenate([v[:, 1:, :], xghost[step, 1, :, f : f + 1, :]], 1)
        below_y = jnp.where(
            group == 0, rolled(yghost[step, 0], -cells * f), rolled(v, cells)
        )
        above_y = jnp.where(
            group == LANES // cells - 1,
            rolled(yghost[step, 1], -cells * f - cells),
            rolled(v, -cells),
        )
        before_k = jnp.concatenate([v[-1:], v[:-1]], 0)
        after_k = jnp.concatenate([v[1:], v[:1]], 0)
        below_z = jnp.where(z_cell == 0, rolled(before_k, 1 - cells), rolled(v, 1))
        above_z = jnp.where(z_cell == cells - 1, rolled(after_k, cells - 1), rolled(v, -1))
        return below_x + above_x + below_y + above_y + below_z + above_z - 6.0 * v

    for step in range(STEPS):
        src = vals if step == 0 else result.at[step - 1]
        exchange(step, [src[f] for f in range(nfield)])
        thermal = xglob / (2.0 * cells) - 1.0 - 0.25 * step
        change = []
        for k in range(NPHASE):
            phi = src[k]
            drive = gain[k] * thermal
            for j in range(nfield - NPHASE):
                drive = drive + couple[k, j] * src[NPHASE + j]
            if step == 0:
                drive = drive + SEED_GAIN * (marks == k).astype(jnp.float32)
            delta = 0.12 * laplace(step, k, phi) + phi * (1.0 - phi) * (phi - 0.5 + drive)
            new = phi + delta
            result[step, k] = new
            change.append(new - phi)
        for j in range(nfield - NPHASE):
            mu = src[NPHASE + j]
            new = mu + (0.1 * diffuse[j]) * laplace(step, NPHASE + j, mu)
            for k in range(NPHASE):
                new = new - latent[j, k] * change[k]
            result[step, NPHASE + j] = new

    for q in range(places):
        k = depth[q]
        tile = result[STEPS - 1, :, jnp.maximum(k, 0)]
        outbuf[q // slots, q % slots] = jnp.where(k >= 0, tile, 0.0)
    moves = []
    for d in range(gz_n - 1, 0, -1):
        to = (gz + d) % gz_n
        copy = pltpu.make_async_remote_copy(
            src_ref=outbuf.at[to],
            dst_ref=window(out, gz),
            send_sem=out_send.at[d - 1],
            recv_sem=out_recv.at[d - 1],
            device_id=(gx, gy, to),
            device_id_type=MESH,
        )
        copy.start()
        moves.append(copy)
    own = pltpu.make_async_copy(outbuf.at[gz], window(out, gz), local_sem.at[2])
    own.start()
    own.wait()
    for copy in moves:
        copy.wait()


def widths(nfield, tiles, cells):
    per_pack = LANES // (STEPS * cells)
    packs = -(-nfield // per_pack)
    fold = per_pack > 1 and nfield % per_pack == 0
    data = [nfield - packs if fold and t > 0 else nfield for t in range(tiles)]
    return data, [w + (packs if t < tiles - 1 else 0) for t, w in enumerate(data)]


def deep_kernel(sizes, fields, seeds, *refs):
    gx_n, gy_n, gz_n, nblk, cells, surface = sizes
    tables, (
        out,
        coords,
        before,
        after,
        couple,
        latent,
        diffuse,
        gain,
        table_sem,
        mine,
        bulk,
        seed_recv,
        vals,
        edge,
        mid,
        mid_edge,
        marks,
        edge_marks,
        xsend,
        xghost,
        xsmall,
        xgsmall,
        packed,
        unpack,
        ysend,
        yrecv,
        ynear,
        ynear_recv,
        result,
        outbuf,
        outrecv,
        local_sem,
        in_sem,
        seed_sem,
        y_sem,
        yn_sem,
        x_sem,
        xs_sem,
        out_sem,
        *recv,
    ) = refs[:7], refs[7:]
    slots, nfield = mine.shape[0], mine.shape[1]
    tiles = surface // LANES
    per_column = vals.shape[2]
    rows, halo = cells // gz_n, STEPS
    ext = rows + 2 * halo
    strip_lanes = halo * cells
    per_pack = LANES // strip_lanes
    packs = -(-nfield // per_pack)
    places = gz_n * slots
    data_width, width = widths(nfield, tiles, cells)
    gx, gy, gz = lax.axis_index("gx"), lax.axis_index("gy"), lax.axis_index("gz")
    odd_x = gx % 2
    turn = 1 - 2 * odd_x

    def tile_of(g):
        return g + odd_x * (gz_n - 1 - 2 * g)

    part = tile_of(gz)
    xpos = gx * gz_n + part
    sides_x = []
    for exists, inside, step_x in (
        (xpos > 0, part > 0, -1),
        (xpos < gx_n * gz_n - 1, part < gz_n - 1, 1),
    ):
        ins = inside.astype(jnp.int32)
        device = (gx + step_x * (1 - ins), gy, gz + step_x * turn * ins)
        sides_x.append((exists, inside, device))
    odd_y = gy % 2
    sides_y = []
    for other in (gy - 1 + 2 * odd_y, gy + 1 - 2 * odd_y):
        sides_y.append((jnp.logical_and(other >= 0, other < gy_n), other))

    barrier = pltpu.get_barrier_semaphore()
    expected = gz_n - 1
    for d in range(1, gz_n):
        pl.semaphore_signal(
            barrier, inc=1, device_id=(gx, gy, (gz + d) % gz_n), device_id_type=MESH
        )
    targets = [(exists, (gx, other, gz)) for exists, other in sides_y]
    for exists_x, _, device in sides_x:
        for exists_y, other in sides_y:
            both = jnp.logical_and(exists_x, exists_y)
            targets.append((both, (device[0], other, device[2])))
    for exists, device in targets:

        @pl.when(exists)
        def _(device=device):
            pl.semaphore_signal(barrier, inc=1, device_id=device, device_id_type=MESH)

        expected = expected + exists.astype(jnp.int32)
    for exists, inside, device in sides_x:
        outside = jnp.logical_and(exists, jnp.logical_not(inside))

        @pl.when(outside)
        def _(device=device):
            pl.semaphore_signal(barrier, inc=1, device_id=device, device_id_type=MESH)

        expected = expected + outside.astype(jnp.int32)

    load = pltpu.make_async_copy(fields, mine, local_sem.at[0])
    load.start()
    load_seed = pltpu.make_async_copy(seeds, seed_recv.at[gz], local_sem.at[1])
    load_seed.start()
    small = (coords, before, after, couple, latent, diffuse, gain)
    fetches = [
        pltpu.make_async_copy(src, dst, table_sem.at[n])
        for n, (src, dst) in enumerate(zip(tables, small))
    ]
    for fetch in fetches:
        fetch.start()

    lane = lax.broadcasted_iota(jnp.int32, (1, 1, LANES), 2)

    def rolled(v, shift):
        shift = shift % LANES
        return v if shift == 0 else pltpu.roll(v, shift, 2)

    def pack(s, n, t):
        row = None
        for j in range(min(per_pack, nfield - n * per_pack)):
            v = mine[s, pl.ds(n * per_pack + j, 1), :, pl.ds(t * LANES, LANES)]
            v = rolled(v, strip_lanes * j)
            row = v if row is None else jnp.where(lane // strip_lanes == j, v, row)
        return [row[:, q * rows : (q + 1) * rows] for q in range(gz_n)]

    def flipped(v):
        count, size = LANES // cells, 1
        while size < count:
            odd_group = lane // cells // size % 2 == 1
            v = jnp.where(odd_group, rolled(v, size * cells), rolled(v, -size * cells))
            size *= 2
        return v

    load.wait()

    @pl.when(odd_y == 1)
    def _():
        for s in range(slots):
            for t in range((tiles + 1) // 2):
                a, b = pl.ds(t * LANES, LANES), pl.ds((tiles - 1 - t) * LANES, LANES)
                low, high = flipped(mine[s, :, :, a]), flipped(mine[s, :, :, b])
                mine[s, :, :, a] = high
                mine[s, :, :, b] = low

    for s in range(slots):
        for n in range(packs):
            for t in range(tiles - 1):
                for q, row in enumerate(pack(s, n, t + 1)):
                    bulk[t, q, s, pl.ds(data_width[t] + n, 1)] = row
    folds = per_pack - 1
    for t in range(tiles):
        if data_width[t] == nfield:
            for q in range(gz_n):
                bulk[t, q, :, pl.ds(0, nfield)] = mine[
                    :, :, q * rows : (q + 1) * rows, t * LANES : (t + 1) * LANES
                ]
            continue
        for n in range(packs):
            extra = mine[:, n * per_pack + folds, :, t * LANES : (t + 1) * LANES]
            for i in range(folds):
                row = mine[:, n * per_pack + i, :, t * LANES : (t + 1) * LANES]
                row = jnp.where(lane < strip_lanes, rolled(extra, -strip_lanes * (i + 1)), row)
                for q in range(gz_n):
                    bulk[t, q, :, n * folds + i] = row[:, q * rows : (q + 1) * rows]
    pl.semaphore_wait(barrier, expected)

    for d in range(1, gz_n):
        pltpu.make_async_remote_copy(
            src_ref=seeds,
            dst_ref=seed_recv.at[gz],
            send_sem=seed_sem.at[0],
            recv_sem=seed_sem.at[1],
            device_id=(gx, gy, (gz + d) % gz_n),
            device_id_type=MESH,
        ).start()

    for t in range(tiles):
        for d in range(gz_n - 1, 0, -1):
            to = (gz + d) % gz_n
            pltpu.make_async_remote_copy(
                src_ref=bulk.at[t, tile_of(to), :, pl.ds(0, width[t])],
                dst_ref=recv[t].at[pl.ds(slots * gz, slots), pl.ds(0, width[t])],
                send_sem=in_sem.at[t],
                recv_sem=in_sem.at[tiles + t],
                device_id=(gx, gy, to),
                device_id_type=MESH,
            ).start()
    for t in range(tiles):
        recv[t][pl.ds(slots * gz, slots), pl.ds(0, width[t])] = bulk[t, part, :, pl.ds(0, width[t])]
    for fetch in fetches:
        fetch.wait()

    base = (gx * gy_n + gy) * places

    def lookup(b, carry):
        source, depth = carry
        here = jnp.logical_and(coords[0, b] == gx, coords[1, b] == gy)
        z = jnp.where(here, coords[2, b], -1)
        was = before[b] - base
        now = jnp.where(here, after[b] - base, -1)
        source = tuple(jnp.where(z == k, was, source[k]) for k in range(per_column))
        depth = tuple(jnp.where(now == p, z, depth[p]) for p in range(places))
        return source, depth

    source, depth = lax.fori_loop(
        0,
        nblk,
        lookup,
        ((jnp.int32(0),) * per_column, (jnp.int32(-1),) * places),
    )

    def drain(ref, sem):
        pltpu.make_async_copy(ref, ref, sem).wait()

    def seed_row(ref, p):
        pair = ref[p // slots]
        row = pair[0:1]
        for s in range(1, slots):
            row = jnp.where(p % slots == s, pair[s : s + 1], row)
        return row.astype(jnp.float32)

    load_seed.wait()
    drain(seed_recv.at[pl.ds(0, gz_n - 1)], seed_sem.at[1])
    for k in range(per_column):
        row = seed_row(seed_recv, source[k])[None]
        cut = [row[:, :, t * LANES : (t + 1) * LANES] for t in range(tiles)]
        for t in range(tiles):
            piece = jnp.where(odd_y == 1, flipped(cut[tiles - 1 - t]), cut[t])[0]
            wide = jnp.broadcast_to(piece, (ext, LANES))
            marks[t, k] = wide
            if t > 0:
                edge_marks[t, k] = wide
            for x in range(2):
                xsmall[t, x, k, pl.ds(packs, 1)] = piece
                if t == tiles - 1:
                    xsmall[t, x, k, pl.ds(0, packs)] = jnp.zeros((packs, LANES), jnp.float32)

    def unfold(block, strips):
        fields_of = []
        for n in range(packs):
            strip_n = strips[n : n + 1]
            extra = rolled(strip_n, -strip_lanes * folds)
            for i in range(folds):
                row = block[n * folds + i : n * folds + i + 1]
                fields_of.append(
                    jnp.where(lane < strip_lanes, rolled(strip_n, -strip_lanes * i), row)
                )
                extra = jnp.where(
                    lane // strip_lanes == i + 1, rolled(row, strip_lanes * (i + 1)), extra
                )
            fields_of.append(extra)
        return fields_of

    near = (halo - 1, halo + rows)
    first = (0, halo + rows)
    shape = (per_column, ext, LANES)
    lane3 = lax.broadcasted_iota(jnp.int32, shape, 2)
    z_cell = lane3 % cells
    group = lane3 // cells
    last_group = LANES // cells - 1
    row_id = lax.broadcasted_iota(jnp.int32, shape, 1)
    far = lane3 >= LANES // 2

    def mirror(v, e):
        ring = None
        for h in range(halo):
            shift = (2 * h + 1) * cells
            w = rolled(v, shift if e else -shift)
            spot = h if e else last_group - h
            ring = w if ring is None else jnp.where(lane // cells == spot, w, ring)
        return ring

    def outer(t):
        return [e for e, spot in ((0, 0), (1, tiles - 1)) if t == spot]

    def send_strips(t, e, other):
        for n in range(packs):
            row = None
            for j in range(min(per_pack, nfield - n * per_pack)):
                v = mirror(vals[n * per_pack + j, t, :, halo : halo + rows, :], e)
                v = rolled(v, strip_lanes * (j if e else j + 1))
                row = v if row is None else jnp.where(lane // strip_lanes == j, v, row)
            ysend[e, :, n] = row
            for x, r in ((0, 0), (1, rows - 1)):
                ynear[e, x, :, pl.ds(n, 1), :] = row[:, r : r + 1]
        ysend[e, :, packs] = mirror(marks[t], e)[:, halo : halo + rows]
        pltpu.make_async_remote_copy(
            src_ref=ysend.at[e],
            dst_ref=yrecv.at[e],
            send_sem=y_sem.at[e],
            recv_sem=y_sem.at[2 + e],
            device_id=(gx, other, gz),
            device_id_type=MESH,
        ).start()
        for x, (exists, _, device) in enumerate(sides_x):

            @pl.when(exists)
            def _(x=x, device=device):
                pltpu.make_async_remote_copy(
                    src_ref=ynear.at[e, x],
                    dst_ref=ynear_recv.at[e, 1 - x],
                    send_sem=yn_sem.at[e, x],
                    recv_sem=yn_sem.at[e, 2 + 1 - x],
                    device_id=(device[0], other, device[2]),
                    device_id_type=MESH,
                ).start()

    def take_strips(e):
        drain(yrecv.at[e], y_sem.at[2 + e])
        for x, (exists, _, _) in enumerate(sides_x):

            @pl.when(exists)
            def _(x=x):
                drain(ynear_recv.at[e, x], yn_sem.at[e, 2 + x])

            @pl.when(jnp.logical_not(exists))
            def _(x=x):
                r = (rows - 1) * x
                for n in range(packs):
                    ynear_recv[e, x, :, pl.ds(n, 1), :] = yrecv[e, :, n, r : r + 1, :]

    for t in range(tiles):
        drain(recv[t].at[pl.ds(0, (gz_n - 1) * slots), pl.ds(0, width[t])], in_sem.at[tiles + t])
        for k in range(per_column):
            block = recv[t][source[k]]
            if data_width[t] == nfield:
                full = block[:nfield]
                xsend[t, 0, k] = full[:, :halo]
                xsend[t, 1, k] = full[:, rows - halo :]
                vals[:, t, k, halo : halo + rows, :] = full
            else:
                for f, v in enumerate(unfold(block, packed[t - 1, k])):
                    xsend[t, 0, k, pl.ds(f, 1)] = v[:, :halo]
                    xsend[t, 1, k, pl.ds(f, 1)] = v[:, rows - halo :]
                    vals[pl.ds(f, 1), t, k, halo : halo + rows, :] = v
            if t < tiles - 1:
                piece = block[data_width[t] :]
                packed[t, k] = piece
                for x, r in ((0, 0), (1, rows - 1)):
                    for n in range(packs):
                        xsmall[t, x, k, pl.ds(n, 1)] = piece[n, r : r + 1]

        for e in outer(t):
            exists, other = sides_y[e]

            @pl.when(exists)
            def _(t=t, e=e, other=other):
                send_strips(t, e, other)

        for e, (exists, _, device) in enumerate(sides_x):

            @pl.when(exists)
            def _(t=t, e=e, device=device):
                for src, dst, sem in ((xsend, xghost, x_sem), (xsmall, xgsmall, xs_sem)):
                    pltpu.make_async_remote_copy(
                        src_ref=src.at[t, e],
                        dst_ref=dst.at[t, 1 - e],
                        send_sem=sem.at[t, e],
                        recv_sem=sem.at[t, 2 + 1 - e],
                        device_id=device,
                        device_id_type=MESH,
                    ).start()

            @pl.when(jnp.logical_not(exists))
            def _(t=t, e=e):
                for h in range(halo):
                    xghost[t, e, :, :, h : h + 1, :] = xsend[t, e, :, :, halo - 1 - h : halo - h, :]
                xgsmall[t, e] = xsmall[t, e]

    def spread(t, e, inner):
        for n in range(packs):
            unpack[:, halo : halo + rows, :] = packed[t, :, n] if inner else yrecv[e, :, n]
            for x in range(2):
                row = xgsmall[t, x, :, pl.ds(n, 1), :] if inner else ynear_recv[e, x, :, pl.ds(n, 1), :]
                unpack[:, near[x] : near[x] + 1, :] = row
            whole = unpack[...]
            for j in range(min(per_pack, nfield - n * per_pack)):
                shift = -strip_lanes * j if e else -strip_lanes * (j + 1)
                edge[e and 1 + t, n * per_pack + j] = rolled(whole, shift)

    def shift_rows(v, by):
        if ext % 8 == 0:
            return pltpu.roll(v, by % ext, 1)
        cut = by % ext
        return jnp.concatenate([v[:, ext - cut :], v[:, : ext - cut]], 1)

    def around(v, below, above):
        below_y = jnp.where(group == 0, below, rolled(v, cells))
        above_y = jnp.where(group == last_group, above, rolled(v, -cells))
        before_k = jnp.concatenate([v[-1:], v[:-1]], 0)
        after_k = jnp.concatenate([v[1:], v[:1]], 0)
        below_z = jnp.where(z_cell == 0, rolled(before_k, 1 - cells), rolled(v, 1))
        above_z = jnp.where(z_cell == cells - 1, rolled(after_k, cells - 1), rolled(v, -1))
        total = shift_rows(v, 1) + shift_rows(v, -1) + below_y + above_y + below_z + above_z
        return total - 6.0 * v

    x_cell = row_id + (gx * cells + part * rows - halo)
    x_cell = jnp.where(x_cell < 0, -1 - x_cell, x_cell)
    x_end = gx_n * cells
    x_cell = jnp.where(x_cell > x_end - 1, 2 * x_end - 1 - x_cell, x_cell)
    xglob = x_cell.astype(jnp.float32)
    unpack[...] = jnp.zeros_like(unpack)

    for t in range(tiles):
        for e, (exists, _, device) in enumerate(sides_x):

            @pl.when(exists)
            def _(t=t, e=e):
                drain(xghost.at[t, e], x_sem.at[t, 2 + e])
                drain(xgsmall.at[t, e], xs_sem.at[t, 2 + e])

        for k in range(per_column):
            for e in range(2):
                vals[:, t, k, first[e] : first[e] + halo, :] = xghost[t, e, k]
                marks[t, k, near[e] : near[e] + 1, :] = xgsmall[t, e, k, pl.ds(packs, 1)]
        for e, (exists, _) in enumerate(sides_y):
            if e == 0 and t > 0:
                continue
            if e == 1 and t < tiles - 1:
                spread(t, e, True)
                continue

            @pl.when(exists)
            def _(t=t, e=e):
                take_strips(e)
                spread(t, e, False)
                for k in range(per_column):
                    edge_marks[e and 1 + t, k] = jnp.broadcast_to(
                        yrecv[e, k, packs, 0:1, :], (ext, LANES)
                    )

            @pl.when(jnp.logical_not(exists))
            def _(t=t, e=e):
                for f in range(nfield):
                    edge[e and 1 + t, f] = mirror(vals[f, t], e)
                edge_marks[e and 1 + t] = mirror(marks[t], e)

        def collect(t, at, count):
            for p in range(places):
                k = depth[p]
                tile = result[t, jnp.maximum(k, 0), pl.ds(at, count)]
                outbuf[t, p // slots, p % slots, pl.ds(at, count)] = jnp.where(k >= 0, tile, 0.0)

        def send_back(t, at, count, order):
            for n in order:
                to = n + (gz <= n).astype(jnp.int32)
                pltpu.make_async_remote_copy(
                    src_ref=outbuf.at[t, to, :, pl.ds(at, count)],
                    dst_ref=outrecv.at[t, part, :, pl.ds(at, count)],
                    send_sem=out_sem.at[t],
                    recv_sem=out_sem.at[tiles + t],
                    device_id=(gx, gy, to),
                    device_id_type=MESH,
                ).start()

        def join(low, high):
            return jnp.where(far, low, high) if t == 0 else high

        for step in range(STEPS):
            last = step == STEPS - 1
            if step == 0:
                body = [vals[f, t] for f in range(nfield)]
                rim = [join(edge[0, f], edge[1 + t, f]) for f in range(nfield)]
                seed = (marks[t], join(edge_marks[0], edge_marks[1 + t]))
            else:
                body = [mid[f, t] for f in range(nfield)]
                rim = [mid_edge[f] for f in range(nfield)]

            def laplace(f):
                v, w = body[f], rim[f]
                prior = w if t == 0 else (vals[f, t - 1] if step == 0 else mid[f, t - 1])
                sums = [around(v, rolled(prior, cells), rolled(w, -cells))]
                if not last:
                    sums.append(around(w, rolled(v, cells), rolled(v, -cells)))
                return sums

            def keep(f, i, new):
                if last:
                    result[t, :, f] = new[:, halo : halo + rows]
                elif i == 0:
                    mid[f, t] = new
                else:
                    mid_edge[f] = new

            thermal = xglob / (2.0 * cells) - 1.0 - 0.25 * step
            change = []
            for k in range(NPHASE):
                moved = []
                for i, lap in enumerate(laplace(k)):
                    have = (body, rim)[i]
                    phi = have[k]
                    drive = gain[k] * thermal
                    for j in range(nfield - NPHASE):
                        drive = drive + couple[k, j] * have[NPHASE + j]
                    if step == 0:
                        drive = drive + jnp.where(seed[i] == float(k), SEED_GAIN, 0.0)
                    delta = 0.12 * lap + phi * (1.0 - phi) * (phi - 0.5 + drive)
                    moved.append(delta)
                    keep(k, i, phi + delta)
                change.append(moved)
            if last:
                collect(t, 0, NPHASE)
                send_back(t, 0, NPHASE, range(gz_n - 1) if t < tiles - 1 else [0])
            for j in range(nfield - NPHASE):
                for i, lap in enumerate(laplace(NPHASE + j)):
                    new = (body, rim)[i][NPHASE + j] + (0.1 * diffuse[j]) * lap
                    for k in range(NPHASE):
                        new = new - latent[j, k] * change[k][i]
                    keep(NPHASE + j, i, new)

        collect(t, NPHASE, nfield - NPHASE)
        early = range(gz_n - 1) if t < tiles - 1 else [0]
        send_back(t, NPHASE, nfield - NPHASE, early)
        send_back(t, 0, nfield, [n for n in range(gz_n - 1) if n not in early])
        outrecv[t, part] = outbuf[t, gz]

    for e, (exists, _) in enumerate(sides_y):

        @pl.when(exists)
        def _(e=e):
            drain(ysend.at[e], y_sem.at[e])
            for x, (exists_x, _, _) in enumerate(sides_x):

                @pl.when(exists_x)
                def _(x=x):
                    drain(ynear.at[e, x], yn_sem.at[e, x])

    drain(seed_recv.at[pl.ds(0, gz_n - 1)], seed_sem.at[0])
    for t in range(tiles):
        drain(recv[t].at[pl.ds(0, (gz_n - 1) * slots), pl.ds(0, width[t])], in_sem.at[t])
        for e, (exists, _, device) in enumerate(sides_x):

            @pl.when(exists)
            def _(t=t, e=e):
                drain(xsend.at[t, e], x_sem.at[t, e])
                drain(xsmall.at[t, e], xs_sem.at[t, e])

    for t in range(tiles):
        drain(outrecv.at[t, pl.ds(0, gz_n - 1)], out_sem.at[tiles + t])

        @pl.when(odd_y == 0)
        def _(t=t):
            for q in range(gz_n):
                out[:, :, q * rows : (q + 1) * rows, t * LANES : (t + 1) * LANES] = outrecv[t, q]

        @pl.when(odd_y == 1)
        def _(t=t):
            lanes = pl.ds((tiles - 1 - t) * LANES, LANES)
            for q in range(gz_n):
                for s in range(slots):
                    out[s, :, q * rows : (q + 1) * rows, lanes] = flipped(outrecv[t, q, s])

    for t in range(tiles):
        drain(outbuf.at[t, pl.ds(0, gz_n - 1)], out_sem.at[t])


def solution(mesh):
    gx_n, gy_n, gz_n = mesh.shape["gx"], mesh.shape["gy"], mesh.shape["gz"]

    def deep(fields, seeds, *tables):
        slots, nfield, cells, surface = fields.shape
        tables = (tables[0].T,) + tables[1:]
        nblk = tables[0].shape[1]
        column = nblk // (gx_n * gy_n)
        tiles = surface // LANES
        rows = cells // gz_n
        ext = rows + 2 * STEPS
        packs = -(-nfield // (LANES // (STEPS * cells)))
        places = gz_n * slots
        f32, i32 = jnp.float32, jnp.int32
        dma = pltpu.SemaphoreType.DMA
        anyspace = pl.BlockSpec(memory_space=pl.ANY)
        block = (column, ext, LANES)
        faces = (tiles, 2, column, nfield, STEPS, LANES)
        thin = (tiles, 2, column, packs + 1, LANES)
        return pl.pallas_call(
            functools.partial(deep_kernel, (gx_n, gy_n, gz_n, nblk, cells, surface)),
            out_shape=pltpu.VMEM(fields.shape, f32),
            in_specs=[anyspace] * 9,
            out_specs=pl.BlockSpec(memory_space=pltpu.VMEM),
            scratch_shapes=[pltpu.SMEM(a.shape, a.dtype) for a in tables]
            + [
                dma((len(tables),)),
                pltpu.VMEM(fields.shape, f32),
                pltpu.VMEM((tiles, gz_n, slots, nfield + packs, rows, LANES), f32),
                pltpu.VMEM((gz_n, slots, surface), i32),
                pltpu.VMEM((nfield, tiles) + block, f32),
                pltpu.VMEM((tiles + 1, nfield) + block, f32),
                pltpu.VMEM((nfield, tiles) + block, f32),
                pltpu.VMEM((nfield,) + block, f32),
                pltpu.VMEM((tiles,) + block, f32),
                pltpu.VMEM((tiles + 1,) + block, f32),
                pltpu.VMEM(faces, f32),
                pltpu.VMEM(faces, f32),
                pltpu.VMEM(thin, f32),
                pltpu.VMEM(thin, f32),
                pltpu.VMEM((max(tiles - 1, 1), column, packs, rows, LANES), f32),
                pltpu.VMEM(block, f32),
                pltpu.VMEM((2, column, packs + 1, rows, LANES), f32),
                pltpu.VMEM((2, column, packs + 1, rows, LANES), f32),
                pltpu.VMEM((2, 2, column, packs, LANES), f32),
                pltpu.VMEM((2, 2, column, packs, LANES), f32),
                pltpu.VMEM((tiles, column, nfield, rows, LANES), f32),
                pltpu.VMEM((tiles, gz_n, slots, nfield, rows, LANES), f32),
                pltpu.VMEM((tiles, gz_n, slots, nfield, rows, LANES), f32),
                dma((2,)),
                dma((2 * tiles,)),
                dma((2,)),
                dma((4,)),
                dma((2, 4)),
                dma((tiles, 4)),
                dma((tiles, 4)),
                dma((2 * tiles,)),
            ]
            + [pltpu.VMEM((places, w, rows, LANES), f32) for w in widths(nfield, tiles, cells)[1]],
            compiler_params=pltpu.CompilerParams(collective_id=0, has_side_effects=True),
        )(fields, seeds, *tables)

    def per_device(fields, seeds, coords, neighbours, before, after, couple, latent, diffuse, gain):
        slots, nfield, cells, surface = fields.shape
        nblk = coords.shape[0]
        per_column = nblk // (gx_n * gy_n)
        halves = surface // LANES
        rows = cells * halves // gz_n
        f32, i32 = jnp.float32, jnp.int32
        dma = pltpu.SemaphoreType.DMA
        smem = pl.BlockSpec(memory_space=pltpu.SMEM)
        anyspace = pl.BlockSpec(memory_space=pl.ANY)
        if cells % gz_n == 0 and cells // gz_n >= STEPS and 2 * STEPS * cells <= LANES:
            return deep(fields, seeds, coords, before, after, couple, latent, diffuse, gain)
        faces_x = (STEPS, 2, per_column, nfield, LANES)
        faces_y = (STEPS, 2, per_column, rows, LANES)
        return pl.pallas_call(
            functools.partial(tile_kernel, (gx_n, gy_n, gz_n, nblk, cells, surface)),
            out_shape=pltpu.VMEM(fields.shape, f32),
            in_specs=[anyspace, anyspace] + [smem] * 7,
            out_specs=pl.BlockSpec(memory_space=pltpu.VMEM),
            scratch_shapes=[
                pltpu.VMEM((gz_n * slots, nfield, rows, LANES), f32),
                pltpu.VMEM((gz_n, slots, LANES), i32),
                pltpu.VMEM((nfield, per_column, rows, LANES), f32),
                pltpu.VMEM(faces_x, f32),
                pltpu.VMEM(faces_x, f32),
                pltpu.VMEM(faces_y, f32),
                pltpu.VMEM(faces_y, f32),
                pltpu.VMEM((STEPS, nfield, per_column, rows, LANES), f32),
                pltpu.VMEM((gz_n, slots, nfield, rows, LANES), f32),
                dma((gz_n,)),
                dma((gz_n,)),
                dma((gz_n,)),
                dma((gz_n,)),
                dma((STEPS, 2)),
                dma((STEPS, 2)),
                dma((STEPS, 2)),
                dma((STEPS, 2)),
                dma((gz_n,)),
                dma((gz_n,)),
                dma((3,)),
            ],
            compiler_params=pltpu.CompilerParams(collective_id=0, has_side_effects=True),
        )(fields, seeds, coords.T, before, after, couple, latent, diffuse, gain)

    placed = (
        P(("gx", "gy", "gz"), None, None, None),
        P(("gx", "gy", "gz"), None),
    ) + (P(),) * 8
    return jax.shard_map(
        per_device,
        mesh=mesh,
        in_specs=placed,
        out_specs=P(("gx", "gy", "gz"), None, None, None),
        check_vma=False,
    )
```

```python
import functools

import jax
import jax.numpy as jnp
from jax import lax
from jax.experimental import pallas as pl
from jax.experimental.pallas import tpu as pltpu
from jax.sharding import PartitionSpec as P

NPHASE = 4
STEPS = 2
LANES = 128
SEED_GAIN = 2.0
MESH = pl.DeviceIdType.MESH


def tile_kernel(
    sizes,
    fields,
    seeds,
    coords,
    before,
    after,
    couple,
    latent,
    diffuse,
    gain,
    out,
    recv,
    seed_recv,
    vals,
    xsend,
    xghost,
    ysend,
    yghost,
    result,
    outbuf,
    in_send,
    in_recv,
    seed_send,
    seed_got,
    x_send,
    x_recv,
    y_send,
    y_recv,
    out_send,
    out_recv,
    local_sem,
):
    gx_n, gy_n, gz_n, nblk, cells, surface = sizes
    slots, nfield = outbuf.shape[1], outbuf.shape[2]
    rows = outbuf.shape[3]
    halves = surface // LANES
    per_column = vals.shape[1]
    x_parts = gz_n // halves
    gx, gy, gz = lax.axis_index("gx"), lax.axis_index("gy"), lax.axis_index("gz")
    odd_x, odd_y = gx % 2, gy % 2

    def part_of(g):
        a, b = g // halves, g % halves
        xh = a + odd_x * (x_parts - 1 - 2 * a)
        yh = b + odd_y * (halves - 1 - 2 * b)
        return xh, yh

    def window(ref, g):
        xh, yh = part_of(g)
        x0 = pl.multiple_of(xh * rows, rows)
        y0 = pl.multiple_of(yh * LANES, LANES)
        return ref.at[:, :, pl.ds(x0, rows), pl.ds(y0, LANES)]

    def seed_window(g):
        _, yh = part_of(g)
        return seeds.at[:, pl.ds(pl.multiple_of(yh * LANES, LANES), LANES)]

    xh, yh = part_of(gz)
    xpos = gx * x_parts + xh
    ypos = gy * halves + yh
    x_total, y_total = gx_n * x_parts, gy_n * halves
    dir_x = 1 - 2 * odd_x
    dir_y = 1 - 2 * odd_y
    xlo_in, xhi_in = xh > 0, xh < x_parts - 1
    ylo_in, yhi_in = yh > 0, yh < halves - 1
    sides = []
    for exists, inside, step_x, step_y, move in (
        (xpos > 0, xlo_in, -1, 0, -halves * dir_x),
        (xpos < x_total - 1, xhi_in, 1, 0, halves * dir_x),
        (ypos > 0, ylo_in, 0, -1, -dir_y),
        (ypos < y_total - 1, yhi_in, 0, 1, dir_y),
    ):
        ins = inside.astype(jnp.int32)
        device = (gx + step_x * (1 - ins), gy + step_y * (1 - ins), gz + move * ins)
        sides.append((exists, inside, device))

    barrier = pltpu.get_barrier_semaphore()
    for d in range(1, gz_n):
        pl.semaphore_signal(
            barrier, inc=1, device_id=(gx, gy, (gz + d) % gz_n), device_id_type=MESH
        )
    expected = gz_n - 1
    for exists, inside, device in sides:
        outside = jnp.logical_and(exists, jnp.logical_not(inside))

        @pl.when(outside)
        def _(device=device):
            pl.semaphore_signal(barrier, inc=1, device_id=device, device_id_type=MESH)

        expected = expected + outside.astype(jnp.int32)
    pl.semaphore_wait(barrier, expected)

    moves = []
    for d in range(gz_n - 1, 0, -1):
        to = (gz + d) % gz_n
        for src, dst, s_sem, r_sem in (
            (window(fields, to), recv.at[pl.ds(slots * gz, slots)], in_send, in_recv),
            (seed_window(to), seed_recv.at[gz], seed_send, seed_got),
        ):
            copy = pltpu.make_async_remote_copy(
                src_ref=src,
                dst_ref=dst,
                send_sem=s_sem.at[d - 1],
                recv_sem=r_sem.at[d - 1],
                device_id=(gx, gy, to),
                device_id_type=MESH,
            )
            copy.start()
            moves.append(copy)
    own = pltpu.make_async_copy(
        window(fields, gz), recv.at[pl.ds(slots * gz, slots)], local_sem.at[0]
    )
    own.start()
    own_seed = pltpu.make_async_copy(seed_window(gz), seed_recv.at[gz], local_sem.at[1])
    own_seed.start()

    base = (gx * gy_n + gy) * (gz_n * slots)
    places = gz_n * slots

    def lookup(b, carry):
        source, depth = carry
        here = jnp.logical_and(coords[0, b] == gx, coords[1, b] == gy)
        z = jnp.where(here, coords[2, b], -1)
        was = before[b] - base
        now = jnp.where(here, after[b] - base, -1)
        source = tuple(jnp.where(z == k, was, source[k]) for k in range(per_column))
        depth = tuple(jnp.where(now == q, z, depth[q]) for q in range(places))
        return source, depth

    source, depth = lax.fori_loop(
        0,
        nblk,
        lookup,
        ((jnp.int32(0),) * per_column, (jnp.int32(-1),) * places),
    )

    own.wait()
    own_seed.wait()
    for copy in moves:
        copy.wait()

    marks = []
    for k in range(per_column):
        p = source[k]
        vals[:, k] = recv[p]
        pair = seed_recv[p // slots]
        row = pair[0:1]
        for s in range(1, slots):
            row = jnp.where(p % slots == s, pair[s : s + 1], row)
        marks.append(row[None])
    marks = jnp.concatenate(marks, 0)

    shape = (per_column, rows, LANES)
    lane = lax.broadcasted_iota(jnp.int32, shape, 2)
    row_id = lax.broadcasted_iota(jnp.int32, shape, 1)
    z_cell = lane % cells
    group = lane // cells
    xglob = (row_id + (gx * cells + xh * rows)).astype(jnp.float32)

    def rolled(v, shift):
        shift = shift % LANES
        return v if shift == 0 else pltpu.roll(v, shift, 2)

    def exchange(step, old):
        low_y = jnp.zeros(shape, jnp.float32)
        high_y = low_y
        for f in range(nfield):
            v = old[f]
            xsend[step, 0, :, f : f + 1, :] = v[:, 0:1, :]
            xsend[step, 1, :, f : f + 1, :] = v[:, rows - 1 : rows, :]
            low_y = jnp.where(group == f, rolled(v, cells * f), low_y)
            high_y = jnp.where(group == f, rolled(v, cells * f + cells), high_y)
        ysend[step, 0] = low_y
        ysend[step, 1] = high_y
        for phase in ("start", "wait"):
            for side, (exists, _, device) in enumerate(sides):
                send, ghost, s_sem, r_sem = (
                    (xsend, xghost, x_send, x_recv)
                    if side < 2
                    else (ysend, yghost, y_send, y_recv)
                )
                e = side % 2

                @pl.when(exists)
                def _(send=send, ghost=ghost, s_sem=s_sem, r_sem=r_sem, e=e, device=device):
                    if phase == "start":
                        pltpu.make_async_remote_copy(
                            src_ref=send.at[step, e],
                            dst_ref=ghost.at[step, 1 - e],
                            send_sem=s_sem.at[step, e],
                            recv_sem=r_sem.at[step, 1 - e],
                            device_id=device,
                            device_id_type=MESH,
                        ).start()
                    else:
                        pltpu.make_async_remote_copy(
                            src_ref=send.at[step, e],
                            dst_ref=ghost.at[step, e],
                            send_sem=s_sem.at[step, e],
                            recv_sem=r_sem.at[step, e],
                            device_id=device,
                            device_id_type=MESH,
                        ).wait()

                if phase == "start":

                    @pl.when(jnp.logical_not(exists))
                    def _(send=send, ghost=ghost, e=e):
                        ghost[step, e] = send[step, e]

    def laplace(step, f, v):
        below_x = jnp.concatenate([xghost[step, 0, :, f : f + 1, :], v[:, :-1, :]], 1)
        above_x = jnp.concatenate([v[:, 1:, :], xghost[step, 1, :, f : f + 1, :]], 1)
        below_y = jnp.where(
            group == 0, rolled(yghost[step, 0], -cells * f), rolled(v, cells)
        )
        above_y = jnp.where(
            group == LANES // cells - 1,
            rolled(yghost[step, 1], -cells * f - cells),
            rolled(v, -cells),
        )
        before_k = jnp.concatenate([v[-1:], v[:-1]], 0)
        after_k = jnp.concatenate([v[1:], v[:1]], 0)
        below_z = jnp.where(z_cell == 0, rolled(before_k, 1 - cells), rolled(v, 1))
        above_z = jnp.where(z_cell == cells - 1, rolled(after_k, cells - 1), rolled(v, -1))
        return below_x + above_x + below_y + above_y + below_z + above_z - 6.0 * v

    for step in range(STEPS):
        src = vals if step == 0 else result.at[step - 1]
        exchange(step, [src[f] for f in range(nfield)])
        thermal = xglob / (2.0 * cells) - 1.0 - 0.25 * step
        change = []
        for k in range(NPHASE):
            phi = src[k]
            drive = gain[k] * thermal
            for j in range(nfield - NPHASE):
                drive = drive + couple[k, j] * src[NPHASE + j]
            if step == 0:
                drive = drive + SEED_GAIN * (marks == k).astype(jnp.float32)
            delta = 0.12 * laplace(step, k, phi) + phi * (1.0 - phi) * (phi - 0.5 + drive)
            new = phi + delta
            result[step, k] = new
            change.append(new - phi)
        for j in range(nfield - NPHASE):
            mu = src[NPHASE + j]
            new = mu + (0.1 * diffuse[j]) * laplace(step, NPHASE + j, mu)
            for k in range(NPHASE):
                new = new - latent[j, k] * change[k]
            result[step, NPHASE + j] = new

    for q in range(places):
        k = depth[q]
        tile = result[STEPS - 1, :, jnp.maximum(k, 0)]
        outbuf[q // slots, q % slots] = jnp.where(k >= 0, tile, 0.0)
    moves = []
    for d in range(gz_n - 1, 0, -1):
        to = (gz + d) % gz_n
        copy = pltpu.make_async_remote_copy(
            src_ref=outbuf.at[to],
            dst_ref=window(out, gz),
            send_sem=out_send.at[d - 1],
            recv_sem=out_recv.at[d - 1],
            device_id=(gx, gy, to),
            device_id_type=MESH,
        )
        copy.start()
        moves.append(copy)
    own = pltpu.make_async_copy(outbuf.at[gz], window(out, gz), local_sem.at[2])
    own.start()
    own.wait()
    for copy in moves:
        copy.wait()


def widths(nfield, tiles, cells):
    per_pack = LANES // (STEPS * cells)
    packs = -(-nfield // per_pack)
    fold = per_pack > 1 and nfield % per_pack == 0
    data = [nfield - packs if fold and t > 0 else nfield for t in range(tiles)]
    return data, [w + (packs if t < tiles - 1 else 0) for t, w in enumerate(data)]


def deep_kernel(sizes, fields, seeds, *refs):
    gx_n, gy_n, gz_n, nblk, cells, surface = sizes
    tables, (
        out,
        coords,
        before,
        after,
        couple,
        latent,
        diffuse,
        gain,
        table_sem,
        mine,
        bulk,
        seed_recv,
        vals,
        edge,
        mid,
        mid_edge,
        marks,
        edge_marks,
        xsend,
        xghost,
        xsmall,
        xgsmall,
        packed,
        unpack,
        ysend,
        yrecv,
        ynear,
        ynear_recv,
        result,
        outbuf,
        outrecv,
        local_sem,
        in_sem,
        seed_sem,
        y_sem,
        yn_sem,
        x_sem,
        xs_sem,
        out_sem,
        *recv,
    ) = refs[:7], refs[7:]
    slots, nfield = mine.shape[0], mine.shape[1]
    tiles = surface // LANES
    per_column = vals.shape[2]
    rows, halo = cells // gz_n, STEPS
    ext = rows + 2 * halo
    strip_lanes = halo * cells
    per_pack = LANES // strip_lanes
    packs = -(-nfield // per_pack)
    places = gz_n * slots
    data_width, width = widths(nfield, tiles, cells)
    gx, gy, gz = lax.axis_index("gx"), lax.axis_index("gy"), lax.axis_index("gz")
    odd_x = gx % 2
    turn = 1 - 2 * odd_x

    def tile_of(g):
        return g + odd_x * (gz_n - 1 - 2 * g)

    part = tile_of(gz)
    xpos = gx * gz_n + part
    sides_x = []
    for exists, inside, step_x in (
        (xpos > 0, part > 0, -1),
        (xpos < gx_n * gz_n - 1, part < gz_n - 1, 1),
    ):
        ins = inside.astype(jnp.int32)
        device = (gx + step_x * (1 - ins), gy, gz + step_x * turn * ins)
        sides_x.append((exists, inside, device))
    odd_y = gy % 2
    sides_y = []
    for other in (gy - 1 + 2 * odd_y, gy + 1 - 2 * odd_y):
        sides_y.append((jnp.logical_and(other >= 0, other < gy_n), other))

    barrier = pltpu.get_barrier_semaphore()
    expected = gz_n - 1
    for d in range(1, gz_n):
        pl.semaphore_signal(
            barrier, inc=1, device_id=(gx, gy, (gz + d) % gz_n), device_id_type=MESH
        )
    targets = [(exists, (gx, other, gz)) for exists, other in sides_y]
    for exists_x, _, device in sides_x:
        for exists_y, other in sides_y:
            both = jnp.logical_and(exists_x, exists_y)
            targets.append((both, (device[0], other, device[2])))
    for exists, device in targets:

        @pl.when(exists)
        def _(device=device):
            pl.semaphore_signal(barrier, inc=1, device_id=device, device_id_type=MESH)

        expected = expected + exists.astype(jnp.int32)
    for exists, inside, device in sides_x:
        outside = jnp.logical_and(exists, jnp.logical_not(inside))

        @pl.when(outside)
        def _(device=device):
            pl.semaphore_signal(barrier, inc=1, device_id=device, device_id_type=MESH)

        expected = expected + outside.astype(jnp.int32)

    load = pltpu.make_async_copy(fields, mine, local_sem.at[0])
    load.start()
    load_seed = pltpu.make_async_copy(seeds, seed_recv.at[gz], local_sem.at[1])
    load_seed.start()
    small = (coords, before, after, couple, latent, diffuse, gain)
    fetches = [
        pltpu.make_async_copy(src, dst, table_sem.at[n])
        for n, (src, dst) in enumerate(zip(tables, small))
    ]
    for fetch in fetches:
        fetch.start()

    lane = lax.broadcasted_iota(jnp.int32, (1, 1, LANES), 2)

    def rolled(v, shift):
        shift = shift % LANES
        return v if shift == 0 else pltpu.roll(v, shift, 2)

    def pack(s, n, t):
        row = None
        for j in range(min(per_pack, nfield - n * per_pack)):
            v = mine[s, pl.ds(n * per_pack + j, 1), :, pl.ds(t * LANES, LANES)]
            v = rolled(v, strip_lanes * j)
            row = v if row is None else jnp.where(lane // strip_lanes == j, v, row)
        return [row[:, q * rows : (q + 1) * rows] for q in range(gz_n)]

    def flipped(v):
        count, size = LANES // cells, 1
        while size < count:
            odd_group = lane // cells // size % 2 == 1
            v = jnp.where(odd_group, rolled(v, size * cells), rolled(v, -size * cells))
            size *= 2
        return v

    load.wait()

    @pl.when(odd_y == 1)
    def _():
        for s in range(slots):
            for t in range((tiles + 1) // 2):
                a, b = pl.ds(t * LANES, LANES), pl.ds((tiles - 1 - t) * LANES, LANES)
                low, high = flipped(mine[s, :, :, a]), flipped(mine[s, :, :, b])
                mine[s, :, :, a] = high
                mine[s, :, :, b] = low

    for s in range(slots):
        for n in range(packs):
            for t in range(tiles - 1):
                for q, row in enumerate(pack(s, n, t + 1)):
                    bulk[t, q, s, pl.ds(data_width[t] + n, 1)] = row
    folds = per_pack - 1
    for t in range(tiles):
        if data_width[t] == nfield:
            for q in range(gz_n):
                bulk[t, q, :, pl.ds(0, nfield)] = mine[
                    :, :, q * rows : (q + 1) * rows, t * LANES : (t + 1) * LANES
                ]
            continue
        for n in range(packs):
            extra = mine[:, n * per_pack + folds, :, t * LANES : (t + 1) * LANES]
            for i in range(folds):
                row = mine[:, n * per_pack + i, :, t * LANES : (t + 1) * LANES]
                row = jnp.where(lane < strip_lanes, rolled(extra, -strip_lanes * (i + 1)), row)
                for q in range(gz_n):
                    bulk[t, q, :, n * folds + i] = row[:, q * rows : (q + 1) * rows]
    pl.semaphore_wait(barrier, expected)

    for d in range(1, gz_n):
        pltpu.make_async_remote_copy(
            src_ref=seeds,
            dst_ref=seed_recv.at[gz],
            send_sem=seed_sem.at[0],
            recv_sem=seed_sem.at[1],
            device_id=(gx, gy, (gz + d) % gz_n),
            device_id_type=MESH,
        ).start()

    for t in range(tiles):
        for d in range(gz_n - 1, 0, -1):
            to = (gz + d) % gz_n
            pltpu.make_async_remote_copy(
                src_ref=bulk.at[t, tile_of(to), :, pl.ds(0, width[t])],
                dst_ref=recv[t].at[pl.ds(slots * gz, slots), pl.ds(0, width[t])],
                send_sem=in_sem.at[t],
                recv_sem=in_sem.at[tiles + t],
                device_id=(gx, gy, to),
                device_id_type=MESH,
            ).start()
    for t in range(tiles):
        recv[t][pl.ds(slots * gz, slots), pl.ds(0, width[t])] = bulk[t, part, :, pl.ds(0, width[t])]
    for fetch in fetches:
        fetch.wait()

    base = (gx * gy_n + gy) * places

    def lookup(b, carry):
        source, depth = carry
        here = jnp.logical_and(coords[0, b] == gx, coords[1, b] == gy)
        z = jnp.where(here, coords[2, b], -1)
        was = before[b] - base
        now = jnp.where(here, after[b] - base, -1)
        source = tuple(jnp.where(z == k, was, source[k]) for k in range(per_column))
        depth = tuple(jnp.where(now == p, z, depth[p]) for p in range(places))
        return source, depth

    source, depth = lax.fori_loop(
        0,
        nblk,
        lookup,
        ((jnp.int32(0),) * per_column, (jnp.int32(-1),) * places),
    )

    def drain(ref, sem):
        pltpu.make_async_copy(ref, ref, sem).wait()

    def seed_row(ref, p):
        pair = ref[p // slots]
        row = pair[0:1]
        for s in range(1, slots):
            row = jnp.where(p % slots == s, pair[s : s + 1], row)
        return row.astype(jnp.float32)

    load_seed.wait()
    drain(seed_recv.at[pl.ds(0, gz_n - 1)], seed_sem.at[1])
    for k in range(per_column):
        row = seed_row(seed_recv, source[k])[None]
        cut = [row[:, :, t * LANES : (t + 1) * LANES] for t in range(tiles)]
        for t in range(tiles):
            piece = jnp.where(odd_y == 1, flipped(cut[tiles - 1 - t]), cut[t])[0]
            wide = jnp.broadcast_to(piece, (ext, LANES))
            marks[t, k] = wide
            if t > 0:
                edge_marks[t, k] = wide
            for x in range(2):
                xsmall[t, x, k, pl.ds(packs, 1)] = piece
                if t == tiles - 1:
                    xsmall[t, x, k, pl.ds(0, packs)] = jnp.zeros((packs, LANES), jnp.float32)

    def unfold(block, strips):
        fields_of = []
        for n in range(packs):
            strip_n = strips[n : n + 1]
            extra = rolled(strip_n, -strip_lanes * folds)
            for i in range(folds):
                row = block[n * folds + i : n * folds + i + 1]
                fields_of.append(
                    jnp.where(lane < strip_lanes, rolled(strip_n, -strip_lanes * i), row)
                )
                extra = jnp.where(
                    lane // strip_lanes == i + 1, rolled(row, strip_lanes * (i + 1)), extra
                )
            fields_of.append(extra)
        return fields_of

    near = (halo - 1, halo + rows)
    first = (0, halo + rows)
    shape = (per_column, ext, LANES)
    lane3 = lax.broadcasted_iota(jnp.int32, shape, 2)
    z_cell = lane3 % cells
    group = lane3 // cells
    last_group = LANES // cells - 1
    row_id = lax.broadcasted_iota(jnp.int32, shape, 1)
    far = lane3 >= LANES // 2

    def mirror(v, e):
        ring = None
        for h in range(halo):
            shift = (2 * h + 1) * cells
            w = rolled(v, shift if e else -shift)
            spot = h if e else last_group - h
            ring = w if ring is None else jnp.where(lane // cells == spot, w, ring)
        return ring

    def outer(t):
        return [e for e, spot in ((0, 0), (1, tiles - 1)) if t == spot]

    def send_strips(t, e, other):
        for n in range(packs):
            row = None
            for j in range(min(per_pack, nfield - n * per_pack)):
                v = mirror(vals[n * per_pack + j, t, :, halo : halo + rows, :], e)
                v = rolled(v, strip_lanes * (j if e else j + 1))
                row = v if row is None else jnp.where(lane // strip_lanes == j, v, row)
            ysend[e, :, n] = row
            for x, r in ((0, 0), (1, rows - 1)):
                ynear[e, x, :, pl.ds(n, 1), :] = row[:, r : r + 1]
        ysend[e, :, packs] = mirror(marks[t], e)[:, halo : halo + rows]
        pltpu.make_async_remote_copy(
            src_ref=ysend.at[e],
            dst_ref=yrecv.at[e],
            send_sem=y_sem.at[e],
            recv_sem=y_sem.at[2 + e],
            device_id=(gx, other, gz),
            device_id_type=MESH,
        ).start()
        for x, (exists, _, device) in enumerate(sides_x):

            @pl.when(exists)
            def _(x=x, device=device):
                pltpu.make_async_remote_copy(
                    src_ref=ynear.at[e, x],
                    dst_ref=ynear_recv.at[e, 1 - x],
                    send_sem=yn_sem.at[e, x],
                    recv_sem=yn_sem.at[e, 2 + 1 - x],
                    device_id=(device[0], other, device[2]),
                    device_id_type=MESH,
                ).start()

    def take_strips(e):
        drain(yrecv.at[e], y_sem.at[2 + e])
        for x, (exists, _, _) in enumerate(sides_x):

            @pl.when(exists)
            def _(x=x):
                drain(ynear_recv.at[e, x], yn_sem.at[e, 2 + x])

            @pl.when(jnp.logical_not(exists))
            def _(x=x):
                r = (rows - 1) * x
                for n in range(packs):
                    ynear_recv[e, x, :, pl.ds(n, 1), :] = yrecv[e, :, n, r : r + 1, :]

    for t in range(tiles):
        drain(recv[t].at[pl.ds(0, (gz_n - 1) * slots), pl.ds(0, width[t])], in_sem.at[tiles + t])
        for k in range(per_column):
            block = recv[t][source[k]]
            if data_width[t] == nfield:
                full = block[:nfield]
                xsend[t, 0, k] = full[:, :halo]
                xsend[t, 1, k] = full[:, rows - halo :]
                vals[:, t, k, halo : halo + rows, :] = full
            else:
                for f, v in enumerate(unfold(block, packed[t - 1, k])):
                    xsend[t, 0, k, pl.ds(f, 1)] = v[:, :halo]
                    xsend[t, 1, k, pl.ds(f, 1)] = v[:, rows - halo :]
                    vals[pl.ds(f, 1), t, k, halo : halo + rows, :] = v
            if t < tiles - 1:
                piece = block[data_width[t] :]
                packed[t, k] = piece
                for x, r in ((0, 0), (1, rows - 1)):
                    for n in range(packs):
                        xsmall[t, x, k, pl.ds(n, 1)] = piece[n, r : r + 1]

        for e in outer(t):
            exists, other = sides_y[e]

            @pl.when(exists)
            def _(t=t, e=e, other=other):
                send_strips(t, e, other)

        for e, (exists, _, device) in enumerate(sides_x):

            @pl.when(exists)
            def _(t=t, e=e, device=device):
                for src, dst, sem in ((xsend, xghost, x_sem), (xsmall, xgsmall, xs_sem)):
                    pltpu.make_async_remote_copy(
                        src_ref=src.at[t, e],
                        dst_ref=dst.at[t, 1 - e],
                        send_sem=sem.at[t, e],
                        recv_sem=sem.at[t, 2 + 1 - e],
                        device_id=device,
                        device_id_type=MESH,
                    ).start()

            @pl.when(jnp.logical_not(exists))
            def _(t=t, e=e):
                for h in range(halo):
                    xghost[t, e, :, :, h : h + 1, :] = xsend[t, e, :, :, halo - 1 - h : halo - h, :]
                xgsmall[t, e] = xsmall[t, e]

    def spread(t, e, inner):
        for n in range(packs):
            unpack[:, halo : halo + rows, :] = packed[t, :, n] if inner else yrecv[e, :, n]
            for x in range(2):
                row = xgsmall[t, x, :, pl.ds(n, 1), :] if inner else ynear_recv[e, x, :, pl.ds(n, 1), :]
                unpack[:, near[x] : near[x] + 1, :] = row
            whole = unpack[...]
            for j in range(min(per_pack, nfield - n * per_pack)):
                shift = -strip_lanes * j if e else -strip_lanes * (j + 1)
                edge[e and 1 + t, n * per_pack + j] = rolled(whole, shift)

    def shift_rows(v, by):
        if ext % 8 == 0:
            return pltpu.roll(v, by % ext, 1)
        cut = by % ext
        return jnp.concatenate([v[:, ext - cut :], v[:, : ext - cut]], 1)

    def around(v, below, above):
        below_y = jnp.where(group == 0, below, rolled(v, cells))
        above_y = jnp.where(group == last_group, above, rolled(v, -cells))
        before_k = jnp.concatenate([v[-1:], v[:-1]], 0)
        after_k = jnp.concatenate([v[1:], v[:1]], 0)
        below_z = jnp.where(z_cell == 0, rolled(before_k, 1 - cells), rolled(v, 1))
        above_z = jnp.where(z_cell == cells - 1, rolled(after_k, cells - 1), rolled(v, -1))
        total = shift_rows(v, 1) + shift_rows(v, -1) + below_y + above_y + below_z + above_z
        return total - 6.0 * v

    x_cell = row_id + (gx * cells + part * rows - halo)
    x_cell = jnp.where(x_cell < 0, -1 - x_cell, x_cell)
    x_end = gx_n * cells
    x_cell = jnp.where(x_cell > x_end - 1, 2 * x_end - 1 - x_cell, x_cell)
    xglob = x_cell.astype(jnp.float32)
    unpack[...] = jnp.zeros_like(unpack)

    for t in range(tiles):
        for e, (exists, _, device) in enumerate(sides_x):

            @pl.when(exists)
            def _(t=t, e=e):
                drain(xghost.at[t, e], x_sem.at[t, 2 + e])
                drain(xgsmall.at[t, e], xs_sem.at[t, 2 + e])

        for k in range(per_column):
            for e in range(2):
                vals[:, t, k, first[e] : first[e] + halo, :] = xghost[t, e, k]
                marks[t, k, near[e] : near[e] + 1, :] = xgsmall[t, e, k, pl.ds(packs, 1)]
        for e, (exists, _) in enumerate(sides_y):
            if e == 0 and t > 0:
                continue
            if e == 1 and t < tiles - 1:
                spread(t, e, True)
                continue

            @pl.when(exists)
            def _(t=t, e=e):
                take_strips(e)
                spread(t, e, False)
                for k in range(per_column):
                    edge_marks[e and 1 + t, k] = jnp.broadcast_to(
                        yrecv[e, k, packs, 0:1, :], (ext, LANES)
                    )

            @pl.when(jnp.logical_not(exists))
            def _(t=t, e=e):
                for f in range(nfield):
                    edge[e and 1 + t, f] = mirror(vals[f, t], e)
                edge_marks[e and 1 + t] = mirror(marks[t], e)

        def collect(t, at, count):
            for p in range(places):
                k = depth[p]
                tile = result[t, jnp.maximum(k, 0), pl.ds(at, count)]
                outbuf[t, p // slots, p % slots, pl.ds(at, count)] = jnp.where(k >= 0, tile, 0.0)

        def send_back(t, at, count, order):
            for n in order:
                to = jnp.where(n < gz, n, gz_n - 1 - n + gz)
                pltpu.make_async_remote_copy(
                    src_ref=outbuf.at[t, to, :, pl.ds(at, count)],
                    dst_ref=outrecv.at[t, part, :, pl.ds(at, count)],
                    send_sem=out_sem.at[t],
                    recv_sem=out_sem.at[tiles + t],
                    device_id=(gx, gy, to),
                    device_id_type=MESH,
                ).start()

        def join(low, high):
            return jnp.where(far, low, high) if t == 0 else high

        for step in range(STEPS):
            last = step == STEPS - 1
            if step == 0:
                body = [vals[f, t] for f in range(nfield)]
                rim = [join(edge[0, f], edge[1 + t, f]) for f in range(nfield)]
                seed = (marks[t], join(edge_marks[0], edge_marks[1 + t]))
            else:
                body = [mid[f, t] for f in range(nfield)]
                rim = [mid_edge[f] for f in range(nfield)]

            def laplace(f):
                v, w = body[f], rim[f]
                prior = w if t == 0 else (vals[f, t - 1] if step == 0 else mid[f, t - 1])
                sums = [around(v, rolled(prior, cells), rolled(w, -cells))]
                if not last:
                    sums.append(around(w, rolled(v, cells), rolled(v, -cells)))
                return sums

            def keep(f, i, new):
                if last:
                    result[t, :, f] = new[:, halo : halo + rows]
                elif i == 0:
                    mid[f, t] = new
                else:
                    mid_edge[f] = new

            thermal = xglob / (2.0 * cells) - 1.0 - 0.25 * step
            change = []
            for k in range(NPHASE):
                moved = []
                for i, lap in enumerate(laplace(k)):
                    have = (body, rim)[i]
                    phi = have[k]
                    drive = gain[k] * thermal
                    for j in range(nfield - NPHASE):
                        drive = drive + couple[k, j] * have[NPHASE + j]
                    if step == 0:
                        drive = drive + jnp.where(seed[i] == float(k), SEED_GAIN, 0.0)
                    delta = 0.12 * lap + phi * (1.0 - phi) * (phi - 0.5 + drive)
                    moved.append(delta)
                    keep(k, i, phi + delta)
                change.append(moved)
            if last:
                collect(t, 0, NPHASE)
                send_back(t, 0, NPHASE, range(gz_n - 1) if t < tiles - 1 else [0])
            for j in range(nfield - NPHASE):
                for i, lap in enumerate(laplace(NPHASE + j)):
                    new = (body, rim)[i][NPHASE + j] + (0.1 * diffuse[j]) * lap
                    for k in range(NPHASE):
                        new = new - latent[j, k] * change[k][i]
                    keep(NPHASE + j, i, new)

        collect(t, NPHASE, nfield - NPHASE)
        early = range(gz_n - 1) if t < tiles - 1 else [0]
        send_back(t, NPHASE, nfield - NPHASE, early)
        send_back(t, 0, nfield, [n for n in range(gz_n - 1) if n not in early])
        outrecv[t, part] = outbuf[t, gz]

    for e, (exists, _) in enumerate(sides_y):

        @pl.when(exists)
        def _(e=e):
            drain(ysend.at[e], y_sem.at[e])
            for x, (exists_x, _, _) in enumerate(sides_x):

                @pl.when(exists_x)
                def _(x=x):
                    drain(ynear.at[e, x], yn_sem.at[e, x])

    drain(seed_recv.at[pl.ds(0, gz_n - 1)], seed_sem.at[0])
    for t in range(tiles):
        drain(recv[t].at[pl.ds(0, (gz_n - 1) * slots), pl.ds(0, width[t])], in_sem.at[t])
        for e, (exists, _, device) in enumerate(sides_x):

            @pl.when(exists)
            def _(t=t, e=e):
                drain(xsend.at[t, e], x_sem.at[t, e])
                drain(xsmall.at[t, e], xs_sem.at[t, e])

    for t in range(tiles):
        drain(outrecv.at[t, pl.ds(0, gz_n - 1)], out_sem.at[tiles + t])

        @pl.when(odd_y == 0)
        def _(t=t):
            for q in range(gz_n):
                out[:, :, q * rows : (q + 1) * rows, t * LANES : (t + 1) * LANES] = outrecv[t, q]

        @pl.when(odd_y == 1)
        def _(t=t):
            lanes = pl.ds((tiles - 1 - t) * LANES, LANES)
            for q in range(gz_n):
                for s in range(slots):
                    out[s, :, q * rows : (q + 1) * rows, lanes] = flipped(outrecv[t, q, s])

    for t in range(tiles):
        drain(outbuf.at[t, pl.ds(0, gz_n - 1)], out_sem.at[t])


def solution(mesh):
    gx_n, gy_n, gz_n = mesh.shape["gx"], mesh.shape["gy"], mesh.shape["gz"]

    def deep(fields, seeds, *tables):
        slots, nfield, cells, surface = fields.shape
        tables = (tables[0].T,) + tables[1:]
        nblk = tables[0].shape[1]
        column = nblk // (gx_n * gy_n)
        tiles = surface // LANES
        rows = cells // gz_n
        ext = rows + 2 * STEPS
        packs = -(-nfield // (LANES // (STEPS * cells)))
        places = gz_n * slots
        f32, i32 = jnp.float32, jnp.int32
        dma = pltpu.SemaphoreType.DMA
        anyspace = pl.BlockSpec(memory_space=pl.ANY)
        block = (column, ext, LANES)
        faces = (tiles, 2, column, nfield, STEPS, LANES)
        thin = (tiles, 2, column, packs + 1, LANES)
        return pl.pallas_call(
            functools.partial(deep_kernel, (gx_n, gy_n, gz_n, nblk, cells, surface)),
            out_shape=pltpu.VMEM(fields.shape, f32),
            in_specs=[anyspace] * 9,
            out_specs=pl.BlockSpec(memory_space=pltpu.VMEM),
            scratch_shapes=[pltpu.SMEM(a.shape, a.dtype) for a in tables]
            + [
                dma((len(tables),)),
                pltpu.VMEM(fields.shape, f32),
                pltpu.VMEM((tiles, gz_n, slots, nfield + packs, rows, LANES), f32),
                pltpu.VMEM((gz_n, slots, surface), i32),
                pltpu.VMEM((nfield, tiles) + block, f32),
                pltpu.VMEM((tiles + 1, nfield) + block, f32),
                pltpu.VMEM((nfield, tiles) + block, f32),
                pltpu.VMEM((nfield,) + block, f32),
                pltpu.VMEM((tiles,) + block, f32),
                pltpu.VMEM((tiles + 1,) + block, f32),
                pltpu.VMEM(faces, f32),
                pltpu.VMEM(faces, f32),
                pltpu.VMEM(thin, f32),
                pltpu.VMEM(thin, f32),
                pltpu.VMEM((max(tiles - 1, 1), column, packs, rows, LANES), f32),
                pltpu.VMEM(block, f32),
                pltpu.VMEM((2, column, packs + 1, rows, LANES), f32),
                pltpu.VMEM((2, column, packs + 1, rows, LANES), f32),
                pltpu.VMEM((2, 2, column, packs, LANES), f32),
                pltpu.VMEM((2, 2, column, packs, LANES), f32),
                pltpu.VMEM((tiles, column, nfield, rows, LANES), f32),
                pltpu.VMEM((tiles, gz_n, slots, nfield, rows, LANES), f32),
                pltpu.VMEM((tiles, gz_n, slots, nfield, rows, LANES), f32),
                dma((2,)),
                dma((2 * tiles,)),
                dma((2,)),
                dma((4,)),
                dma((2, 4)),
                dma((tiles, 4)),
                dma((tiles, 4)),
                dma((2 * tiles,)),
            ]
            + [pltpu.VMEM((places, w, rows, LANES), f32) for w in widths(nfield, tiles, cells)[1]],
            compiler_params=pltpu.CompilerParams(collective_id=0, has_side_effects=True),
        )(fields, seeds, *tables)

    def per_device(fields, seeds, coords, neighbours, before, after, couple, latent, diffuse, gain):
        slots, nfield, cells, surface = fields.shape
        nblk = coords.shape[0]
        per_column = nblk // (gx_n * gy_n)
        halves = surface // LANES
        rows = cells * halves // gz_n
        f32, i32 = jnp.float32, jnp.int32
        dma = pltpu.SemaphoreType.DMA
        smem = pl.BlockSpec(memory_space=pltpu.SMEM)
        anyspace = pl.BlockSpec(memory_space=pl.ANY)
        if cells % gz_n == 0 and cells // gz_n >= STEPS and 2 * STEPS * cells <= LANES:
            return deep(fields, seeds, coords, before, after, couple, latent, diffuse, gain)
        faces_x = (STEPS, 2, per_column, nfield, LANES)
        faces_y = (STEPS, 2, per_column, rows, LANES)
        return pl.pallas_call(
            functools.partial(tile_kernel, (gx_n, gy_n, gz_n, nblk, cells, surface)),
            out_shape=pltpu.VMEM(fields.shape, f32),
            in_specs=[anyspace, anyspace] + [smem] * 7,
            out_specs=pl.BlockSpec(memory_space=pltpu.VMEM),
            scratch_shapes=[
                pltpu.VMEM((gz_n * slots, nfield, rows, LANES), f32),
                pltpu.VMEM((gz_n, slots, LANES), i32),
                pltpu.VMEM((nfield, per_column, rows, LANES), f32),
                pltpu.VMEM(faces_x, f32),
                pltpu.VMEM(faces_x, f32),
                pltpu.VMEM(faces_y, f32),
                pltpu.VMEM(faces_y, f32),
                pltpu.VMEM((STEPS, nfield, per_column, rows, LANES), f32),
                pltpu.VMEM((gz_n, slots, nfield, rows, LANES), f32),
                dma((gz_n,)),
                dma((gz_n,)),
                dma((gz_n,)),
                dma((gz_n,)),
                dma((STEPS, 2)),
                dma((STEPS, 2)),
                dma((STEPS, 2)),
                dma((STEPS, 2)),
                dma((gz_n,)),
                dma((gz_n,)),
                dma((3,)),
            ],
            compiler_params=pltpu.CompilerParams(collective_id=0, has_side_effects=True),
        )(fields, seeds, coords.T, before, after, couple, latent, diffuse, gain)

    placed = (
        P(("gx", "gy", "gz"), None, None, None),
        P(("gx", "gy", "gz"), None),
    ) + (P(),) * 8
    return jax.shard_map(
        per_device,
        mesh=mesh,
        in_specs=placed,
        out_specs=P(("gx", "gy", "gz"), None, None, None),
        check_vma=False,
    )
```

```python
import functools

import jax
import jax.numpy as jnp
from jax import lax
from jax.experimental import pallas as pl
from jax.experimental.pallas import tpu as pltpu
from jax.sharding import PartitionSpec as P

NPHASE = 4
STEPS = 2
LANES = 128
SEED_GAIN = 2.0
MESH = pl.DeviceIdType.MESH


def tile_kernel(
    sizes,
    fields,
    seeds,
    coords,
    before,
    after,
    couple,
    latent,
    diffuse,
    gain,
    out,
    recv,
    seed_recv,
    vals,
    xsend,
    xghost,
    ysend,
    yghost,
    result,
    outbuf,
    in_send,
    in_recv,
    seed_send,
    seed_got,
    x_send,
    x_recv,
    y_send,
    y_recv,
    out_send,
    out_recv,
    local_sem,
):
    gx_n, gy_n, gz_n, nblk, cells, surface = sizes
    slots, nfield = outbuf.shape[1], outbuf.shape[2]
    rows = outbuf.shape[3]
    halves = surface // LANES
    per_column = vals.shape[1]
    x_parts = gz_n // halves
    gx, gy, gz = lax.axis_index("gx"), lax.axis_index("gy"), lax.axis_index("gz")
    odd_x, odd_y = gx % 2, gy % 2

    def part_of(g):
        a, b = g // halves, g % halves
        xh = a + odd_x * (x_parts - 1 - 2 * a)
        yh = b + odd_y * (halves - 1 - 2 * b)
        return xh, yh

    def window(ref, g):
        xh, yh = part_of(g)
        x0 = pl.multiple_of(xh * rows, rows)
        y0 = pl.multiple_of(yh * LANES, LANES)
        return ref.at[:, :, pl.ds(x0, rows), pl.ds(y0, LANES)]

    def seed_window(g):
        _, yh = part_of(g)
        return seeds.at[:, pl.ds(pl.multiple_of(yh * LANES, LANES), LANES)]

    xh, yh = part_of(gz)
    xpos = gx * x_parts + xh
    ypos = gy * halves + yh
    x_total, y_total = gx_n * x_parts, gy_n * halves
    dir_x = 1 - 2 * odd_x
    dir_y = 1 - 2 * odd_y
    xlo_in, xhi_in = xh > 0, xh < x_parts - 1
    ylo_in, yhi_in = yh > 0, yh < halves - 1
    sides = []
    for exists, inside, step_x, step_y, move in (
        (xpos > 0, xlo_in, -1, 0, -halves * dir_x),
        (xpos < x_total - 1, xhi_in, 1, 0, halves * dir_x),
        (ypos > 0, ylo_in, 0, -1, -dir_y),
        (ypos < y_total - 1, yhi_in, 0, 1, dir_y),
    ):
        ins = inside.astype(jnp.int32)
        device = (gx + step_x * (1 - ins), gy + step_y * (1 - ins), gz + move * ins)
        sides.append((exists, inside, device))

    barrier = pltpu.get_barrier_semaphore()
    for d in range(1, gz_n):
        pl.semaphore_signal(
            barrier, inc=1, device_id=(gx, gy, (gz + d) % gz_n), device_id_type=MESH
        )
    expected = gz_n - 1
    for exists, inside, device in sides:
        outside = jnp.logical_and(exists, jnp.logical_not(inside))

        @pl.when(outside)
        def _(device=device):
            pl.semaphore_signal(barrier, inc=1, device_id=device, device_id_type=MESH)

        expected = expected + outside.astype(jnp.int32)
    pl.semaphore_wait(barrier, expected)

    moves = []
    for d in range(gz_n - 1, 0, -1):
        to = (gz + d) % gz_n
        for src, dst, s_sem, r_sem in (
            (window(fields, to), recv.at[pl.ds(slots * gz, slots)], in_send, in_recv),
            (seed_window(to), seed_recv.at[gz], seed_send, seed_got),
        ):
            copy = pltpu.make_async_remote_copy(
                src_ref=src,
                dst_ref=dst,
                send_sem=s_sem.at[d - 1],
                recv_sem=r_sem.at[d - 1],
                device_id=(gx, gy, to),
                device_id_type=MESH,
            )
            copy.start()
            moves.append(copy)
    own = pltpu.make_async_copy(
        window(fields, gz), recv.at[pl.ds(slots * gz, slots)], local_sem.at[0]
    )
    own.start()
    own_seed = pltpu.make_async_copy(seed_window(gz), seed_recv.at[gz], local_sem.at[1])
    own_seed.start()

    base = (gx * gy_n + gy) * (gz_n * slots)
    places = gz_n * slots

    def lookup(b, carry):
        source, depth = carry
        here = jnp.logical_and(coords[0, b] == gx, coords[1, b] == gy)
        z = jnp.where(here, coords[2, b], -1)
        was = before[b] - base
        now = jnp.where(here, after[b] - base, -1)
        source = tuple(jnp.where(z == k, was, source[k]) for k in range(per_column))
        depth = tuple(jnp.where(now == q, z, depth[q]) for q in range(places))
        return source, depth

    source, depth = lax.fori_loop(
        0,
        nblk,
        lookup,
        ((jnp.int32(0),) * per_column, (jnp.int32(-1),) * places),
    )

    own.wait()
    own_seed.wait()
    for copy in moves:
        copy.wait()

    marks = []
    for k in range(per_column):
        p = source[k]
        vals[:, k] = recv[p]
        pair = seed_recv[p // slots]
        row = pair[0:1]
        for s in range(1, slots):
            row = jnp.where(p % slots == s, pair[s : s + 1], row)
        marks.append(row[None])
    marks = jnp.concatenate(marks, 0)

    shape = (per_column, rows, LANES)
    lane = lax.broadcasted_iota(jnp.int32, shape, 2)
    row_id = lax.broadcasted_iota(jnp.int32, shape, 1)
    z_cell = lane % cells
    group = lane // cells
    xglob = (row_id + (gx * cells + xh * rows)).astype(jnp.float32)

    def rolled(v, shift):
        shift = shift % LANES
        return v if shift == 0 else pltpu.roll(v, shift, 2)

    def exchange(step, old):
        low_y = jnp.zeros(shape, jnp.float32)
        high_y = low_y
        for f in range(nfield):
            v = old[f]
            xsend[step, 0, :, f : f + 1, :] = v[:, 0:1, :]
            xsend[step, 1, :, f : f + 1, :] = v[:, rows - 1 : rows, :]
            low_y = jnp.where(group == f, rolled(v, cells * f), low_y)
            high_y = jnp.where(group == f, rolled(v, cells * f + cells), high_y)
        ysend[step, 0] = low_y
        ysend[step, 1] = high_y
        for phase in ("start", "wait"):
            for side, (exists, _, device) in enumerate(sides):
                send, ghost, s_sem, r_sem = (
                    (xsend, xghost, x_send, x_recv)
                    if side < 2
                    else (ysend, yghost, y_send, y_recv)
                )
                e = side % 2

                @pl.when(exists)
                def _(send=send, ghost=ghost, s_sem=s_sem, r_sem=r_sem, e=e, device=device):
                    if phase == "start":
                        pltpu.make_async_remote_copy(
                            src_ref=send.at[step, e],
                            dst_ref=ghost.at[step, 1 - e],
                            send_sem=s_sem.at[step, e],
                            recv_sem=r_sem.at[step, 1 - e],
                            device_id=device,
                            device_id_type=MESH,
                        ).start()
                    else:
                        pltpu.make_async_remote_copy(
                            src_ref=send.at[step, e],
                            dst_ref=ghost.at[step, e],
                            send_sem=s_sem.at[step, e],
                            recv_sem=r_sem.at[step, e],
                            device_id=device,
                            device_id_type=MESH,
                        ).wait()

                if phase == "start":

                    @pl.when(jnp.logical_not(exists))
                    def _(send=send, ghost=ghost, e=e):
                        ghost[step, e] = send[step, e]

    def laplace(step, f, v):
        below_x = jnp.concatenate([xghost[step, 0, :, f : f + 1, :], v[:, :-1, :]], 1)
        above_x = jnp.concatenate([v[:, 1:, :], xghost[step, 1, :, f : f + 1, :]], 1)
        below_y = jnp.where(
            group == 0, rolled(yghost[step, 0], -cells * f), rolled(v, cells)
        )
        above_y = jnp.where(
            group == LANES // cells - 1,
            rolled(yghost[step, 1], -cells * f - cells),
            rolled(v, -cells),
        )
        before_k = jnp.concatenate([v[-1:], v[:-1]], 0)
        after_k = jnp.concatenate([v[1:], v[:1]], 0)
        below_z = jnp.where(z_cell == 0, rolled(before_k, 1 - cells), rolled(v, 1))
        above_z = jnp.where(z_cell == cells - 1, rolled(after_k, cells - 1), rolled(v, -1))
        return below_x + above_x + below_y + above_y + below_z + above_z - 6.0 * v

    for step in range(STEPS):
        src = vals if step == 0 else result.at[step - 1]
        exchange(step, [src[f] for f in range(nfield)])
        thermal = xglob / (2.0 * cells) - 1.0 - 0.25 * step
        change = []
        for k in range(NPHASE):
            phi = src[k]
            drive = gain[k] * thermal
            for j in range(nfield - NPHASE):
                drive = drive + couple[k, j] * src[NPHASE + j]
            if step == 0:
                drive = drive + SEED_GAIN * (marks == k).astype(jnp.float32)
            delta = 0.12 * laplace(step, k, phi) + phi * (1.0 - phi) * (phi - 0.5 + drive)
            new = phi + delta
            result[step, k] = new
            change.append(new - phi)
        for j in range(nfield - NPHASE):
            mu = src[NPHASE + j]
            new = mu + (0.1 * diffuse[j]) * laplace(step, NPHASE + j, mu)
            for k in range(NPHASE):
                new = new - latent[j, k] * change[k]
            result[step, NPHASE + j] = new

    for q in range(places):
        k = depth[q]
        tile = result[STEPS - 1, :, jnp.maximum(k, 0)]
        outbuf[q // slots, q % slots] = jnp.where(k >= 0, tile, 0.0)
    moves = []
    for d in range(gz_n - 1, 0, -1):
        to = (gz + d) % gz_n
        copy = pltpu.make_async_remote_copy(
            src_ref=outbuf.at[to],
            dst_ref=window(out, gz),
            send_sem=out_send.at[d - 1],
            recv_sem=out_recv.at[d - 1],
            device_id=(gx, gy, to),
            device_id_type=MESH,
        )
        copy.start()
        moves.append(copy)
    own = pltpu.make_async_copy(outbuf.at[gz], window(out, gz), local_sem.at[2])
    own.start()
    own.wait()
    for copy in moves:
        copy.wait()


def widths(nfield, tiles, cells):
    per_pack = LANES // (STEPS * cells)
    packs = -(-nfield // per_pack)
    fold = per_pack > 1 and nfield % per_pack == 0
    data = [nfield - packs if fold and t > 0 else nfield for t in range(tiles)]
    return data, [w + (packs if t < tiles - 1 else 0) for t, w in enumerate(data)]


def deep_kernel(sizes, fields, seeds, *refs):
    gx_n, gy_n, gz_n, nblk, cells, surface = sizes
    tables, (
        out,
        coords,
        before,
        after,
        couple,
        latent,
        diffuse,
        gain,
        table_sem,
        mine,
        bulk,
        seed_recv,
        vals,
        edge,
        mid,
        mid_edge,
        marks,
        edge_marks,
        xsend,
        xghost,
        xsmall,
        xgsmall,
        packed,
        unpack,
        ysend,
        yrecv,
        ynear,
        ynear_recv,
        result,
        outbuf,
        outrecv,
        local_sem,
        in_sem,
        seed_sem,
        y_sem,
        yn_sem,
        x_sem,
        xs_sem,
        out_sem,
        *recv,
    ) = refs[:7], refs[7:]
    slots, nfield = mine.shape[0], mine.shape[1]
    tiles = surface // LANES
    per_column = vals.shape[2]
    rows, halo = cells // gz_n, STEPS
    ext = rows + 2 * halo
    strip_lanes = halo * cells
    per_pack = LANES // strip_lanes
    packs = -(-nfield // per_pack)
    places = gz_n * slots
    data_width, width = widths(nfield, tiles, cells)
    gx, gy, gz = lax.axis_index("gx"), lax.axis_index("gy"), lax.axis_index("gz")
    odd_x = gx % 2
    turn = 1 - 2 * odd_x

    def tile_of(g):
        return g + odd_x * (gz_n - 1 - 2 * g)

    part = tile_of(gz)
    xpos = gx * gz_n + part
    sides_x = []
    for exists, inside, step_x in (
        (xpos > 0, part > 0, -1),
        (xpos < gx_n * gz_n - 1, part < gz_n - 1, 1),
    ):
        ins = inside.astype(jnp.int32)
        device = (gx + step_x * (1 - ins), gy, gz + step_x * turn * ins)
        sides_x.append((exists, inside, device))
    odd_y = gy % 2
    sides_y = []
    for other in (gy - 1 + 2 * odd_y, gy + 1 - 2 * odd_y):
        sides_y.append((jnp.logical_and(other >= 0, other < gy_n), other))

    barrier = pltpu.get_barrier_semaphore()
    expected = gz_n - 1
    for d in range(1, gz_n):
        pl.semaphore_signal(
            barrier, inc=1, device_id=(gx, gy, (gz + d) % gz_n), device_id_type=MESH
        )
    targets = [(exists, (gx, other, gz)) for exists, other in sides_y]
    for exists_x, _, device in sides_x:
        for exists_y, other in sides_y:
            both = jnp.logical_and(exists_x, exists_y)
            targets.append((both, (device[0], other, device[2])))
    for exists, device in targets:

        @pl.when(exists)
        def _(device=device):
            pl.semaphore_signal(barrier, inc=1, device_id=device, device_id_type=MESH)

        expected = expected + exists.astype(jnp.int32)
    for exists, inside, device in sides_x:
        outside = jnp.logical_and(exists, jnp.logical_not(inside))

        @pl.when(outside)
        def _(device=device):
            pl.semaphore_signal(barrier, inc=1, device_id=device, device_id_type=MESH)

        expected = expected + outside.astype(jnp.int32)

    load = pltpu.make_async_copy(fields, mine, local_sem.at[0])
    load.start()
    load_seed = pltpu.make_async_copy(seeds, seed_recv.at[gz], local_sem.at[1])
    load_seed.start()
    small = (coords, before, after, couple, latent, diffuse, gain)
    fetches = [
        pltpu.make_async_copy(src, dst, table_sem.at[n])
        for n, (src, dst) in enumerate(zip(tables, small))
    ]
    for fetch in fetches:
        fetch.start()

    lane = lax.broadcasted_iota(jnp.int32, (1, 1, LANES), 2)

    def rolled(v, shift):
        shift = shift % LANES
        return v if shift == 0 else pltpu.roll(v, shift, 2)

    def pack(s, n, t):
        row = None
        for j in range(min(per_pack, nfield - n * per_pack)):
            v = mine[s, pl.ds(n * per_pack + j, 1), :, pl.ds(t * LANES, LANES)]
            v = rolled(v, strip_lanes * j)
            row = v if row is None else jnp.where(lane // strip_lanes == j, v, row)
        return [row[:, q * rows : (q + 1) * rows] for q in range(gz_n)]

    def flipped(v):
        count, size = LANES // cells, 1
        while size < count:
            odd_group = lane // cells // size % 2 == 1
            v = jnp.where(odd_group, rolled(v, size * cells), rolled(v, -size * cells))
            size *= 2
        return v

    load.wait()

    @pl.when(odd_y == 1)
    def _():
        for s in range(slots):
            for t in range((tiles + 1) // 2):
                a, b = pl.ds(t * LANES, LANES), pl.ds((tiles - 1 - t) * LANES, LANES)
                low, high = flipped(mine[s, :, :, a]), flipped(mine[s, :, :, b])
                mine[s, :, :, a] = high
                mine[s, :, :, b] = low

    for s in range(slots):
        for n in range(packs):
            for t in range(tiles - 1):
                for q, row in enumerate(pack(s, n, t + 1)):
                    bulk[t, q, s, pl.ds(data_width[t] + n, 1)] = row
    folds = per_pack - 1
    for t in range(tiles):
        if data_width[t] == nfield:
            for q in range(gz_n):
                bulk[t, q, :, pl.ds(0, nfield)] = mine[
                    :, :, q * rows : (q + 1) * rows, t * LANES : (t + 1) * LANES
                ]
            continue
        for n in range(packs):
            extra = mine[:, n * per_pack + folds, :, t * LANES : (t + 1) * LANES]
            for i in range(folds):
                row = mine[:, n * per_pack + i, :, t * LANES : (t + 1) * LANES]
                row = jnp.where(lane < strip_lanes, rolled(extra, -strip_lanes * (i + 1)), row)
                for q in range(gz_n):
                    bulk[t, q, :, n * folds + i] = row[:, q * rows : (q + 1) * rows]
    pl.semaphore_wait(barrier, expected)

    for d in range(1, gz_n):
        pltpu.make_async_remote_copy(
            src_ref=seeds,
            dst_ref=seed_recv.at[gz],
            send_sem=seed_sem.at[0],
            recv_sem=seed_sem.at[1],
            device_id=(gx, gy, (gz + d) % gz_n),
            device_id_type=MESH,
        ).start()

    for t in range(tiles):
        for d in range(gz_n - 1, 0, -1):
            to = (gz + d) % gz_n
            pltpu.make_async_remote_copy(
                src_ref=bulk.at[t, tile_of(to), :, pl.ds(0, width[t])],
                dst_ref=recv[t].at[pl.ds(slots * gz, slots), pl.ds(0, width[t])],
                send_sem=in_sem.at[t],
                recv_sem=in_sem.at[tiles + t],
                device_id=(gx, gy, to),
                device_id_type=MESH,
            ).start()
    for t in range(tiles):
        recv[t][pl.ds(slots * gz, slots), pl.ds(0, width[t])] = bulk[t, part, :, pl.ds(0, width[t])]
    for fetch in fetches:
        fetch.wait()

    base = (gx * gy_n + gy) * places

    def lookup(b, carry):
        source, depth = carry
        here = jnp.logical_and(coords[0, b] == gx, coords[1, b] == gy)
        z = jnp.where(here, coords[2, b], -1)
        was = before[b] - base
        now = jnp.where(here, after[b] - base, -1)
        source = tuple(jnp.where(z == k, was, source[k]) for k in range(per_column))
        depth = tuple(jnp.where(now == p, z, depth[p]) for p in range(places))
        return source, depth

    source, depth = lax.fori_loop(
        0,
        nblk,
        lookup,
        ((jnp.int32(0),) * per_column, (jnp.int32(-1),) * places),
    )

    def drain(ref, sem):
        pltpu.make_async_copy(ref, ref, sem).wait()

    def seed_row(ref, p):
        pair = ref[p // slots]
        row = pair[0:1]
        for s in range(1, slots):
            row = jnp.where(p % slots == s, pair[s : s + 1], row)
        return row.astype(jnp.float32)

    load_seed.wait()
    drain(seed_recv.at[pl.ds(0, gz_n - 1)], seed_sem.at[1])
    for k in range(per_column):
        row = seed_row(seed_recv, source[k])[None]
        cut = [row[:, :, t * LANES : (t + 1) * LANES] for t in range(tiles)]
        for t in range(tiles):
            piece = jnp.where(odd_y == 1, flipped(cut[tiles - 1 - t]), cut[t])[0]
            wide = jnp.broadcast_to(piece, (ext, LANES))
            marks[t, k] = wide
            if t > 0:
                edge_marks[t, k] = wide
            for x in range(2):
                xsmall[t, x, k, pl.ds(packs, 1)] = piece
                if t == tiles - 1:
                    xsmall[t, x, k, pl.ds(0, packs)] = jnp.zeros((packs, LANES), jnp.float32)

    def unfold(block, strips):
        fields_of = []
        for n in range(packs):
            strip_n = strips[n : n + 1]
            extra = rolled(strip_n, -strip_lanes * folds)
            for i in range(folds):
                row = block[n * folds + i : n * folds + i + 1]
                fields_of.append(
                    jnp.where(lane < strip_lanes, rolled(strip_n, -strip_lanes * i), row)
                )
                extra = jnp.where(
                    lane // strip_lanes == i + 1, rolled(row, strip_lanes * (i + 1)), extra
                )
            fields_of.append(extra)
        return fields_of

    near = (halo - 1, halo + rows)
    first = (0, halo + rows)
    shape = (per_column, ext, LANES)
    lane3 = lax.broadcasted_iota(jnp.int32, shape, 2)
    z_cell = lane3 % cells
    group = lane3 // cells
    last_group = LANES // cells - 1
    row_id = lax.broadcasted_iota(jnp.int32, shape, 1)
    far = lane3 >= LANES // 2

    def mirror(v, e):
        ring = None
        for h in range(halo):
            shift = (2 * h + 1) * cells
            w = rolled(v, shift if e else -shift)
            spot = h if e else last_group - h
            ring = w if ring is None else jnp.where(lane // cells == spot, w, ring)
        return ring

    def outer(t):
        return [e for e, spot in ((0, 0), (1, tiles - 1)) if t == spot]

    def send_strips(t, e, other):
        for n in range(packs):
            row = None
            for j in range(min(per_pack, nfield - n * per_pack)):
                v = mirror(vals[n * per_pack + j, t, :, halo : halo + rows, :], e)
                v = rolled(v, strip_lanes * (j if e else j + 1))
                row = v if row is None else jnp.where(lane // strip_lanes == j, v, row)
            ysend[e, :, n] = row
            for x, r in ((0, 0), (1, rows - 1)):
                ynear[e, x, :, pl.ds(n, 1), :] = row[:, r : r + 1]
        for x, (exists, _, device) in enumerate(sides_x):

            @pl.when(exists)
            def _(x=x, device=device):
                pltpu.make_async_remote_copy(
                    src_ref=ynear.at[e, x],
                    dst_ref=ynear_recv.at[e, 1 - x],
                    send_sem=yn_sem.at[e, x],
                    recv_sem=yn_sem.at[e, 2 + 1 - x],
                    device_id=(device[0], other, device[2]),
                    device_id_type=MESH,
                ).start()

        ysend[e, :, packs] = mirror(marks[t], e)[:, halo : halo + rows]
        pltpu.make_async_remote_copy(
            src_ref=ysend.at[e],
            dst_ref=yrecv.at[e],
            send_sem=y_sem.at[e],
            recv_sem=y_sem.at[2 + e],
            device_id=(gx, other, gz),
            device_id_type=MESH,
        ).start()

    def take_strips(e):
        drain(yrecv.at[e], y_sem.at[2 + e])
        for x, (exists, _, _) in enumerate(sides_x):

            @pl.when(exists)
            def _(x=x):
                drain(ynear_recv.at[e, x], yn_sem.at[e, 2 + x])

            @pl.when(jnp.logical_not(exists))
            def _(x=x):
                r = (rows - 1) * x
                for n in range(packs):
                    ynear_recv[e, x, :, pl.ds(n, 1), :] = yrecv[e, :, n, r : r + 1, :]

    for t in range(tiles):
        drain(recv[t].at[pl.ds(0, (gz_n - 1) * slots), pl.ds(0, width[t])], in_sem.at[tiles + t])
        for k in range(per_column):
            block = recv[t][source[k]]
            if data_width[t] == nfield:
                full = block[:nfield]
                xsend[t, 0, k] = full[:, :halo]
                xsend[t, 1, k] = full[:, rows - halo :]
                vals[:, t, k, halo : halo + rows, :] = full
            else:
                for f, v in enumerate(unfold(block, packed[t - 1, k])):
                    vals[pl.ds(f, 1), t, k, halo : halo + rows, :] = v
            if t < tiles - 1:
                piece = block[data_width[t] :]
                packed[t, k] = piece
                for x, r in ((0, 0), (1, rows - 1)):
                    for n in range(packs):
                        xsmall[t, x, k, pl.ds(n, 1)] = piece[n, r : r + 1]

        for e in outer(t):
            exists, other = sides_y[e]

            @pl.when(exists)
            def _(t=t, e=e, other=other):
                send_strips(t, e, other)

        if data_width[t] < nfield:
            for k in range(per_column):
                xsend[t, 0, k] = vals[:, t, k, halo : 2 * halo, :]
                xsend[t, 1, k] = vals[:, t, k, rows : rows + halo, :]
        for e, (exists, _, device) in enumerate(sides_x):

            @pl.when(exists)
            def _(t=t, e=e, device=device):
                for src, dst, sem in ((xsend, xghost, x_sem), (xsmall, xgsmall, xs_sem)):
                    pltpu.make_async_remote_copy(
                        src_ref=src.at[t, e],
                        dst_ref=dst.at[t, 1 - e],
                        send_sem=sem.at[t, e],
                        recv_sem=sem.at[t, 2 + 1 - e],
                        device_id=device,
                        device_id_type=MESH,
                    ).start()

            @pl.when(jnp.logical_not(exists))
            def _(t=t, e=e):
                for h in range(halo):
                    xghost[t, e, :, :, h : h + 1, :] = xsend[t, e, :, :, halo - 1 - h : halo - h, :]
                xgsmall[t, e] = xsmall[t, e]

    def spread(t, e, inner):
        for n in range(packs):
            unpack[:, halo : halo + rows, :] = packed[t, :, n] if inner else yrecv[e, :, n]
            for x in range(2):
                row = xgsmall[t, x, :, pl.ds(n, 1), :] if inner else ynear_recv[e, x, :, pl.ds(n, 1), :]
                unpack[:, near[x] : near[x] + 1, :] = row
            whole = unpack[...]
            for j in range(min(per_pack, nfield - n * per_pack)):
                shift = -strip_lanes * j if e else -strip_lanes * (j + 1)
                edge[e and 1 + t, n * per_pack + j] = rolled(whole, shift)

    def shift_rows(v, by):
        if ext % 8 == 0:
            return pltpu.roll(v, by % ext, 1)
        cut = by % ext
        return jnp.concatenate([v[:, ext - cut :], v[:, : ext - cut]], 1)

    def around(v, below, above):
        below_y = jnp.where(group == 0, below, rolled(v, cells))
        above_y = jnp.where(group == last_group, above, rolled(v, -cells))
        before_k = jnp.concatenate([v[-1:], v[:-1]], 0)
        after_k = jnp.concatenate([v[1:], v[:1]], 0)
        below_z = jnp.where(z_cell == 0, rolled(before_k, 1 - cells), rolled(v, 1))
        above_z = jnp.where(z_cell == cells - 1, rolled(after_k, cells - 1), rolled(v, -1))
        total = shift_rows(v, 1) + shift_rows(v, -1) + below_y + above_y + below_z + above_z
        return total - 6.0 * v

    x_cell = row_id + (gx * cells + part * rows - halo)
    x_cell = jnp.where(x_cell < 0, -1 - x_cell, x_cell)
    x_end = gx_n * cells
    x_cell = jnp.where(x_cell > x_end - 1, 2 * x_end - 1 - x_cell, x_cell)
    xglob = x_cell.astype(jnp.float32)
    unpack[...] = jnp.zeros_like(unpack)

    for t in range(tiles):
        for e, (exists, _, device) in enumerate(sides_x):

            @pl.when(exists)
            def _(t=t, e=e):
                drain(xghost.at[t, e], x_sem.at[t, 2 + e])
                drain(xgsmall.at[t, e], xs_sem.at[t, 2 + e])

        for k in range(per_column):
            for e in range(2):
                vals[:, t, k, first[e] : first[e] + halo, :] = xghost[t, e, k]
                marks[t, k, near[e] : near[e] + 1, :] = xgsmall[t, e, k, pl.ds(packs, 1)]
        for e, (exists, _) in enumerate(sides_y):
            if e == 0 and t > 0:
                continue
            if e == 1 and t < tiles - 1:
                spread(t, e, True)
                continue

            @pl.when(exists)
            def _(t=t, e=e):
                take_strips(e)
                spread(t, e, False)
                for k in range(per_column):
                    edge_marks[e and 1 + t, k] = jnp.broadcast_to(
                        yrecv[e, k, packs, 0:1, :], (ext, LANES)
                    )

            @pl.when(jnp.logical_not(exists))
            def _(t=t, e=e):
                for f in range(nfield):
                    edge[e and 1 + t, f] = mirror(vals[f, t], e)
                edge_marks[e and 1 + t] = mirror(marks[t], e)

        def collect(t, at, count):
            for p in range(places):
                k = depth[p]
                tile = result[t, jnp.maximum(k, 0), pl.ds(at, count)]
                outbuf[t, p // slots, p % slots, pl.ds(at, count)] = jnp.where(k >= 0, tile, 0.0)

        def send_back(t, at, count, order):
            for n in order:
                to = jnp.where(n < gz, n, gz_n - 1 - n + gz)
                pltpu.make_async_remote_copy(
                    src_ref=outbuf.at[t, to, :, pl.ds(at, count)],
                    dst_ref=outrecv.at[t, part, :, pl.ds(at, count)],
                    send_sem=out_sem.at[t],
                    recv_sem=out_sem.at[tiles + t],
                    device_id=(gx, gy, to),
                    device_id_type=MESH,
                ).start()

        def join(low, high):
            return jnp.where(far, low, high) if t == 0 else high

        for step in range(STEPS):
            last = step == STEPS - 1
            if step == 0:
                body = [vals[f, t] for f in range(nfield)]
                rim = [join(edge[0, f], edge[1 + t, f]) for f in range(nfield)]
                seed = (marks[t], join(edge_marks[0], edge_marks[1 + t]))
            else:
                body = [mid[f, t] for f in range(nfield)]
                rim = [mid_edge[f] for f in range(nfield)]

            def laplace(f):
                v, w = body[f], rim[f]
                prior = w if t == 0 else (vals[f, t - 1] if step == 0 else mid[f, t - 1])
                sums = [around(v, rolled(prior, cells), rolled(w, -cells))]
                if not last:
                    sums.append(around(w, rolled(v, cells), rolled(v, -cells)))
                return sums

            def keep(f, i, new):
                if last:
                    result[t, :, f] = new[:, halo : halo + rows]
                elif i == 0:
                    mid[f, t] = new
                else:
                    mid_edge[f] = new

            thermal = xglob / (2.0 * cells) - 1.0 - 0.25 * step
            change = []
            for k in range(NPHASE):
                moved = []
                for i, lap in enumerate(laplace(k)):
                    have = (body, rim)[i]
                    phi = have[k]
                    drive = gain[k] * thermal
                    for j in range(nfield - NPHASE):
                        drive = drive + couple[k, j] * have[NPHASE + j]
                    if step == 0:
                        drive = drive + jnp.where(seed[i] == float(k), SEED_GAIN, 0.0)
                    delta = 0.12 * lap + phi * (1.0 - phi) * (phi - 0.5 + drive)
                    moved.append(delta)
                    keep(k, i, phi + delta)
                change.append(moved)
            if last:
                collect(t, 0, NPHASE)
                send_back(t, 0, NPHASE, range(gz_n - 1) if t < tiles - 1 else [0])
            for j in range(nfield - NPHASE):
                for i, lap in enumerate(laplace(NPHASE + j)):
                    new = (body, rim)[i][NPHASE + j] + (0.1 * diffuse[j]) * lap
                    for k in range(NPHASE):
                        new = new - latent[j, k] * change[k][i]
                    keep(NPHASE + j, i, new)

        collect(t, NPHASE, nfield - NPHASE)
        early = range(gz_n - 1) if t < tiles - 1 else [0]
        send_back(t, NPHASE, nfield - NPHASE, early)
        send_back(t, 0, nfield, [n for n in range(gz_n - 1) if n not in early])
        outrecv[t, part] = outbuf[t, gz]

    for e, (exists, _) in enumerate(sides_y):

        @pl.when(exists)
        def _(e=e):
            drain(ysend.at[e], y_sem.at[e])
            for x, (exists_x, _, _) in enumerate(sides_x):

                @pl.when(exists_x)
                def _(x=x):
                    drain(ynear.at[e, x], yn_sem.at[e, x])

    drain(seed_recv.at[pl.ds(0, gz_n - 1)], seed_sem.at[0])
    for t in range(tiles):
        drain(recv[t].at[pl.ds(0, (gz_n - 1) * slots), pl.ds(0, width[t])], in_sem.at[t])
        for e, (exists, _, device) in enumerate(sides_x):

            @pl.when(exists)
            def _(t=t, e=e):
                drain(xsend.at[t, e], x_sem.at[t, e])
                drain(xsmall.at[t, e], xs_sem.at[t, e])

    for t in range(tiles):
        drain(outrecv.at[t, pl.ds(0, gz_n - 1)], out_sem.at[tiles + t])

        @pl.when(odd_y == 0)
        def _(t=t):
            for q in range(gz_n):
                out[:, :, q * rows : (q + 1) * rows, t * LANES : (t + 1) * LANES] = outrecv[t, q]

        @pl.when(odd_y == 1)
        def _(t=t):
            lanes = pl.ds((tiles - 1 - t) * LANES, LANES)
            for q in range(gz_n):
                for s in range(slots):
                    out[s, :, q * rows : (q + 1) * rows, lanes] = flipped(outrecv[t, q, s])

    for t in range(tiles):
        drain(outbuf.at[t, pl.ds(0, gz_n - 1)], out_sem.at[t])


def solution(mesh):
    gx_n, gy_n, gz_n = mesh.shape["gx"], mesh.shape["gy"], mesh.shape["gz"]

    def deep(fields, seeds, *tables):
        slots, nfield, cells, surface = fields.shape
        tables = (tables[0].T,) + tables[1:]
        nblk = tables[0].shape[1]
        column = nblk // (gx_n * gy_n)
        tiles = surface // LANES
        rows = cells // gz_n
        ext = rows + 2 * STEPS
        packs = -(-nfield // (LANES // (STEPS * cells)))
        places = gz_n * slots
        f32, i32 = jnp.float32, jnp.int32
        dma = pltpu.SemaphoreType.DMA
        anyspace = pl.BlockSpec(memory_space=pl.ANY)
        block = (column, ext, LANES)
        faces = (tiles, 2, column, nfield, STEPS, LANES)
        thin = (tiles, 2, column, packs + 1, LANES)
        return pl.pallas_call(
            functools.partial(deep_kernel, (gx_n, gy_n, gz_n, nblk, cells, surface)),
            out_shape=pltpu.VMEM(fields.shape, f32),
            in_specs=[anyspace] * 9,
            out_specs=pl.BlockSpec(memory_space=pltpu.VMEM),
            scratch_shapes=[pltpu.SMEM(a.shape, a.dtype) for a in tables]
            + [
                dma((len(tables),)),
                pltpu.VMEM(fields.shape, f32),
                pltpu.VMEM((tiles, gz_n, slots, nfield + packs, rows, LANES), f32),
                pltpu.VMEM((gz_n, slots, surface), i32),
                pltpu.VMEM((nfield, tiles) + block, f32),
                pltpu.VMEM((tiles + 1, nfield) + block, f32),
                pltpu.VMEM((nfield, tiles) + block, f32),
                pltpu.VMEM((nfield,) + block, f32),
                pltpu.VMEM((tiles,) + block, f32),
                pltpu.VMEM((tiles + 1,) + block, f32),
                pltpu.VMEM(faces, f32),
                pltpu.VMEM(faces, f32),
                pltpu.VMEM(thin, f32),
                pltpu.VMEM(thin, f32),
                pltpu.VMEM((max(tiles - 1, 1), column, packs, rows, LANES), f32),
                pltpu.VMEM(block, f32),
                pltpu.VMEM((2, column, packs + 1, rows, LANES), f32),
                pltpu.VMEM((2, column, packs + 1, rows, LANES), f32),
                pltpu.VMEM((2, 2, column, packs, LANES), f32),
                pltpu.VMEM((2, 2, column, packs, LANES), f32),
                pltpu.VMEM((tiles, column, nfield, rows, LANES), f32),
                pltpu.VMEM((tiles, gz_n, slots, nfield, rows, LANES), f32),
                pltpu.VMEM((tiles, gz_n, slots, nfield, rows, LANES), f32),
                dma((2,)),
                dma((2 * tiles,)),
                dma((2,)),
                dma((4,)),
                dma((2, 4)),
                dma((tiles, 4)),
                dma((tiles, 4)),
                dma((2 * tiles,)),
            ]
            + [pltpu.VMEM((places, w, rows, LANES), f32) for w in widths(nfield, tiles, cells)[1]],
            compiler_params=pltpu.CompilerParams(collective_id=0, has_side_effects=True),
        )(fields, seeds, *tables)

    def per_device(fields, seeds, coords, neighbours, before, after, couple, latent, diffuse, gain):
        slots, nfield, cells, surface = fields.shape
        nblk = coords.shape[0]
        per_column = nblk // (gx_n * gy_n)
        halves = surface // LANES
        rows = cells * halves // gz_n
        f32, i32 = jnp.float32, jnp.int32
        dma = pltpu.SemaphoreType.DMA
        smem = pl.BlockSpec(memory_space=pltpu.SMEM)
        anyspace = pl.BlockSpec(memory_space=pl.ANY)
        if cells % gz_n == 0 and cells // gz_n >= STEPS and 2 * STEPS * cells <= LANES:
            return deep(fields, seeds, coords, before, after, couple, latent, diffuse, gain)
        faces_x = (STEPS, 2, per_column, nfield, LANES)
        faces_y = (STEPS, 2, per_column, rows, LANES)
        return pl.pallas_call(
            functools.partial(tile_kernel, (gx_n, gy_n, gz_n, nblk, cells, surface)),
            out_shape=pltpu.VMEM(fields.shape, f32),
            in_specs=[anyspace, anyspace] + [smem] * 7,
            out_specs=pl.BlockSpec(memory_space=pltpu.VMEM),
            scratch_shapes=[
                pltpu.VMEM((gz_n * slots, nfield, rows, LANES), f32),
                pltpu.VMEM((gz_n, slots, LANES), i32),
                pltpu.VMEM((nfield, per_column, rows, LANES), f32),
                pltpu.VMEM(faces_x, f32),
                pltpu.VMEM(faces_x, f32),
                pltpu.VMEM(faces_y, f32),
                pltpu.VMEM(faces_y, f32),
                pltpu.VMEM((STEPS, nfield, per_column, rows, LANES), f32),
                pltpu.VMEM((gz_n, slots, nfield, rows, LANES), f32),
                dma((gz_n,)),
                dma((gz_n,)),
                dma((gz_n,)),
                dma((gz_n,)),
                dma((STEPS, 2)),
                dma((STEPS, 2)),
                dma((STEPS, 2)),
                dma((STEPS, 2)),
                dma((gz_n,)),
                dma((gz_n,)),
                dma((3,)),
            ],
            compiler_params=pltpu.CompilerParams(collective_id=0, has_side_effects=True),
        )(fields, seeds, coords.T, before, after, couple, latent, diffuse, gain)

    placed = (
        P(("gx", "gy", "gz"), None, None, None),
        P(("gx", "gy", "gz"), None),
    ) + (P(),) * 8
    return jax.shard_map(
        per_device,
        mesh=mesh,
        in_specs=placed,
        out_specs=P(("gx", "gy", "gz"), None, None, None),
        check_vma=False,
    )
```
